128 devices in a mesh: sub: 8 (over z, core), row: 4 (over x), col: 4 (over y).
Axes of the slice: x: 4, y: 4, z: 4, core: 2. Of those that a mesh axis runs over, the one named last changes fastest.
Arguments:
- front: float32 [4, 32, 128, 32, 4, 128], P(None, ('sub', 'row'), None, None, 'col'), may hold values from -2.4 to 7.5, as said below
- child_tiles: bfloat16 [16384, 128, 128], P(('sub', 'row', 'col')), may hold values from -2.390625 to 2.390625
- tile_owner: int32 [16384, 1], P(('sub', 'row', 'col')), may hold values from 0 to 127; in each aligned block of 128 rows (0 to 127, 128 to 255, ...) at most 2 rows name the same one
- tile_slot: int32 [16384], P(('sub', 'row', 'col')), may hold values from 2 to 127
Outputs:
- updated: float32 [4, 32, 128, 32, 4, 128], P(None, ('sub', 'row'), None, None, 'col')
- panel: bfloat16 [4, 32, 128, 2, 4, 128], P(None, ('sub', 'row'), None, None, 'col')
The draws below stay inside these ranges and needn't reach their ends.
Inputs may be any that keep to these rules, and one draw needn't show every extreme that they name: The leading 1024 x 1024 block of front, made symmetric from its lower triangle, is positive definite. `tile_owner`: at most 2 of the tiles of one device go to one owner.
All inputs are finite; a program needn't handle non-finite values.
Results may differ from the reference program's by a relative error of at most 0.0038.
Values may be sent and summed in bfloat16 or wider, within the bound.
A program may use at most 128 MiB of HBM per device.

```python
import math
import jax
import jax.numpy as jnp
import numpy as np
from jax import lax

P_SIZE = 16384
NB = 1024
TB = 128
TILES_DEV = 128
CAP = 2
TILES = 16384
ROW_TILES = 4
COL_TILES = 32
N_SUB = 8
N_ROW = 4
N_COL = 4
DEVICES = 128


def draw_front(key, part):
    group_count = N_SUB * N_ROW
    row_tiles = P_SIZE // TB // group_count
    col_tiles = P_SIZE // TB // N_COL
    extent = (row_tiles, group_count, TB, col_tiles, N_COL, TB)
    key_base, key_mix, key_diag = jax.random.split(key, 3)
    base = jnp.clip(0.4 * jax.random.normal(key_base, extent, jnp.float32), -2.4, 2.4)
    mixing = jnp.clip(jax.random.normal(key_mix, (NB, NB), jnp.float32), -4.0, 4.0)
    lengths = jnp.sqrt(jnp.sum(mixing * mixing, 1, keepdims=True) + 1e-06)
    unit_rows = mixing / lengths
    gram = jnp.dot(unit_rows, unit_rows.T, precision=lax.Precision.HIGHEST, preferred_element_type=jnp.float32)
    shift = jax.random.uniform(key_diag, (NB,), jnp.float32, 2.5, 3.5)
    identity = jnp.eye(NB, dtype=jnp.bool_)
    pivot = jnp.where(identity, 4.0 + shift[:, None], 4.0 * gram)
    pivot_tiles = pivot.reshape(NB // TB, TB, NB // (TB * N_COL), N_COL, TB)
    return base.at[0, :NB // TB, :, :NB // (TB * N_COL), :, :].set(pivot_tiles)


def touch_ends(array, own_key, low, largest):
    shape = array.shape
    place = [jax.random.randint(jax.random.fold_in(own_key, axis), (), 0, shape[axis]) for axis in range(len(shape))]
    array = array.at[tuple(place)].set(low)
    longest = shape.index(max(shape))
    place[longest] = (place[longest] + 1) % shape[longest]
    return array.at[tuple(place)].set(largest)


def levels(key, shape, cuts, low, largest):
    factor_of = 1.0
    for position, shards_of in cuts:
        steps = jax.random.uniform(jax.random.fold_in(jax.random.fold_in(key, 6), position), (shards_of,), jnp.float32, low / len(cuts), largest / len(cuts))
        factor_of = factor_of * jnp.repeat(jnp.exp(steps), shape[position] // shards_of).reshape((-1,) + (1,) * (len(shape) - 1 - position))
    return factor_of


def routed_block(own_key, own, number, rows, count, top, limit, slope):
    sequence = jax.random.permutation(own_key, count)
    heavy_load, common = load_shares(count, rows * top, limit, slope, True), load_shares(count, rows * top, limit, slope, False)
    places = jnp.arange(count)

    def named(sizes, offset_by):
        used = int((sizes > 0).sum())
        fixed = max(1, used // 4)
        shifted = fixed + (places - fixed + offset_by * (used - fixed)) % max(1, count - fixed)
        return jnp.zeros((count,), jnp.int32).at[sequence[jnp.where(places < fixed, places, shifted)]].set(jnp.asarray(sizes, jnp.int32))

    sizes = jnp.where(number % 4 == 0, named(heavy_load, number // 4), named(common, number - number // 4 - 1))
    mixed = jax.random.permutation(jax.random.fold_in(own, 3), count)
    giver, taker = mixed[0:count // 2 * 2:2], mixed[1:count // 2 * 2:2]
    margin = jnp.minimum(sizes[giver] - 1, limit - sizes[taker]) // 2
    margin = jnp.where((giver == sequence[0]) | (taker == sequence[0]) | (sizes[taker] == 0), 0, jnp.maximum(margin, 0))
    shifted = jax.random.randint(jax.random.fold_in(own, 4), (count // 2,), 0, 1 << 20) % (margin + 1)
    sizes = sizes.at[giver].add(-shifted).at[taker].add(shifted)
    labels = jnp.searchsorted(jnp.cumsum(sizes), jnp.arange(rows * top), side="right").astype(jnp.int32)
    table = labels.reshape(top, rows).T
    table = table[jax.random.permutation(jax.random.fold_in(own, 1), rows)]
    offset_by = jax.random.randint(jax.random.fold_in(own, 2), (rows, 1), 0, top)
    return jnp.take_along_axis(table, (jnp.arange(top)[None, :] + offset_by) % top, axis=1)


def load_shares(count, total, most, lean, full):
    loads = [(1 << 20) // math.isqrt(rank ** lean) + 1 for rank in range(1, count + 1)]
    largest = most if full else min(most, max(-(-total // count), total * loads[0] // sum(loads)))
    least = 1 if total - largest >= count - 1 else 0
    counts, spare = [largest] + [least] * (count - 1), total - largest - least * (count - 1)
    while spare > 0:
        movable = [i for i in range(1, count) if counts[i] < largest] or [i for i in range(1, count) if counts[i] < most]
        whole, budget = sum([loads[i] for i in movable]), spare
        for i in movable:
            extra = min(most - counts[i], max(1, budget * loads[i] // whole), spare)
            counts[i] = counts[i] + extra
            spare = spare - extra
    return np.array(counts)


def noise(own_key, shape, deviation, limit, cuts=(), held_as=jnp.bfloat16):
    drawn = jax.random.normal(own_key, shape, jnp.float32) * deviation
    if len(cuts) > 0:
        drawn = levels(own_key, shape, cuts, -0.22, 0.18) * drawn
    return jnp.clip(drawn, min=-limit, max=limit).astype(held_as)


def setup_inputs(seed: int = 0) -> dict:
    key_list = jax.random.split(jax.random.key(seed), 5)
    front = draw_front(jax.random.fold_in(key_list[4], 71), 0)
    child_tiles = noise(key_list[1], (TILES, TB, TB), 0.4, 2.390625, ((0, 128),))
    tile_owner_keys = jax.random.split(jax.random.fold_in(key_list[2], 1), TILES // TILES_DEV)
    tile_owner_turns = jax.random.permutation(jax.random.fold_in(key_list[2], 3), TILES // TILES_DEV)
    tile_owner = jax.vmap(lambda own, number: routed_block(jax.random.fold_in(key_list[2], 2), own, number, TILES_DEV, DEVICES, 1, CAP, 2))(tile_owner_keys, tile_owner_turns).reshape((TILES, 1))
    tile_slot = touch_ends(jax.random.randint(key_list[3], (TILES,), NB // (TB * N_COL), ROW_TILES * COL_TILES), jax.random.fold_in(key_list[3], 1), NB // (TB * N_COL), (ROW_TILES * COL_TILES) - 1).astype(jnp.int32)
    return dict(front=front, child_tiles=child_tiles, tile_owner=tile_owner, tile_slot=tile_slot)


def reference(front, child_tiles, tile_owner, tile_slot):
    group_count = N_SUB * N_ROW
    tile_total = P_SIZE // TB
    col_tiles = tile_total // N_COL
    owners = tile_owner[:, 0]
    tile_row = tile_slot // col_tiles * group_count + owners // N_COL
    tile_col = tile_slot % col_tiles * N_COL + owners % N_COL
    tiled = front.reshape(tile_total, TB, tile_total, TB)
    tiled = tiled.at[tile_row, :, tile_col, :].add(child_tiles.astype(jnp.float32))
    assembled = tiled.reshape(P_SIZE, P_SIZE)
    pivot = assembled[:NB, :NB]
    symmetric = jnp.tril(pivot) + jnp.tril(pivot, -1).T
    factor = jnp.linalg.cholesky(symmetric)
    below = jax.scipy.linalg.solve_triangular(factor, assembled[NB:, :NB].T, lower=True).T
    panel = jnp.concatenate([factor, below], 0).astype(jnp.bfloat16)
    lower = panel[NB:].astype(jnp.float32)
    trailing = assembled[NB:, NB:] - jnp.dot(lower.astype(jnp.float32), lower.T.astype(jnp.float32), precision=lax.Precision.HIGHEST, preferred_element_type=jnp.float32)
    updated = assembled.at[NB:, NB:].set(trailing)
    panel_out = panel.reshape(tile_total // group_count, group_count, TB, NB // (TB * N_COL), N_COL, TB)
    return (updated.reshape(front.shape), panel_out)
```

```python
import jax
import jax.numpy as jnp
from jax import lax
from jax.experimental import pallas as pl
from jax.experimental.pallas import tpu as pltpu
from jax.sharding import PartitionSpec as P

F32, BF = jnp.float32, jnp.bfloat16
HI = lax.Precision.HIGHEST
V = pltpu.VMEM
ANY = pl.ANY


def nt(a, b):
    return lax.dot_general(a, b, (((1,), (1,)), ((), ())), precision=HI, preferred_element_type=F32)
def nn(a, b):
    return lax.dot_general(a, b, (((1,), (0,)), ((), ())), precision=HI, preferred_element_type=F32)

def split3(x):
    h = x.astype(BF).astype(F32)
    r = x - h
    m = r.astype(BF).astype(F32)
    return h, m, r - m

def diag_factor(d_ref, u_ref, x_ref, cb_ref, r_ref):
    def body(b, carry):
        r0 = pl.multiple_of(b * 8, 8)
        block = d_ref[pl.ds(r0, 8), 0:128]
        rolled = pltpu.roll(block, (128 - r0) % 128, 1)
        for j in range(8):
            cb_ref[j] = jnp.broadcast_to(rolled[:, j:j + 1], (8, 128))
        r_ref[:, 0:128] = block
        r_ref[:, 128:256] = d_ref[pl.ds(r0, 8), 128:256]
        e = {}
        for i in range(8):
            for j in range(i + 1):
                e[i, j] = cb_ref[j, i:i + 1, :]
        rows = []
        for i in range(8):
            rows.append([r_ref[i:i + 1, 0:128], r_ref[i:i + 1, 128:256]])
        for j in range(8):
            inv = lax.rsqrt(e[j, j])
            low = {}
            for i in range(j + 1, 8):
                low[i] = e[i, j] * inv
            for h in range(2):
                rows[j][h] = rows[j][h] * inv
            for i in range(j + 1, 8):
                for m in range(j + 1, i + 1):
                    e[i, m] = e[i, m] - low[i] * low[m]
                for h in range(2):
                    rows[i][h] = rows[i][h] - low[i] * rows[j][h]
        for i in range(8):
            r_ref[i:i + 1, 0:128] = rows[i][0]
            r_ref[i:i + 1, 128:256] = rows[i][1]
        r = r_ref[...]
        u_ref[pl.ds(r0, 8), :] = r[:, 0:128]
        x_ref[pl.ds(r0, 8), :] = r[:, 128:256]
        h, m, l = split3(r)
        left = jnp.concatenate([h, h, m, h, l, m], 0)[:, 0:128].astype(BF)
        right = jnp.concatenate([h, m, h, l, h, m], 0).astype(BF)
        d_ref[...] = d_ref[...] - lax.dot_general(left, right, (((0,), (0,)), ((), ())), preferred_element_type=F32)
        return carry
    lax.fori_loop(0, 16, body, 0)

def chol_kernel(lead_ref, l_ref, hi_ref, lo_ref, s_ref, w_ref, d_ref, u_ref, x_ref, cb_ref, r_ref):
    row = lax.broadcasted_iota(jnp.int32, (128, 128), 0)
    col = lax.broadcasted_iota(jnp.int32, (128, 128), 1)
    eye = (row == col).astype(F32)
    n = 8
    for i in range(n):
        for j in range(i + 1):
            t = lead_ref[i, j]
            if i == j:
                t = jnp.where(row >= col, t, t.T)
            s_ref[i * 128:(i + 1) * 128, j * 128:(j + 1) * 128] = t
    w_ref[...] = jnp.zeros_like(w_ref)
    l_ref[...] = jnp.zeros_like(l_ref)
    for k in range(n):
        a, b = k * 128, (k + 1) * 128
        d_ref[:, 0:128] = s_ref[a:b, a:b]
        d_ref[:, 128:256] = eye
        diag_factor(d_ref, u_ref, x_ref, cb_ref, r_ref)
        x = x_ref[...]
        l_ref[a:b, a:b] = jnp.where(row >= col, u_ref[...].T, 0.0).astype(BF)
        if k > 0:
            w_ref[a:b, 0:a] = nn(x, w_ref[a:b, 0:a])
        w_ref[a:b, a:b] = x
        if k < n - 1:
            p = nt(s_ref[b:, a:b], x)
            s_ref[b:, a:b] = p
            l_ref[b:, a:b] = p.astype(BF)
            for j in range(k + 1, n):
                c, d = j * 128, (j + 1) * 128
                s_ref[c:, c:d] = s_ref[c:, c:d] - nt(s_ref[c:, a:b], s_ref[c:d, a:b])
            w_ref[b:, 0:b] = w_ref[b:, 0:b] - nn(p, w_ref[a:b, 0:b])
    for k in range(n):
        a, b = k * 128, (k + 1) * 128
        y = w_ref[a:b, :]
        h = y.astype(BF)
        hi_ref[a:b, :] = h
        lo_ref[a:b, :] = (y - h.astype(F32)).astype(BF)

def chol(lead):
    return pl.pallas_call(
        chol_kernel,
        out_shape=[jax.ShapeDtypeStruct((1024, 1024), BF)] * 3,
        in_specs=[pl.BlockSpec(memory_space=V)],
        out_specs=[pl.BlockSpec(memory_space=V)] * 3,
        scratch_shapes=[V((1024, 1024), F32), V((1024, 1024), F32), V((128, 256), F32), V((128, 128), F32),
                        V((128, 128), F32), V((8, 8, 128), F32), V((8, 256), F32)],
        compiler_params=pltpu.CompilerParams(vmem_limit_bytes=60 << 20),
        name="chol",
    )(lead)


def route_kernel(own_ref, slot_ref, child_ref, out_ref, tgt_ref, idx_ref, cnt_ref):
    step = pl.program_id(0)

    @pl.when(step == 0)
    def _():
        def clear(k, c):
            cnt_ref[k] = 0
            for u in range(2):
                idx_ref[2 * k + u] = 0
                tgt_ref[2 * k + u] = -1
            return c
        lax.fori_loop(0, 128, clear, 0)

        def place(k, c):
            o = own_ref[k]
            n = cnt_ref[o]
            idx_ref[2 * o + n] = k
            tgt_ref[2 * o + n] = slot_ref[k]
            cnt_ref[o] = n + 1
            return c
        lax.fori_loop(0, 128, place, 0)

    def copy(j, c):
        for u in range(2):
            out_ref[j, u] = child_ref[idx_ref[step * 32 + 2 * j + u]]
        return c
    lax.fori_loop(0, 16, copy, 0)


def route(owner, slot, child):
    return pl.pallas_call(
        route_kernel,
        out_shape=(jax.ShapeDtypeStruct((128, 2, 128, 128), BF), jax.ShapeDtypeStruct((256,), jnp.int32)),
        grid_spec=pltpu.PrefetchScalarGridSpec(
            num_scalar_prefetch=2, grid=(8,),
            in_specs=[pl.BlockSpec((128, 128, 128), lambda g, a, b: (0, 0, 0), pipeline_mode=pl.Buffered(1))],
            out_specs=(pl.BlockSpec((16, 2, 128, 128), lambda g, a, b: (g, 0, 0, 0)),
                       pl.BlockSpec(memory_space=pltpu.SMEM)),
            scratch_shapes=[pltpu.SMEM((256,), jnp.int32), pltpu.SMEM((128,), jnp.int32)]),
        compiler_params=pltpu.CompilerParams(vmem_limit_bytes=24 << 20),
        name="route",
    )(owner, slot, child)


def head_kernel(land_ref, front_ref, arr_ref, out_ref, buf_ref, acc_ref, fsem, asem):
    def arrive(c):
        return pltpu.make_async_copy(arr_ref.at[pl.ds(c * 32, 32)], buf_ref.at[c], asem.at[c])
    def fetch(s):
        return pltpu.make_async_copy(front_ref.at[:, 0, :, s, 0, :], acc_ref.at[s], fsem.at[s])
    for s in range(2):
        fetch(s).start()
    for c in range(8):
        arrive(c).start()
    for s in range(2):
        fetch(s).wait()
    for c in range(8):
        arrive(c).wait()
        def add(k, carry):
            slot = land_ref[c * 32 + k]
            s, q = slot % 32, slot // 32
            @pl.when((slot >= 0) & (s < 2))
            def _():
                acc_ref[s, q] = acc_ref[s, q] + buf_ref[c, k].astype(F32)
            return carry
        lax.fori_loop(0, 32, add, 0)
    out_ref[...] = acc_ref[...]


def head(land, front, arrived):
    return pl.pallas_call(
        head_kernel,
        out_shape=jax.ShapeDtypeStruct((2, 4, 128, 128), F32),
        grid_spec=pltpu.PrefetchScalarGridSpec(
            num_scalar_prefetch=1, grid=(1,),
            in_specs=[pl.BlockSpec(memory_space=ANY)] * 2,
            out_specs=pl.BlockSpec((2, 4, 128, 128), lambda g, a: (0, 0, 0, 0)),
            scratch_shapes=[V((8, 32, 128, 128), BF), V((2, 4, 128, 128), F32),
                            pltpu.SemaphoreType.DMA((2,)), pltpu.SemaphoreType.DMA((8,))]),
        compiler_params=pltpu.CompilerParams(vmem_limit_bytes=60 << 20),
        name="head",
    )(land, front, arrived)


def fin_kernel(land_ref, front_ref, arr_ref, brow_ref, bcol_ref, out_ref, buf_ref, acc_ref, bc_ref, fsem, asem, bsem, osem):
    def arrive(c):
        return pltpu.make_async_copy(arr_ref.at[pl.ds(c * 32, 32)], buf_ref.at[c], asem.at[c])
    def fetch(s):
        return pltpu.make_async_copy(front_ref.at[:, 0, :, s, 0, :], acc_ref.at[s], fsem.at[s])
    def column(s):
        return pltpu.make_async_copy(bcol_ref.at[s % 8, s // 8], bc_ref.at[pl.ds(s * 128, 128)], bsem.at[s])
    def put(s):
        return pltpu.make_async_copy(acc_ref.at[s], out_ref.at[:, 0, :, s, 0, :], osem.at[s])
    def each(low, high, f):
        def go(s, c):
            f(s)
            return c
        lax.fori_loop(low, high, go, 0)
    each(0, 32, lambda s: fetch(s).start())
    for c in range(8):
        arrive(c).start()
    each(2, 32, lambda s: column(s).start())
    each(0, 32, lambda s: fetch(s).wait())
    for c in range(8):
        arrive(c).wait()
        def add(k, carry):
            slot = land_ref[c * 32 + k]
            @pl.when(slot >= 0)
            def _():
                s, q = slot % 32, slot // 32
                acc_ref[s, q] = acc_ref[s, q] + buf_ref[c, k].astype(F32)
            return carry
        lax.fori_loop(0, 32, add, 0)
    for s in range(2):
        put(s).start()
    def update(g, carry):
        s = 2 * g
        column(s).wait()
        column(s + 1).wait()
        y = lax.dot_general(brow_ref[...], bc_ref[pl.ds(pl.multiple_of(g * 256, 256), 256), :],
                            (((1,), (1,)), ((), ())), preferred_element_type=F32)
        for u in range(2):
            acc_ref[s + u] = acc_ref[s + u] - y[:, u * 128:(u + 1) * 128].reshape(4, 128, 128)
            put(s + u).start()
        return carry
    lax.fori_loop(1, 16, update, 0)
    each(0, 32, lambda s: put(s).wait())


def fin(land, front, arrived, brow, bcol):
    D = pltpu.SemaphoreType.DMA
    return pl.pallas_call(
        fin_kernel,
        out_shape=jax.ShapeDtypeStruct((4, 1, 128, 32, 1, 128), F32),
        grid_spec=pltpu.PrefetchScalarGridSpec(
            num_scalar_prefetch=1, grid=(1,),
            in_specs=[pl.BlockSpec(memory_space=ANY)] * 2
            + [pl.BlockSpec((512, 1024), lambda g, a: (0, 0), pipeline_mode=pl.Buffered(1)), pl.BlockSpec(memory_space=ANY)],
            out_specs=pl.BlockSpec(memory_space=ANY),
            scratch_shapes=[V((8, 32, 128, 128), BF), V((32, 4, 128, 128), F32), V((4096, 1024), BF),
                            D((32,)), D((8,)), D((32,)), D((32,))]),
        compiler_params=pltpu.CompilerParams(vmem_limit_bytes=60 << 20),
        name="fin",
    )(land, front, arrived, brow, bcol)


def solve_kernel(a_ref, hi_ref, lo_ref, b_ref):
    a = a_ref[...]
    ah = a.astype(BF)
    al = (a - ah.astype(F32)).astype(BF)
    def mm(x, y):
        return lax.dot_general(x, y, (((1,), (1,)), ((), ())), preferred_element_type=F32)
    b_ref[...] = (mm(ah, hi_ref[...]) + (mm(ah, lo_ref[...]) + mm(al, hi_ref[...]))).astype(BF)


def solve(a, hi, lo):
    full = pl.BlockSpec((1024, 1024), lambda g: (0, 0), pipeline_mode=pl.Buffered(1))
    return pl.pallas_call(
        solve_kernel,
        out_shape=jax.ShapeDtypeStruct((512, 1024), BF),
        grid=(4,),
        in_specs=[pl.BlockSpec((128, 1024), lambda g: (g, 0)), full, full],
        out_specs=pl.BlockSpec((128, 1024), lambda g: (g, 0)),
        compiler_params=pltpu.CompilerParams(vmem_limit_bytes=24 << 20),
        name="solve",
    )(a, hi, lo)


def local(front, child_tiles, tile_owner, tile_slot):
    sub = lax.axis_index("sub")
    row = lax.axis_index("row")
    col = lax.axis_index("col")
    group = sub * 4 + row
    outgoing, targets = route(tile_owner[:, 0], tile_slot, child_tiles)
    landing = lax.all_to_all(targets.reshape(128, 2), ("sub", "row", "col"), split_axis=0, concat_axis=0, tiled=True).reshape(256)
    corner = front[0, 0, :, :2, 0, :].transpose(1, 0, 2)
    held = jnp.stack([jnp.where(sub == g, corner, jnp.zeros_like(corner)) for g in range(2)])
    held = lax.psum(held, "sub")
    lead = lax.all_gather(held, ("row", "col"), axis=0, tiled=False)
    lead = lead.reshape(4, 4, 2, 2, 128, 128).transpose(2, 0, 3, 1, 4, 5).reshape(8, 8, 128, 128)
    outgoing, lead = lax.optimization_barrier((outgoing, lead))
    arrived = lax.all_to_all(outgoing, ("sub", "row", "col"), split_axis=0, concat_axis=0, tiled=True)
    arrived = arrived.reshape(256, 128, 128)
    factor, hi, lo = chol(lead)
    panel = head(landing, front, arrived)
    wide = lax.all_gather(panel, "col", axis=0, tiled=False)
    wide = wide.transpose(2, 3, 1, 0, 4).reshape(512, 1024) if False else wide.transpose(2, 3, 1, 0, 4).reshape(4 * 128, 1024)
    solved = solve(wide, hi, lo)
    return solved, factor, landing, arrived, front, sub, row, col, group


def finish(front, child_tiles, tile_owner, tile_slot):
    solved, factor, landing, arrived, front, sub, row, col, group = local(front, child_tiles, tile_owner, tile_slot)
    mine = lax.dynamic_slice_in_dim(factor, jnp.minimum(group, 7) * 128, 128, 0)
    top = group < 8
    brow = solved.reshape(4, 128, 1024)
    rows = brow.at[0].set(jnp.where(top, mine, brow[0]))
    panel_out = lax.dynamic_index_in_dim(rows.reshape(4, 128, 2, 4, 128), col, 3, keepdims=True)
    panel_out = panel_out.reshape(4, 1, 128, 2, 1, 128)
    brow = brow.at[0].set(jnp.where(top, jnp.zeros_like(mine), brow[0])).reshape(512, 1024)
    across = lax.psum(jnp.where(row == col, solved, jnp.zeros_like(solved)), "row")
    bcol = lax.all_gather(across.reshape(1, 4, 128, 1024), "sub", axis=0, tiled=True)
    return fin(landing, front, arrived, brow, bcol), panel_out


def solution(mesh):
    return jax.shard_map(
        finish,
        mesh=mesh,
        in_specs=(
            P(None, ("sub", "row"), None, None, "col", None),
            P(("sub", "row", "col"), None, None),
            P(("sub", "row", "col"), None),
            P(("sub", "row", "col")),
        ),
        out_specs=(
            P(None, ("sub", "row"), None, None, "col", None),
            P(None, ("sub", "row"), None, None, "col", None),
        ),
        check_vma=False,
    )
```

```python
import jax
import jax.numpy as jnp
from jax import lax
from jax.experimental import pallas as pl
from jax.experimental.pallas import tpu as pltpu
from jax.sharding import PartitionSpec as P

F32, BF = jnp.float32, jnp.bfloat16
HI = lax.Precision.HIGHEST
V = pltpu.VMEM
ANY = pl.ANY
MESH = pl.DeviceIdType.MESH


def nt(a, b):
    return lax.dot_general(a, b, (((1,), (1,)), ((), ())), precision=HI, preferred_element_type=F32)


def nn(a, b):
    return lax.dot_general(a, b, (((1,), (0,)), ((), ())), precision=HI, preferred_element_type=F32)


def split3(x):
    h = x.astype(BF).astype(F32)
    r = x - h
    m = r.astype(BF).astype(F32)
    return h, m, r - m


def diag_factor(d_ref, u_ref, x_ref, cb_ref, r_ref):
    def body(b, carry):
        r0 = pl.multiple_of(b * 8, 8)
        block = d_ref[pl.ds(r0, 8), 0:128]
        rolled = pltpu.roll(block, (128 - r0) % 128, 1)
        for j in range(8):
            cb_ref[j] = jnp.broadcast_to(rolled[:, j:j + 1], (8, 128))
        r_ref[:, 0:128] = block
        r_ref[:, 128:256] = d_ref[pl.ds(r0, 8), 128:256]
        e = {}
        for i in range(8):
            for j in range(i + 1):
                e[i, j] = cb_ref[j, i:i + 1, :]
        rows = []
        for i in range(8):
            rows.append([r_ref[i:i + 1, 0:128], r_ref[i:i + 1, 128:256]])
        for j in range(8):
            inv = lax.rsqrt(e[j, j])
            low = {}
            for i in range(j + 1, 8):
                low[i] = e[i, j] * inv
            for h in range(2):
                rows[j][h] = rows[j][h] * inv
            for i in range(j + 1, 8):
                for m in range(j + 1, i + 1):
                    e[i, m] = e[i, m] - low[i] * low[m]
                for h in range(2):
                    rows[i][h] = rows[i][h] - low[i] * rows[j][h]
        for i in range(8):
            r_ref[i:i + 1, 0:128] = rows[i][0]
            r_ref[i:i + 1, 128:256] = rows[i][1]
        r = r_ref[...]
        u_ref[pl.ds(r0, 8), :] = r[:, 0:128]
        x_ref[pl.ds(r0, 8), :] = r[:, 128:256]
        h, m, l = split3(r)
        left = jnp.concatenate([h, h, m, h, l, m], 0)[:, 0:128].astype(BF)
        right = jnp.concatenate([h, m, h, l, h, m], 0).astype(BF)
        d_ref[...] = d_ref[...] - lax.dot_general(left, right, (((0,), (0,)), ((), ())), preferred_element_type=F32)
        return carry
    lax.fori_loop(0, 16, body, 0)


def chol_kernel(lead_ref, l_ref, hi_ref, lo_ref, s_ref, w_ref, d_ref, u_ref, x_ref, cb_ref, r_ref):
    row = lax.broadcasted_iota(jnp.int32, (128, 128), 0)
    col = lax.broadcasted_iota(jnp.int32, (128, 128), 1)
    eye = (row == col).astype(F32)
    n = 8
    for i in range(n):
        for j in range(i + 1):
            t = lead_ref[i, j]
            if i == j:
                t = jnp.where(row >= col, t, t.T)
            s_ref[i * 128:(i + 1) * 128, j * 128:(j + 1) * 128] = t
    w_ref[...] = jnp.zeros_like(w_ref)
    l_ref[...] = jnp.zeros_like(l_ref)
    for k in range(n):
        a, b = k * 128, (k + 1) * 128
        d_ref[:, 0:128] = s_ref[a:b, a:b]
        d_ref[:, 128:256] = eye
        diag_factor(d_ref, u_ref, x_ref, cb_ref, r_ref)
        x = x_ref[...]
        l_ref[a:b, a:b] = jnp.where(row >= col, u_ref[...].T, 0.0).astype(BF)
        if k > 0:
            w_ref[a:b, 0:a] = nn(x, w_ref[a:b, 0:a])
        w_ref[a:b, a:b] = x
        if k < n - 1:
            p = nt(s_ref[b:, a:b], x)
            s_ref[b:, a:b] = p
            l_ref[b:, a:b] = p.astype(BF)
            for j in range(k + 1, n):
                c, d = j * 128, (j + 1) * 128
                s_ref[c:, c:d] = s_ref[c:, c:d] - nt(s_ref[c:, a:b], s_ref[c:d, a:b])
            w_ref[b:, 0:b] = w_ref[b:, 0:b] - nn(p, w_ref[a:b, 0:b])
    for k in range(n):
        a, b = k * 128, (k + 1) * 128
        y = w_ref[a:b, :]
        h = y.astype(BF)
        hi_ref[a:b, :] = h
        lo_ref[a:b, :] = (y - h.astype(F32)).astype(BF)


def chol(lead):
    return pl.pallas_call(
        chol_kernel,
        out_shape=[jax.ShapeDtypeStruct((1024, 1024), BF)] * 3,
        in_specs=[pl.BlockSpec(memory_space=V)],
        out_specs=[pl.BlockSpec(memory_space=V)] * 3,
        scratch_shapes=[V((1024, 1024), F32), V((1024, 1024), F32), V((128, 256), F32), V((128, 128), F32),
                        V((128, 128), F32), V((8, 8, 128), F32), V((8, 256), F32)],
        compiler_params=pltpu.CompilerParams(vmem_limit_bytes=30 << 20),
        name="chol",
    )(lead)


def route_kernel(own_ref, child_ref, out_ref, idx_ref, cnt_ref):
    step = pl.program_id(0)

    @pl.when(step == 0)
    def _():
        def clear(k, c):
            cnt_ref[k] = 0
            for u in range(2):
                idx_ref[2 * k + u] = 0
            return c
        lax.fori_loop(0, 128, clear, 0)

        def place(k, c):
            o = own_ref[k]
            n = cnt_ref[o]
            idx_ref[2 * o + n] = k
            cnt_ref[o] = n + 1
            return c
        lax.fori_loop(0, 128, place, 0)

    def copy(j, c):
        for u in range(2):
            out_ref[j, u] = child_ref[idx_ref[step * 32 + 2 * j + u]]
        return c
    lax.fori_loop(0, 16, copy, 0)


def route(owner, child):
    return pl.pallas_call(
        route_kernel,
        out_shape=jax.ShapeDtypeStruct((128, 2, 128, 128), BF),
        grid_spec=pltpu.PrefetchScalarGridSpec(
            num_scalar_prefetch=1, grid=(8,),
            in_specs=[pl.BlockSpec((128, 128, 128), lambda g, a: (0, 0, 0), pipeline_mode=pl.Buffered(1))],
            out_specs=pl.BlockSpec((16, 2, 128, 128), lambda g, a: (g, 0, 0, 0)),
            scratch_shapes=[pltpu.SMEM((256,), jnp.int32), pltpu.SMEM((128,), jnp.int32)]),
        compiler_params=pltpu.CompilerParams(vmem_limit_bytes=60 << 20),
        name="route",
    )(owner, child)


def head_kernel(land_ref, front_ref, arr_ref, out_ref, buf_ref, acc_ref, fsem, asem):
    def arrive(c):
        return pltpu.make_async_copy(arr_ref.at[pl.ds(c * 32, 32)], buf_ref.at[c], asem.at[c])
    def fetch(s):
        return pltpu.make_async_copy(front_ref.at[:, 0, :, s, 0, :], acc_ref.at[s], fsem.at[s])
    for s in range(2):
        fetch(s).start()
    for c in range(8):
        arrive(c).start()
    for s in range(2):
        fetch(s).wait()
    for c in range(8):
        arrive(c).wait()
        def add(k, carry):
            slot = land_ref[c * 32 + k]
            s, q = slot % 32, slot // 32
            @pl.when((slot >= 0) & (s < 2))
            def _():
                acc_ref[s, q] = acc_ref[s, q] + buf_ref[c, k].astype(F32)
            return carry
        lax.fori_loop(0, 32, add, 0)
    out_ref[...] = acc_ref[...]


def head(land, front, arrived):
    return pl.pallas_call(
        head_kernel,
        out_shape=jax.ShapeDtypeStruct((2, 4, 128, 128), F32),
        grid_spec=pltpu.PrefetchScalarGridSpec(
            num_scalar_prefetch=1, grid=(1,),
            in_specs=[pl.BlockSpec(memory_space=ANY)] * 2,
            out_specs=pl.BlockSpec((2, 4, 128, 128), lambda g, a: (0, 0, 0, 0)),
            scratch_shapes=[V((8, 32, 128, 128), BF), V((2, 4, 128, 128), F32),
                            pltpu.SemaphoreType.DMA((2,)), pltpu.SemaphoreType.DMA((8,))]),
        compiler_params=pltpu.CompilerParams(vmem_limit_bytes=60 << 20),
        name="head",
    )(land, front, arrived)


def fin_kernel(land_ref, front_ref, arr_ref, brow_ref, bcol_ref, out_ref, buf_ref, acc_ref, bc_ref, fsem, asem, bsem, osem):
    def arrive(c):
        return pltpu.make_async_copy(arr_ref.at[pl.ds(c * 32, 32)], buf_ref.at[c], asem.at[c])
    def fetch(s):
        return pltpu.make_async_copy(front_ref.at[:, 0, :, s, 0, :], acc_ref.at[s], fsem.at[s])
    def column(s):
        return pltpu.make_async_copy(bcol_ref.at[s % 8, s // 8], bc_ref.at[pl.ds(s * 128, 128)], bsem.at[s])
    def put(s):
        return pltpu.make_async_copy(acc_ref.at[s], out_ref.at[:, 0, :, s, 0, :], osem.at[s])
    def each(low, high, f):
        def go(s, c):
            f(s)
            return c
        lax.fori_loop(low, high, go, 0)
    each(0, 32, lambda s: fetch(s).start())
    for c in range(8):
        arrive(c).start()
    each(2, 32, lambda s: column(s).start())
    each(0, 32, lambda s: fetch(s).wait())
    for c in range(8):
        arrive(c).wait()
        def add(k, carry):
            slot = land_ref[c * 32 + k]
            @pl.when(slot >= 0)
            def _():
                s, q = slot % 32, slot // 32
                acc_ref[s, q] = acc_ref[s, q] + buf_ref[c, k].astype(F32)
            return carry
        lax.fori_loop(0, 32, add, 0)
    for s in range(2):
        put(s).start()
    def update(g, carry):
        s = 2 * g
        column(s).wait()
        column(s + 1).wait()
        y = lax.dot_general(brow_ref[...], bc_ref[pl.ds(pl.multiple_of(g * 256, 256), 256), :],
                            (((1,), (1,)), ((), ())), preferred_element_type=F32)
        for u in range(2):
            acc_ref[s + u] = acc_ref[s + u] - y[:, u * 128:(u + 1) * 128].reshape(4, 128, 128)
            put(s + u).start()
        return carry
    lax.fori_loop(1, 16, update, 0)
    each(0, 32, lambda s: put(s).wait())


def fin(land, front, arrived, brow, bcol):
    D = pltpu.SemaphoreType.DMA
    return pl.pallas_call(
        fin_kernel,
        out_shape=jax.ShapeDtypeStruct((4, 1, 128, 32, 1, 128), F32),
        grid_spec=pltpu.PrefetchScalarGridSpec(
            num_scalar_prefetch=1, grid=(1,),
            in_specs=[pl.BlockSpec(memory_space=ANY)] * 2
            + [pl.BlockSpec((512, 1024), lambda g, a: (0, 0), pipeline_mode=pl.Buffered(1)), pl.BlockSpec(memory_space=ANY)],
            out_specs=pl.BlockSpec(memory_space=ANY),
            scratch_shapes=[V((8, 32, 128, 128), BF), V((32, 4, 128, 128), F32), V((4096, 1024), BF),
                            D((32,)), D((8,)), D((32,)), D((32,))]),
        compiler_params=pltpu.CompilerParams(vmem_limit_bytes=60 << 20),
        name="fin",
    )(land, front, arrived, brow, bcol)


def solve_kernel(a_ref, hi_ref, lo_ref, b_ref):
    a = a_ref[...]
    ah = a.astype(BF)
    al = (a - ah.astype(F32)).astype(BF)
    def mm(x, y):
        return lax.dot_general(x, y, (((1,), (1,)), ((), ())), preferred_element_type=F32)
    b_ref[...] = (mm(ah, hi_ref[...]) + (mm(ah, lo_ref[...]) + mm(al, hi_ref[...]))).astype(BF)


def solve(a, hi, lo):
    full = pl.BlockSpec((1024, 1024), lambda g: (0, 0), pipeline_mode=pl.Buffered(1))
    return pl.pallas_call(
        solve_kernel,
        out_shape=jax.ShapeDtypeStruct((512, 1024), BF),
        grid=(4,),
        in_specs=[pl.BlockSpec((128, 1024), lambda g: (g, 0)), full, full],
        out_specs=pl.BlockSpec((128, 1024), lambda g: (g, 0)),
        compiler_params=pltpu.CompilerParams(vmem_limit_bytes=24 << 20),
        name="solve",
    )(a, hi, lo)


def lead_kernel(front_ref, code_ref, lead_ref, codes_ref, own_ref, lsem, zs, zr, zls, zlr, xs, xr, ys, yr, as_, ar, bs, br, cs, cr):
    sub, row, col = lax.axis_index("sub"), lax.axis_index("row"), lax.axis_index("col")
    par = lax.rem(sub, 2)
    mate = sub + 1 - 2 * par
    line = 4 * par + row
    need = (par == 1) | (col <= row)

    def remote(src, dst, send, recv, **where):
        return pltpu.make_async_remote_copy(src, dst, send, recv, device_id=where, device_id_type=MESH)

    barrier = pltpu.get_barrier_semaphore()
    for d in range(1, 8):
        pl.semaphore_signal(barrier, inc=1, device_id={"sub": lax.rem(sub + d, 8)}, device_id_type=MESH)
    for d in range(1, 4):
        pl.semaphore_signal(barrier, inc=1, device_id={"row": lax.rem(row + d, 4)}, device_id_type=MESH)
        pl.semaphore_signal(barrier, inc=1, device_id={"col": lax.rem(col + d, 4)}, device_id_type=MESH)

    mine = [pltpu.make_async_copy(front_ref.at[0, 0, :, s, 0, :], own_ref.at[s], lsem.at[s]) for s in range(2)]
    code = pltpu.make_async_copy(code_ref, codes_ref.at[col, row, sub], lsem.at[2])
    code.start()
    mine[0].start()
    mine[1].start()
    mine[0].wait()
    mine[1].wait()
    keep = [pltpu.make_async_copy(own_ref.at[s], lead_ref.at[line, 4 * s + col], lsem.at[3 + s]) for s in range(2)]

    @pl.when(sub < 2)
    def _():
        keep[0].start()
        keep[1].start()
    pl.semaphore_wait(barrier, 13)

    def zcode(d):
        return remote(code_ref, codes_ref.at[col, row, sub], zs.at[d - 1], zr.at[d - 1], sub=lax.rem(sub + d, 8))
    def zcode_in(d):
        return remote(code_ref, codes_ref.at[col, row, lax.rem(sub + 8 - d, 8)], zs.at[d - 1], zr.at[d - 1], sub=lax.rem(sub + d, 8))
    need1 = (par == 1) & (col <= row)

    @pl.when(sub < 2)
    def _():
        for d in (1, 3, 2):
            @pl.when(need)
            def _():
                remote(own_ref.at[0], lead_ref.at[line, col], zls.at[d - 1, 0], zlr.at[0], sub=sub + 2 * d).start()
            @pl.when(need1)
            def _():
                remote(own_ref.at[1], lead_ref.at[line, 4 + col], zls.at[d - 1, 1], zlr.at[1], sub=sub + 2 * d).start()
    for d in range(1, 8):
        zcode(d).start()

    @pl.when(sub < 2)
    def _():
        keep[0].wait()
        keep[1].wait()

    @pl.when(sub >= 2)
    def _():
        @pl.when(need)
        def _():
            remote(own_ref.at[0], lead_ref.at[line, col], zls.at[0, 0], zlr.at[0], sub=par).wait_recv()
        @pl.when(need1)
        def _():
            remote(own_ref.at[1], lead_ref.at[line, 4 + col], zls.at[0, 1], zlr.at[1], sub=par).wait_recv()

    def ax(d, r):
        return remote(lead_ref.at[4 + r, col], lead_ref.at[4 + r, col], as_.at[0, d - 1], ar.at[0, d - 1], row=lax.rem(row + d, 4))
    def ay(d, c):
        return remote(lead_ref.at[pl.ds(4, 4), c], lead_ref.at[pl.ds(4, 4), c], as_.at[1, d - 1], ar.at[1, d - 1], col=lax.rem(col + d, 4))
    def by(d, c):
        at = lead_ref.at[line, 4 * par + c]
        return remote(at, at, bs.at[d - 1, 4], br.at[d - 1, 4], col=lax.rem(col + d, 4))
    def bx(d, r, c):
        at = lead_ref.at[4 * par + r, 4 * par + c]
        return remote(at, at, bs.at[d - 1, c], br.at[d - 1, c], row=lax.rem(row + d, 4))
    for d in (1, 3, 2):
        @pl.when(par == 1)
        def _():
            ax(d, row).start()
        @pl.when(col <= row)
        def _():
            by(d, col).start()
    code.wait()
    for d in range(1, 8):
        zcode_in(d).wait_recv()
    def cx(d, r):
        return remote(codes_ref.at[col, r], codes_ref.at[col, r], xs.at[d - 1], xr.at[d - 1], row=lax.rem(row + d, 4))
    def cy(d, c):
        return remote(codes_ref.at[c], codes_ref.at[c], ys.at[d - 1], yr.at[d - 1], col=lax.rem(col + d, 4))
    for d in range(1, 4):
        cx(d, row).start()
    for d in range(1, 4):
        @pl.when(par == 1)
        def _():
            ax(d, lax.rem(row + 4 - d, 4)).wait_recv()
        @pl.when(lax.rem(col + 4 - d, 4) <= row)
        def _():
            by(d, lax.rem(col + 4 - d, 4)).wait_recv()
    for d in (1, 3, 2):
        @pl.when(par == 1)
        def _():
            ay(d, col).start()
        for c in range(4):
            @pl.when(c <= row)
            def _():
                bx(d, row, c).start()
    for d in range(1, 4):
        cx(d, lax.rem(row + 4 - d, 4)).wait_recv()
    for d in range(1, 4):
        cy(d, col).start()
    for d in range(1, 4):
        @pl.when(par == 1)
        def _():
            ay(d, lax.rem(col + 4 - d, 4)).wait_recv()
        for c in range(4):
            r = lax.rem(row + 4 - d, 4)
            @pl.when(c <= r)
            def _():
                bx(d, r, c).wait_recv()

    def swap(i):
        at = lead_ref.at[i, pl.ds(0, i + 1)]
        return remote(at, at, cs.at[i % 4], cr.at[i % 4], sub=mate)
    for i in range(8):
        @pl.when(par == i // 4)
        def _():
            swap(i).start()
    for i in range(8):
        @pl.when(par != i // 4)
        def _():
            swap(i).wait_recv()
    for d in range(1, 4):
        cy(d, lax.rem(col + 4 - d, 4)).wait_recv()

    for d in range(1, 8):
        zcode(d).wait_send()
    @pl.when(sub < 2)
    def _():
        for d in (1, 2, 3):
            @pl.when(need)
            def _():
                remote(own_ref.at[0], lead_ref.at[line, col], zls.at[d - 1, 0], zlr.at[0], sub=sub + 2 * d).wait_send()
            @pl.when(need1)
            def _():
                remote(own_ref.at[1], lead_ref.at[line, 4 + col], zls.at[d - 1, 1], zlr.at[1], sub=sub + 2 * d).wait_send()
    for d in range(1, 4):
        cx(d, row).wait_send()
        cy(d, col).wait_send()
        @pl.when(par == 1)
        def _():
            ax(d, row).wait_send()
            ay(d, col).wait_send()
        @pl.when(col <= row)
        def _():
            by(d, col).wait_send()
        for c in range(4):
            @pl.when(c <= row)
            def _():
                bx(d, row, c).wait_send()
    for i in range(8):
        @pl.when(par == i // 4)
        def _():
            swap(i).wait_send()


def lead_gather(front, code):
    D = pltpu.SemaphoreType.DMA
    return pl.pallas_call(
        lead_kernel,
        out_shape=(jax.ShapeDtypeStruct((8, 8, 128, 128), F32), jax.ShapeDtypeStruct((4, 4, 8, 1, 128), jnp.int32)),
        in_specs=[pl.BlockSpec(memory_space=pltpu.HBM), pl.BlockSpec(memory_space=V)],
        out_specs=(pl.BlockSpec(memory_space=V), pl.BlockSpec(memory_space=V)),
        scratch_shapes=[V((2, 128, 128), F32), D((5,)), D((7,)), D((7,)), D((3, 2)), D((2,)), D((3,)), D((3,)), D((3,)), D((3,)),
                        D((2, 3)), D((2, 3)), D((3, 5)), D((3, 5)), D((4,)), D((4,))],
        compiler_params=pltpu.CompilerParams(vmem_limit_bytes=24 << 20, collective_id=1, has_side_effects=True),
        name="lead",
    )(front, code)


def landings(codes, me):
    codes = codes[:, :, :, 0, :].transpose(2, 1, 0, 3).reshape(128, 128)
    place = lax.broadcasted_iota(jnp.int32, (128, 128), 1) * 128 + codes % 128
    match = codes // 128 == me
    first = jnp.min(jnp.where(match, place, 1 << 20), 1)
    last = jnp.max(jnp.where(match, place, -1), 1)
    one = jnp.where(last >= 0, first % 128, -1)
    two = jnp.where(last > first, last % 128, -1)
    return jnp.stack([one, two], 1).reshape(256)


def local(front, child_tiles, tile_owner, tile_slot):
    sub = lax.axis_index("sub")
    row = lax.axis_index("row")
    col = lax.axis_index("col")
    group = sub * 4 + row
    owner = tile_owner[:, 0]
    outgoing = route(owner, child_tiles)
    lead, codes = lead_gather(front, (owner * 128 + tile_slot).reshape(1, 128))
    outgoing, lead = lax.optimization_barrier((outgoing, lead))
    arrived = lax.all_to_all(outgoing, ("sub", "row", "col"), split_axis=0, concat_axis=0, tiled=True)
    arrived = arrived.reshape(256, 128, 128)
    factor, hi, lo = chol(lead)
    landing = landings(codes, group * 4 + col)
    panel = head(landing, front, arrived)
    wide = lax.all_gather(panel, "col", axis=0, tiled=False)
    wide = wide.transpose(2, 3, 1, 0, 4).reshape(512, 1024)
    solved = solve(wide, hi, lo)
    return solved, factor, landing, arrived, front, sub, row, col, group


def finish(front, child_tiles, tile_owner, tile_slot):
  solved, factor, landing, arrived, front, _, row, col, group = local(front, child_tiles, tile_owner, tile_slot)
  mine = lax.dynamic_slice_in_dim(factor, jnp.minimum(group, 7) * 128, 128, 0)
  top = group < 8
  brow = solved.reshape(4, 128, 1024)
  rows = brow.at[0].set(jnp.where(top, mine, brow[0]))
  panel_out = lax.dynamic_index_in_dim(rows.reshape(4, 128, 2, 4, 128), col, 3, keepdims=True)
  panel_out = panel_out.reshape(4, 1, 128, 2, 1, 128)
  brow = brow.at[0].set(jnp.where(top, jnp.zeros_like(mine), brow[0])).reshape(512, 1024)
  across = lax.psum(jnp.where(row == col, solved, jnp.zeros_like(solved)), "row")
  bcol = lax.all_gather(across.reshape(1, 4, 128, 1024), "sub", axis=0, tiled=True)
  return fin(landing, front, arrived, brow, bcol), panel_out


def solution(mesh):
    return jax.shard_map(
        finish,
        mesh=mesh,
        in_specs=(
            P(None, ("sub", "row"), None, None, "col", None),
            P(("sub", "row", "col"), None, None),
            P(("sub", "row", "col"), None),
            P(("sub", "row", "col")),
        ),
        out_specs=(
            P(None, ("sub", "row"), None, None, "col", None),
            P(None, ("sub", "row"), None, None, "col", None),
        ),
        check_vma=False,
    )
```

```python
import jax
import jax.numpy as jnp
from jax import lax
from jax.experimental import pallas as pl
from jax.experimental.pallas import tpu as pltpu
from jax.sharding import PartitionSpec as P

F32, BF = jnp.float32, jnp.bfloat16
HI = lax.Precision.HIGHEST
V = pltpu.VMEM
ANY = pl.ANY
MESH = pl.DeviceIdType.MESH


def nt(a, b):
    return lax.dot_general(a, b, (((1,), (1,)), ((), ())), precision=HI, preferred_element_type=F32)


def nn(a, b):
    return lax.dot_general(a, b, (((1,), (0,)), ((), ())), precision=HI, preferred_element_type=F32)


def split3(x):
    h = x.astype(BF).astype(F32)
    r = x - h
    m = r.astype(BF).astype(F32)
    return h, m, r - m


def diag_factor(d_ref, u_ref, x_ref, cb_ref, r_ref):
    def body(b, carry):
        r0 = pl.multiple_of(b * 8, 8)
        block = d_ref[pl.ds(r0, 8), 0:128]
        rolled = pltpu.roll(block, (128 - r0) % 128, 1)
        for j in range(8):
            cb_ref[j] = jnp.broadcast_to(rolled[:, j:j + 1], (8, 128))
        r_ref[:, 0:128] = block
        r_ref[:, 128:256] = d_ref[pl.ds(r0, 8), 128:256]
        e = {}
        for i in range(8):
            for j in range(i + 1):
                e[i, j] = cb_ref[j, i:i + 1, :]
        rows = []
        for i in range(8):
            rows.append([r_ref[i:i + 1, 0:128], r_ref[i:i + 1, 128:256]])
        for j in range(8):
            inv = lax.rsqrt(e[j, j])
            low = {}
            for i in range(j + 1, 8):
                low[i] = e[i, j] * inv
            for h in range(2):
                rows[j][h] = rows[j][h] * inv
            for i in range(j + 1, 8):
                for m in range(j + 1, i + 1):
                    e[i, m] = e[i, m] - low[i] * low[m]
                for h in range(2):
                    rows[i][h] = rows[i][h] - low[i] * rows[j][h]
        for i in range(8):
            r_ref[i:i + 1, 0:128] = rows[i][0]
            r_ref[i:i + 1, 128:256] = rows[i][1]
        r = r_ref[...]
        u_ref[pl.ds(r0, 8), :] = r[:, 0:128]
        x_ref[pl.ds(r0, 8), :] = r[:, 128:256]
        h, m, l = split3(r)
        left = jnp.concatenate([h, h, m, h, l, m], 0)[:, 0:128].astype(BF)
        right = jnp.concatenate([h, m, h, l, h, m], 0).astype(BF)
        d_ref[...] = d_ref[...] - lax.dot_general(left, right, (((0,), (0,)), ((), ())), preferred_element_type=F32)
        return carry
    lax.fori_loop(0, 16, body, 0)


def chol_kernel(lead_ref, l_ref, hi_ref, lo_ref, s_ref, w_ref, d_ref, u_ref, x_ref, cb_ref, r_ref):
    row = lax.broadcasted_iota(jnp.int32, (128, 128), 0)
    col = lax.broadcasted_iota(jnp.int32, (128, 128), 1)
    eye = (row == col).astype(F32)
    n = 8
    for i in range(n):
        for j in range(i + 1):
            t = lead_ref[i, j]
            if i == j:
                t = jnp.where(row >= col, t, t.T)
            s_ref[i * 128:(i + 1) * 128, j * 128:(j + 1) * 128] = t
    w_ref[...] = jnp.zeros_like(w_ref)
    l_ref[...] = jnp.zeros_like(l_ref)
    for k in range(n):
        a, b = k * 128, (k + 1) * 128
        d_ref[:, 0:128] = s_ref[a:b, a:b]
        d_ref[:, 128:256] = eye
        diag_factor(d_ref, u_ref, x_ref, cb_ref, r_ref)
        x = x_ref[...]
        l_ref[a:b, a:b] = jnp.where(row >= col, u_ref[...].T, 0.0).astype(BF)
        if k > 0:
            w_ref[a:b, 0:a] = nn(x, w_ref[a:b, 0:a])
        w_ref[a:b, a:b] = x
        if k < n - 1:
            p = nt(s_ref[b:, a:b], x)
            s_ref[b:, a:b] = p
            l_ref[b:, a:b] = p.astype(BF)
            for j in range(k + 1, n):
                c, d = j * 128, (j + 1) * 128
                s_ref[c:, c:d] = s_ref[c:, c:d] - nt(s_ref[c:, a:b], s_ref[c:d, a:b])
            w_ref[b:, 0:b] = w_ref[b:, 0:b] - nn(p, w_ref[a:b, 0:b])
    for k in range(n):
        a, b = k * 128, (k + 1) * 128
        y = w_ref[a:b, :]
        h = y.astype(BF)
        hi_ref[a:b, :] = h
        lo_ref[a:b, :] = (y - h.astype(F32)).astype(BF)


def chol(lead):
    return pl.pallas_call(
        chol_kernel,
        out_shape=[jax.ShapeDtypeStruct((1024, 1024), BF)] * 3,
        in_specs=[pl.BlockSpec(memory_space=V)],
        out_specs=[pl.BlockSpec(memory_space=V)] * 3,
        scratch_shapes=[V((1024, 1024), F32), V((1024, 1024), F32), V((128, 256), F32), V((128, 128), F32),
                        V((128, 128), F32), V((8, 8, 128), F32), V((8, 256), F32)],
        compiler_params=pltpu.CompilerParams(vmem_limit_bytes=30 << 20),
        name="chol",
    )(lead)


def route_kernel(own_ref, child_ref, out_ref, idx_ref, cnt_ref):
    step = pl.program_id(0)

    @pl.when(step == 0)
    def _():
        def clear(k, c):
            cnt_ref[k] = 0
            for u in range(2):
                idx_ref[2 * k + u] = 0
            return c
        lax.fori_loop(0, 128, clear, 0)

        def place(k, c):
            o = own_ref[k]
            n = cnt_ref[o]
            idx_ref[2 * o + n] = k
            cnt_ref[o] = n + 1
            return c
        lax.fori_loop(0, 128, place, 0)

    def copy(j, c):
        for u in range(2):
            out_ref[j, u] = child_ref[idx_ref[step * 32 + 2 * j + u]]
        return c
    lax.fori_loop(0, 16, copy, 0)


def route(owner, child):
    return pl.pallas_call(
        route_kernel,
        out_shape=jax.ShapeDtypeStruct((128, 2, 128, 128), BF),
        grid_spec=pltpu.PrefetchScalarGridSpec(
            num_scalar_prefetch=1, grid=(8,),
            in_specs=[pl.BlockSpec((128, 128, 128), lambda g, a: (0, 0, 0), pipeline_mode=pl.Buffered(1))],
            out_specs=pl.BlockSpec((16, 2, 128, 128), lambda g, a: (g, 0, 0, 0)),
            scratch_shapes=[pltpu.SMEM((256,), jnp.int32), pltpu.SMEM((128,), jnp.int32)]),
        compiler_params=pltpu.CompilerParams(vmem_limit_bytes=60 << 20),
        name="route",
    )(owner, child)


def head_kernel(land_ref, front_ref, arr_ref, out_ref, buf_ref, acc_ref, fsem, asem):
    def arrive(c):
        return pltpu.make_async_copy(arr_ref.at[pl.ds(c * 32, 32)], buf_ref.at[c], asem.at[c])
    def fetch(s):
        return pltpu.make_async_copy(front_ref.at[:, 0, :, s, 0, :], acc_ref.at[s], fsem.at[s])
    for s in range(2):
        fetch(s).start()
    for c in range(8):
        arrive(c).start()
    for s in range(2):
        fetch(s).wait()
    for c in range(8):
        arrive(c).wait()
        def add(k, carry):
            slot = land_ref[c * 32 + k]
            s, q = slot % 32, slot // 32
            @pl.when((slot >= 0) & (s < 2))
            def _():
                acc_ref[s, q] = acc_ref[s, q] + buf_ref[c, k].astype(F32)
            return carry
        lax.fori_loop(0, 32, add, 0)
    out_ref[...] = acc_ref[...]


def head(land, front, arrived):
    return pl.pallas_call(
        head_kernel,
        out_shape=jax.ShapeDtypeStruct((2, 4, 128, 128), F32),
        grid_spec=pltpu.PrefetchScalarGridSpec(
            num_scalar_prefetch=1, grid=(1,),
            in_specs=[pl.BlockSpec(memory_space=ANY)] * 2,
            out_specs=pl.BlockSpec((2, 4, 128, 128), lambda g, a: (0, 0, 0, 0)),
            scratch_shapes=[V((8, 32, 128, 128), BF), V((2, 4, 128, 128), F32),
                            pltpu.SemaphoreType.DMA((2,)), pltpu.SemaphoreType.DMA((8,))]),
        compiler_params=pltpu.CompilerParams(vmem_limit_bytes=60 << 20),
        name="head",
    )(land, front, arrived)


def fin_kernel(land_ref, front_ref, arr_ref, brow_ref, bcol_ref, out_ref, buf_ref, acc_ref, bc_ref, fsem, asem, bsem, osem):
    def arrive(c):
        return pltpu.make_async_copy(arr_ref.at[pl.ds(c * 32, 32)], buf_ref.at[c], asem.at[c])
    def fetch(s):
        return pltpu.make_async_copy(front_ref.at[:, 0, :, s, 0, :], acc_ref.at[s], fsem.at[s])
    def column(s):
        return pltpu.make_async_copy(bcol_ref.at[s % 8, s // 8], bc_ref.at[pl.ds(s * 128, 128)], bsem.at[s])
    def put(s):
        return pltpu.make_async_copy(acc_ref.at[s], out_ref.at[:, 0, :, s, 0, :], osem.at[s])
    def each(low, high, f):
        def go(s, c):
            f(s)
            return c
        lax.fori_loop(low, high, go, 0)
    each(0, 32, lambda s: fetch(s).start())
    for c in range(8):
        arrive(c).start()
    each(2, 32, lambda s: column(s).start())
    each(0, 32, lambda s: fetch(s).wait())
    for c in range(8):
        arrive(c).wait()
        def add(k, carry):
            slot = land_ref[c * 32 + k]
            @pl.when(slot >= 0)
            def _():
                s, q = slot % 32, slot // 32
                acc_ref[s, q] = acc_ref[s, q] + buf_ref[c, k].astype(F32)
            return carry
        lax.fori_loop(0, 32, add, 0)
    for s in range(2):
        put(s).start()
    def update(g, carry):
        s = 2 * g
        column(s).wait()
        column(s + 1).wait()
        y = lax.dot_general(brow_ref[...], bc_ref[pl.ds(pl.multiple_of(g * 256, 256), 256), :],
                            (((1,), (1,)), ((), ())), preferred_element_type=F32)
        for u in range(2):
            z = y[:, u * 128:(u + 1) * 128].reshape(4, 128, 128)
            acc_ref[s + u, 0] = acc_ref[s + u, 0] - jnp.where(land_ref[256] > 0, z[0], 0.0)
            acc_ref[s + u, 1:4] = acc_ref[s + u, 1:4] - z[1:4]
            put(s + u).start()
        return carry
    lax.fori_loop(1, 16, update, 0)
    each(0, 32, lambda s: put(s).wait())


def fin(land, front, arrived, brow, bcol):
    D = pltpu.SemaphoreType.DMA
    return pl.pallas_call(
        fin_kernel,
        out_shape=jax.ShapeDtypeStruct((4, 1, 128, 32, 1, 128), F32),
        grid_spec=pltpu.PrefetchScalarGridSpec(
            num_scalar_prefetch=1, grid=(1,),
            in_specs=[pl.BlockSpec(memory_space=ANY)] * 2
            + [pl.BlockSpec((512, 1024), lambda g, a: (0, 0), pipeline_mode=pl.Buffered(1)), pl.BlockSpec(memory_space=ANY)],
            out_specs=pl.BlockSpec(memory_space=ANY),
            scratch_shapes=[V((8, 32, 128, 128), BF), V((32, 4, 128, 128), F32), V((4096, 1024), BF),
                            D((32,)), D((8,)), D((32,)), D((32,))]),
        compiler_params=pltpu.CompilerParams(vmem_limit_bytes=60 << 20),
        name="fin",
    )(land, front, arrived, brow, bcol)


def panel_kernel(panel_ref, hi_hbm, lo_hbm, low_hbm, brow_ref, bcol_ref, arow, ah, al, hi, lo, low, xb, rl,
                 lsem, ps, pr, xs, xr, ws, wr, ys, yr, rs, rr, zs, zr, fs, fr, ms, mr):
    sub, row, col = lax.axis_index("sub"), lax.axis_index("row"), lax.axis_index("col")
    group = 4 * sub + row
    mate = sub + 1 - 2 * lax.rem(sub, 2)

    def n4(x, d):
        return lax.rem(x + 4 + d, 4)

    def n8(x, d):
        return lax.rem(x + 8 + d, 8)

    def remote(src, dst, send, recv, **where):
        return pltpu.make_async_remote_copy(src, dst, send, recv, device_id=where, device_id_type=MESH)

    loads = [pltpu.make_async_copy(hi_hbm, hi, lsem.at[0]), pltpu.make_async_copy(lo_hbm, lo, lsem.at[1]),
             pltpu.make_async_copy(low_hbm.at[pl.ds(pl.multiple_of(lax.min(group, 7) * 128, 128), 128)], low, lsem.at[2]),
             pltpu.make_async_copy(panel_ref.at[:, col], arow.at[col], lsem.at[3])]
    barrier = pltpu.get_barrier_semaphore()
    for d in (1, 3):
        pl.semaphore_signal(barrier, inc=1, device_id={"row": n4(row, d)}, device_id_type=MESH)
        pl.semaphore_signal(barrier, inc=1, device_id={"sub": n8(sub, 2 * d if d == 1 else -2)}, device_id_type=MESH)
    for d in (1, 2, 3):
        pl.semaphore_signal(barrier, inc=1, device_id={"col": n4(col, d)}, device_id_type=MESH)
    pl.semaphore_signal(barrier, inc=1, device_id={"sub": mate}, device_id_type=MESH)
    for copy in loads:
        copy.start()
    pl.semaphore_wait(barrier, 8)

    def take(d):
        return remote(panel_ref.at[:, n4(col, d)], arow.at[col], ps.at[d - 1], pr.at[d - 1], col=n4(col, d))
    def taken(d):
        return remote(panel_ref.at[:, n4(col, d)], arow.at[n4(col, -d)], ps.at[d - 1], pr.at[d - 1], col=n4(col, d))
    for d in (1, 3, 2):
        take(d).start()
    loads[3].wait()
    for d in (1, 3, 2):
        taken(d).wait_recv()
    for s in range(2):
        for t in range(4):
            a = arow[t, s]
            h = a.astype(BF)
            at = (4 * s + t) * 128
            ah[:, at:at + 128] = h
            al[:, at:at + 128] = (a - h.astype(F32)).astype(BF)
    for copy in loads[:3]:
        copy.wait()
    top = (group < 8) & (col == 0)

    def mm(x, y):
        return lax.dot_general(x, y, (((1,), (1,)), ((), ())), preferred_element_type=F32)
    for b in range(4):
        w = 256 * (b + 1)
        rows = pl.ds(256 * b, 256)
        y = mm(ah[:, 0:w], hi[rows, 0:w]) + (mm(ah[:, 0:w], lo[rows, 0:w]) + mm(al[:, 0:w], hi[rows, 0:w]))
        y = jnp.where(top, low[:, 256 * b:w], y.astype(BF))
        xb[row, :, 256 * b:w] = y
        brow_ref[col, :, 256 * b:w] = y

    half = [pl.ds(0, 64), pl.ds(64, 64)]
    step = [1, -1]
    def xsend(i):
        return remote(xb.at[row], xb.at[row], xs.at[i], xr.at[i], row=n4(row, step[i]))
    def xrecv(i):
        at = xb.at[n4(row, -step[i])]
        return remote(at, at, xs.at[i], xr.at[i], row=n4(row, step[i]))
    def xforward(i, r):
        at = xb.at[r, half[i]]
        return remote(at, at, xs.at[2 + i], xr.at[2 + i], row=n4(row, step[i]))
    def wsend(i):
        return remote(brow_ref.at[col], brow_ref.at[col], ws.at[i], wr.at[i], col=n4(col, step[i]))
    def wrecv(i):
        at = brow_ref.at[n4(col, -step[i])]
        return remote(at, at, ws.at[i], wr.at[i], col=n4(col, step[i]))
    def wforward(i, c):
        at = brow_ref.at[c, half[i]]
        return remote(at, at, ws.at[2 + i], wr.at[2 + i], col=n4(col, step[i]))

    def ynear(i):
        return remote(xb.at[n4(col, step[i])], bcol_ref.at[sub, col], ys.at[i], yr.at[i], col=n4(col, step[i]))
    def ynear_in(i):
        return remote(xb.at[0], bcol_ref.at[sub, n4(col, -step[i])], ys.at[i], yr.at[i], col=n4(col, step[i]))
    def yfar(i):
        return remote(xb.at[n4(col, 2), half[i]], rl.at[i], rs.at[i], rr.at[i], col=n4(col, step[i]))
    def yrelay(i):
        return remote(rl.at[i], bcol_ref.at[sub, n4(col, -step[i]), half[i]], ys.at[2 + i], yr.at[2 + i], col=n4(col, step[i]))
    def yfar_in(i):
        return remote(rl.at[i], bcol_ref.at[sub, n4(col, 2), half[i]], ys.at[2 + i], yr.at[2 + i], col=n4(col, step[i]))
    home = pltpu.make_async_copy(xb.at[col], bcol_ref.at[sub, col], lsem.at[4])

    def ysend(c):
        d = n4(c, -col)
        @pl.when(d == 0)
        def _():
            home.start()
        for i in range(2):
            @pl.when(d == (1, 3)[i])
            def _():
                ynear(i).start()
        @pl.when(d == 2)
        def _():
            yfar(0).start()
            yfar(1).start()

    for i in range(2):
        xsend(i).start()
    for i in range(2):
        wsend(i).start()
    ysend(row)
    for i in range(2):
        xrecv(i).wait_recv()
        xforward(i, n4(row, -step[i])).start()
        ysend(n4(row, -step[i]))
    for i in range(2):
        wrecv(i).wait_recv()
        wforward(i, n4(col, -step[i])).start()
    for i in range(2):
        xforward(i, n4(row, 2)).wait_recv()
    ysend(n4(row, 2))
    for i in range(2):
        yfar(i).wait_recv()
        yrelay(i).start()

    def own(e, i):
        at = bcol_ref.at[sub, n4(col, e)]
        return remote(at, at, zs.at[i, e], zr.at[i, e], sub=n8(sub, 2 * step[i]))
    def arrive(e, i):
        at = bcol_ref.at[n8(sub, -2 * step[i]), n4(col, e)]
        return remote(at, at, zs.at[i, e], zr.at[i, e], sub=n8(sub, 2 * step[i]))
    side = [0, 0, 1, 1]
    def onward(e, z):
        at = bcol_ref.at[n8(sub, z), n4(col, e)]
        return remote(at, at, fs.at[e], fr.at[e], sub=n8(sub, 2 * step[side[e]]))
    def swap(e, k, z):
        at = bcol_ref.at[n8(sub, z), n4(col, e)]
        return remote(at, at, ms.at[k, e], mr.at[k, e], sub=mate)
    def swapped(e, k, z):
        at = bcol_ref.at[n8(mate, z), n4(col, e)]
        return remote(at, at, ms.at[k, e], mr.at[k, e], sub=mate)

    def launch(e):
        own(e, 0).start()
        own(e, 1).start()
        swap(e, 0, 0).start()
    home.wait()
    launch(0)
    ynear_in(1).wait_recv()
    launch(1)
    ynear_in(0).wait_recv()
    launch(3)
    yfar_in(0).wait_recv()
    yfar_in(1).wait_recv()
    launch(2)
    for e in (0, 1, 3, 2):
        for i in range(2):
            arrive(e, i).wait_recv()
            if side[e] == i:
                onward(e, -2 * step[i]).start()
            swap(e, 1 + i, -2 * step[i]).start()
    for e in (0, 1, 3, 2):
        onward(e, 4).wait_recv()
        swap(e, 3, 4).start()
    for e in range(4):
        swapped(e, 0, 0).wait_recv()
        swapped(e, 1, -2).wait_recv()
        swapped(e, 2, 2).wait_recv()
        swapped(e, 3, 4).wait_recv()
    for i in range(2):
        wforward(i, n4(col, 2)).wait_recv()

    for d in (1, 2, 3):
        take(d).wait_send()
    for i in range(2):
        xsend(i).wait_send()
        wsend(i).wait_send()
        xforward(i, n4(row, -step[i])).wait_send()
        wforward(i, n4(col, -step[i])).wait_send()
        ynear(i).wait_send()
        yfar(i).wait_send()
        yrelay(i).wait_send()
    for e in range(4):
        own(e, 0).wait_send()
        own(e, 1).wait_send()
        onward(e, -2 * step[side[e]]).wait_send()
        swap(e, 0, 0).wait_send()
        swap(e, 1, -2).wait_send()
        swap(e, 2, 2).wait_send()
        swap(e, 3, 4).wait_send()


def panel_exchange(panel, hi, lo, low):
    D = pltpu.SemaphoreType.DMA
    H = pltpu.HBM
    return pl.pallas_call(
        panel_kernel,
        out_shape=(jax.ShapeDtypeStruct((4, 128, 1024), BF), jax.ShapeDtypeStruct((8, 4, 128, 1024), BF)),
        in_specs=[pl.BlockSpec(memory_space=V)] + [pl.BlockSpec(memory_space=H)] * 3,
        out_specs=(pl.BlockSpec(memory_space=V), pl.BlockSpec(memory_space=H)),
        scratch_shapes=[V((4, 2, 128, 128), F32), V((128, 1024), BF), V((128, 1024), BF), V((1024, 1024), BF), V((1024, 1024), BF),
                        V((128, 1024), BF), V((4, 128, 1024), BF), V((2, 64, 1024), BF),
                        D((5,)), D((3,)), D((3,)), D((4,)), D((4,)), D((4,)), D((4,)), D((4,)), D((4,)), D((2,)), D((2,)),
                        D((2, 4)), D((2, 4)), D((4,)), D((4,)), D((4, 4)), D((4, 4))],
        compiler_params=pltpu.CompilerParams(vmem_limit_bytes=60 << 20, collective_id=2, has_side_effects=True),
        name="panel",
    )(panel, hi, lo, low)


def lead_kernel(front_ref, code_ref, lead_ref, codes_ref, own_ref, lsem, zs, zr, zls, zlr, xs, xr, ys, yr, as_, ar, bs, br, cs, cr):
    sub, row, col = lax.axis_index("sub"), lax.axis_index("row"), lax.axis_index("col")
    par = lax.rem(sub, 2)
    mate = sub + 1 - 2 * par
    line = 4 * par + row
    need = (par == 1) | (col <= row)

    def remote(src, dst, send, recv, **where):
        return pltpu.make_async_remote_copy(src, dst, send, recv, device_id=where, device_id_type=MESH)

    barrier = pltpu.get_barrier_semaphore()
    for d in range(1, 8):
        pl.semaphore_signal(barrier, inc=1, device_id={"sub": lax.rem(sub + d, 8)}, device_id_type=MESH)
    for d in range(1, 4):
        pl.semaphore_signal(barrier, inc=1, device_id={"row": lax.rem(row + d, 4)}, device_id_type=MESH)
        pl.semaphore_signal(barrier, inc=1, device_id={"col": lax.rem(col + d, 4)}, device_id_type=MESH)

    mine = [pltpu.make_async_copy(front_ref.at[0, 0, :, s, 0, :], own_ref.at[s], lsem.at[s]) for s in range(2)]
    code = pltpu.make_async_copy(code_ref, codes_ref.at[col, row, sub], lsem.at[2])
    code.start()
    mine[0].start()
    mine[1].start()
    mine[0].wait()
    mine[1].wait()
    keep = [pltpu.make_async_copy(own_ref.at[s], lead_ref.at[line, 4 * s + col], lsem.at[3 + s]) for s in range(2)]

    @pl.when(sub < 2)
    def _():
        keep[0].start()
        keep[1].start()
    pl.semaphore_wait(barrier, 13)

    def zcode(d):
        return remote(code_ref, codes_ref.at[col, row, sub], zs.at[d - 1], zr.at[d - 1], sub=lax.rem(sub + d, 8))
    def zcode_in(d):
        return remote(code_ref, codes_ref.at[col, row, lax.rem(sub + 8 - d, 8)], zs.at[d - 1], zr.at[d - 1], sub=lax.rem(sub + d, 8))
    need1 = (par == 1) & (col <= row)

    @pl.when(sub < 2)
    def _():
        for d in (1, 3, 2):
            @pl.when(need)
            def _():
                remote(own_ref.at[0], lead_ref.at[line, col], zls.at[d - 1, 0], zlr.at[0], sub=sub + 2 * d).start()
            @pl.when(need1)
            def _():
                remote(own_ref.at[1], lead_ref.at[line, 4 + col], zls.at[d - 1, 1], zlr.at[1], sub=sub + 2 * d).start()
    for d in range(1, 8):
        zcode(d).start()

    @pl.when(sub < 2)
    def _():
        keep[0].wait()
        keep[1].wait()

    @pl.when(sub >= 2)
    def _():
        @pl.when(need)
        def _():
            remote(own_ref.at[0], lead_ref.at[line, col], zls.at[0, 0], zlr.at[0], sub=par).wait_recv()
        @pl.when(need1)
        def _():
            remote(own_ref.at[1], lead_ref.at[line, 4 + col], zls.at[0, 1], zlr.at[1], sub=par).wait_recv()

    def ax(d, r):
        return remote(lead_ref.at[4 + r, col], lead_ref.at[4 + r, col], as_.at[0, d - 1], ar.at[0, d - 1], row=lax.rem(row + d, 4))
    def ay(d, c):
        return remote(lead_ref.at[pl.ds(4, 4), c], lead_ref.at[pl.ds(4, 4), c], as_.at[1, d - 1], ar.at[1, d - 1], col=lax.rem(col + d, 4))
    def by(d, c):
        at = lead_ref.at[line, 4 * par + c]
        return remote(at, at, bs.at[d - 1, 4], br.at[d - 1, 4], col=lax.rem(col + d, 4))
    def bx(d, r, c):
        at = lead_ref.at[4 * par + r, 4 * par + c]
        return remote(at, at, bs.at[d - 1, c], br.at[d - 1, c], row=lax.rem(row + d, 4))
    for d in (1, 3, 2):
        @pl.when(par == 1)
        def _():
            ax(d, row).start()
        @pl.when(col <= row)
        def _():
            by(d, col).start()
    code.wait()
    for d in range(1, 8):
        zcode_in(d).wait_recv()
    def cx(d, r):
        return remote(codes_ref.at[col, r], codes_ref.at[col, r], xs.at[d - 1], xr.at[d - 1], row=lax.rem(row + d, 4))
    def cy(d, c):
        return remote(codes_ref.at[c], codes_ref.at[c], ys.at[d - 1], yr.at[d - 1], col=lax.rem(col + d, 4))
    for d in range(1, 4):
        cx(d, row).start()
    for d in range(1, 4):
        @pl.when(par == 1)
        def _():
            ax(d, lax.rem(row + 4 - d, 4)).wait_recv()
        @pl.when(lax.rem(col + 4 - d, 4) <= row)
        def _():
            by(d, lax.rem(col + 4 - d, 4)).wait_recv()
    for d in (1, 3, 2):
        @pl.when(par == 1)
        def _():
            ay(d, col).start()
        for c in range(4):
            @pl.when(c <= row)
            def _():
                bx(d, row, c).start()
    for d in range(1, 4):
        cx(d, lax.rem(row + 4 - d, 4)).wait_recv()
    for d in range(1, 4):
        cy(d, col).start()
    for d in range(1, 4):
        @pl.when(par == 1)
        def _():
            ay(d, lax.rem(col + 4 - d, 4)).wait_recv()
        for c in range(4):
            r = lax.rem(row + 4 - d, 4)
            @pl.when(c <= r)
            def _():
                bx(d, r, c).wait_recv()

    def swap(i):
        at = lead_ref.at[i, pl.ds(0, i + 1)]
        return remote(at, at, cs.at[i % 4], cr.at[i % 4], sub=mate)
    for i in range(8):
        @pl.when(par == i // 4)
        def _():
            swap(i).start()
    for i in range(8):
        @pl.when(par != i // 4)
        def _():
            swap(i).wait_recv()
    for d in range(1, 4):
        cy(d, lax.rem(col + 4 - d, 4)).wait_recv()

    for d in range(1, 8):
        zcode(d).wait_send()
    @pl.when(sub < 2)
    def _():
        for d in (1, 2, 3):
            @pl.when(need)
            def _():
                remote(own_ref.at[0], lead_ref.at[line, col], zls.at[d - 1, 0], zlr.at[0], sub=sub + 2 * d).wait_send()
            @pl.when(need1)
            def _():
                remote(own_ref.at[1], lead_ref.at[line, 4 + col], zls.at[d - 1, 1], zlr.at[1], sub=sub + 2 * d).wait_send()
    for d in range(1, 4):
        cx(d, row).wait_send()
        cy(d, col).wait_send()
        @pl.when(par == 1)
        def _():
            ax(d, row).wait_send()
            ay(d, col).wait_send()
        @pl.when(col <= row)
        def _():
            by(d, col).wait_send()
        for c in range(4):
            @pl.when(c <= row)
            def _():
                bx(d, row, c).wait_send()
    for i in range(8):
        @pl.when(par == i // 4)
        def _():
            swap(i).wait_send()


def lead_gather(front, code):
    D = pltpu.SemaphoreType.DMA
    return pl.pallas_call(
        lead_kernel,
        out_shape=(jax.ShapeDtypeStruct((8, 8, 128, 128), F32), jax.ShapeDtypeStruct((4, 4, 8, 1, 128), jnp.int32)),
        in_specs=[pl.BlockSpec(memory_space=pltpu.HBM), pl.BlockSpec(memory_space=V)],
        out_specs=(pl.BlockSpec(memory_space=V), pl.BlockSpec(memory_space=V)),
        scratch_shapes=[V((2, 128, 128), F32), D((5,)), D((7,)), D((7,)), D((3, 2)), D((2,)), D((3,)), D((3,)), D((3,)), D((3,)),
                        D((2, 3)), D((2, 3)), D((3, 5)), D((3, 5)), D((4,)), D((4,))],
        compiler_params=pltpu.CompilerParams(vmem_limit_bytes=60 << 20, collective_id=1, has_side_effects=True),
        name="lead",
    )(front, code)


def landings(codes, me):
    codes = codes[:, :, :, 0, :].transpose(2, 1, 0, 3).reshape(128, 128)
    place = lax.broadcasted_iota(jnp.int32, (128, 128), 1) * 128 + codes % 128
    match = codes // 128 == me
    first = jnp.min(jnp.where(match, place, 1 << 20), 1)
    last = jnp.max(jnp.where(match, place, -1), 1)
    one = jnp.where(last >= 0, first % 128, -1)
    two = jnp.where(last > first, last % 128, -1)
    return jnp.stack([one, two], 1).reshape(256)


def local(front, child_tiles, tile_owner, tile_slot):
    sub = lax.axis_index("sub")
    row = lax.axis_index("row")
    col = lax.axis_index("col")
    group = sub * 4 + row
    owner = tile_owner[:, 0]
    outgoing = route(owner, child_tiles)
    lead, codes = lead_gather(front, (owner * 128 + tile_slot).reshape(1, 128))
    outgoing, lead = lax.optimization_barrier((outgoing, lead))
    arrived = lax.all_to_all(outgoing, ("sub", "row", "col"), split_axis=0, concat_axis=0, tiled=True)
    arrived = arrived.reshape(256, 128, 128)
    factor, hi, lo = chol(lead)
    landing = landings(codes, group * 4 + col)
    panel = head(landing, front, arrived)
    brow, bcol = panel_exchange(panel, hi, lo, factor)
    panel_out = lax.dynamic_index_in_dim(brow.reshape(4, 128, 2, 4, 128), col, 3, keepdims=True)
    panel_out = panel_out.reshape(4, 1, 128, 2, 1, 128)
    notes = jnp.concatenate([landing, jnp.where(group < 8, 0, 1).astype(jnp.int32).reshape(1)])
    return fin(notes, front, arrived, brow.reshape(512, 1024), bcol), panel_out


def solution(mesh):
    return jax.shard_map(
        local,
        mesh=mesh,
        in_specs=(
            P(None, ("sub", "row"), None, None, "col", None),
            P(("sub", "row", "col"), None, None),
            P(("sub", "row", "col"), None),
            P(("sub", "row", "col")),
        ),
        out_specs=(
            P(None, ("sub", "row"), None, None, "col", None),
            P(None, ("sub", "row"), None, None, "col", None),
        ),
        check_vma=False,
    )
```

```python
import jax
import jax.numpy as jnp
from jax import lax
from jax.experimental import pallas as pl
from jax.experimental.pallas import tpu as pltpu
from jax.sharding import PartitionSpec as P

F32, BF = jnp.float32, jnp.bfloat16
HI = lax.Precision.HIGHEST
V = pltpu.VMEM
ANY = pl.ANY
MESH = pl.DeviceIdType.MESH


def nt(a, b):
    return lax.dot_general(a, b, (((1,), (1,)), ((), ())), precision=HI, preferred_element_type=F32)


def nn(a, b):
    return lax.dot_general(a, b, (((1,), (0,)), ((), ())), precision=HI, preferred_element_type=F32)


def split3(x):
    h = x.astype(BF).astype(F32)
    r = x - h
    m = r.astype(BF).astype(F32)
    return h, m, r - m


def diag_factor(d_ref, u_ref, x_ref, cb_ref, r_ref):
    def body(b, carry):
        r0 = pl.multiple_of(b * 8, 8)
        block = d_ref[pl.ds(r0, 8), 0:128]
        rolled = pltpu.roll(block, (128 - r0) % 128, 1)
        for j in range(8):
            cb_ref[j] = jnp.broadcast_to(rolled[:, j:j + 1], (8, 128))
        r_ref[:, 0:128] = block
        r_ref[:, 128:256] = d_ref[pl.ds(r0, 8), 128:256]
        e = {}
        for i in range(8):
            for j in range(i + 1):
                e[i, j] = cb_ref[j, i:i + 1, :]
        rows = []
        for i in range(8):
            rows.append([r_ref[i:i + 1, 0:128], r_ref[i:i + 1, 128:256]])
        for j in range(8):
            inv = lax.rsqrt(e[j, j])
            low = {}
            for i in range(j + 1, 8):
                low[i] = e[i, j] * inv
            for h in range(2):
                rows[j][h] = rows[j][h] * inv
            for i in range(j + 1, 8):
                for m in range(j + 1, i + 1):
                    e[i, m] = e[i, m] - low[i] * low[m]
                for h in range(2):
                    rows[i][h] = rows[i][h] - low[i] * rows[j][h]
        for i in range(8):
            r_ref[i:i + 1, 0:128] = rows[i][0]
            r_ref[i:i + 1, 128:256] = rows[i][1]
        r = r_ref[...]
        u_ref[pl.ds(r0, 8), :] = r[:, 0:128]
        x_ref[pl.ds(r0, 8), :] = r[:, 128:256]
        h, m, l = split3(r)
        left = jnp.concatenate([h, h, m, h, l, m], 0)[:, 0:128].astype(BF)
        right = jnp.concatenate([h, m, h, l, h, m], 0).astype(BF)
        d_ref[...] = d_ref[...] - lax.dot_general(left, right, (((0,), (0,)), ((), ())), preferred_element_type=F32)
        return carry
    lax.fori_loop(0, 16, body, 0)


def chol_kernel(lead_ref, l_ref, hi_ref, lo_ref, s_ref, w_ref, d_ref, u_ref, x_ref, cb_ref, r_ref):
    row = lax.broadcasted_iota(jnp.int32, (128, 128), 0)
    col = lax.broadcasted_iota(jnp.int32, (128, 128), 1)
    eye = (row == col).astype(F32)
    n = 8
    for i in range(n):
        for j in range(i + 1):
            t = lead_ref[i, j]
            if i == j:
                t = jnp.where(row >= col, t, t.T)
            s_ref[i * 128:(i + 1) * 128, j * 128:(j + 1) * 128] = t
    w_ref[...] = jnp.zeros_like(w_ref)
    l_ref[...] = jnp.zeros_like(l_ref)
    for k in range(n):
        a, b = k * 128, (k + 1) * 128
        d_ref[:, 0:128] = s_ref[a:b, a:b]
        d_ref[:, 128:256] = eye
        diag_factor(d_ref, u_ref, x_ref, cb_ref, r_ref)
        x = x_ref[...]
        l_ref[a:b, a:b] = jnp.where(row >= col, u_ref[...].T, 0.0).astype(BF)
        if k > 0:
            w_ref[a:b, 0:a] = nn(x, w_ref[a:b, 0:a])
        w_ref[a:b, a:b] = x
        if k < n - 1:
            p = nt(s_ref[b:, a:b], x)
            s_ref[b:, a:b] = p
            l_ref[b:, a:b] = p.astype(BF)
            for j in range(k + 1, n):
                c, d = j * 128, (j + 1) * 128
                s_ref[c:, c:d] = s_ref[c:, c:d] - nt(s_ref[c:, a:b], s_ref[c:d, a:b])
            w_ref[b:, 0:b] = w_ref[b:, 0:b] - nn(p, w_ref[a:b, 0:b])
    for k in range(n):
        a, b = k * 128, (k + 1) * 128
        y = w_ref[a:b, :]
        h = y.astype(BF)
        hi_ref[a:b, :] = h
        lo_ref[a:b, :] = (y - h.astype(F32)).astype(BF)


def chol(lead):
    return pl.pallas_call(
        chol_kernel,
        out_shape=[jax.ShapeDtypeStruct((1024, 1024), BF)] * 3,
        in_specs=[pl.BlockSpec(memory_space=V)],
        out_specs=[pl.BlockSpec(memory_space=V)] * 3,
        scratch_shapes=[V((1024, 1024), F32), V((1024, 1024), F32), V((128, 256), F32), V((128, 128), F32),
                        V((128, 128), F32), V((8, 8, 128), F32), V((8, 256), F32)],
        compiler_params=pltpu.CompilerParams(vmem_limit_bytes=30 << 20),
        name="chol",
    )(lead)


def route_kernel(own_ref, child_ref, out_ref, idx_ref, cnt_ref):
    step = pl.program_id(0)

    @pl.when(step == 0)
    def _():
        def clear(k, c):
            cnt_ref[k] = 0
            for u in range(2):
                idx_ref[2 * k + u] = 0
            return c
        lax.fori_loop(0, 128, clear, 0)

        def place(k, c):
            o = own_ref[k]
            n = cnt_ref[o]
            idx_ref[2 * o + n] = k
            cnt_ref[o] = n + 1
            return c
        lax.fori_loop(0, 128, place, 0)

    def copy(j, c):
        for u in range(2):
            out_ref[j, u] = child_ref[idx_ref[step * 32 + 2 * j + u]]
        return c
    lax.fori_loop(0, 16, copy, 0)


def route(owner, child):
    return pl.pallas_call(
        route_kernel,
        out_shape=jax.ShapeDtypeStruct((128, 2, 128, 128), BF),
        grid_spec=pltpu.PrefetchScalarGridSpec(
            num_scalar_prefetch=1, grid=(8,),
            in_specs=[pl.BlockSpec((128, 128, 128), lambda g, a: (0, 0, 0), pipeline_mode=pl.Buffered(1))],
            out_specs=pl.BlockSpec((16, 2, 128, 128), lambda g, a: (g, 0, 0, 0)),
            scratch_shapes=[pltpu.SMEM((256,), jnp.int32), pltpu.SMEM((128,), jnp.int32)]),
        compiler_params=pltpu.CompilerParams(vmem_limit_bytes=60 << 20),
        name="route",
    )(owner, child)


def plan_kernel(land_ref, list_ref):
    def look(k, n):
        slot = land_ref[k]
        hit = (slot >= 0) & (lax.rem(lax.max(slot, 0), 32) < 2)
        @pl.when(hit)
        def _():
            list_ref[n + 1] = k
        return n + hit.astype(jnp.int32)
    list_ref[0] = lax.fori_loop(0, 256, look, 0)


def plan(land):
    return pl.pallas_call(
        plan_kernel,
        out_shape=jax.ShapeDtypeStruct((264,), jnp.int32),
        in_specs=[pl.BlockSpec(memory_space=pltpu.SMEM)],
        out_specs=pl.BlockSpec(memory_space=pltpu.SMEM),
        name="plan",
    )(land)


def head_kernel(land_ref, list_ref, front_ref, arr_ref, out_ref, buf_ref, acc_ref, fsem, asem):
    count = list_ref[0]
    def arrive(n, i):
        return pltpu.make_async_copy(arr_ref.at[list_ref[n + 1]], buf_ref.at[i], asem.at[i])
    def fetch(s):
        return pltpu.make_async_copy(front_ref.at[:, 0, :, s, 0, :], acc_ref.at[s], fsem.at[s])
    for s in range(2):
        fetch(s).start()
    def batch(b, carry):
        def begin(i, c):
            arrive(b * 16 + i, i).start()
            return c
        def end(i, c):
            n = b * 16 + i
            slot = land_ref[list_ref[n + 1]]
            s, q = slot % 32, slot // 32
            arrive(n, i).wait()
            acc_ref[s, q] = acc_ref[s, q] + buf_ref[i].astype(F32)
            return c
        here = lax.min(count - b * 16, 16)
        lax.fori_loop(0, here, begin, 0)
        @pl.when(b == 0)
        def _():
            for s in range(2):
                fetch(s).wait()
        lax.fori_loop(0, here, end, 0)
        return carry
    lax.fori_loop(0, lax.max((count + 15) // 16, 1), batch, 0)
    out_ref[...] = acc_ref[...]


def head(land, listed, front, arrived):
    return pl.pallas_call(
        head_kernel,
        out_shape=jax.ShapeDtypeStruct((2, 4, 128, 128), F32),
        grid_spec=pltpu.PrefetchScalarGridSpec(
            num_scalar_prefetch=2, grid=(1,),
            in_specs=[pl.BlockSpec(memory_space=ANY)] * 2,
            out_specs=pl.BlockSpec((2, 4, 128, 128), lambda g, a, b: (0, 0, 0, 0)),
            scratch_shapes=[V((16, 128, 128), BF), V((2, 4, 128, 128), F32),
                            pltpu.SemaphoreType.DMA((2,)), pltpu.SemaphoreType.DMA((16,))]),
        compiler_params=pltpu.CompilerParams(vmem_limit_bytes=60 << 20),
        name="head",
    )(land, listed, front, arrived)


def fin_kernel(land_ref, front_ref, arr_ref, brow_ref, bcol_ref, out_ref, pout_ref, buf_ref, acc_ref, bc_ref, fsem, asem, bsem, osem):
    def arrive(c):
        return pltpu.make_async_copy(arr_ref.at[pl.ds(c * 32, 32)], buf_ref.at[c], asem.at[c])
    def fetch(s):
        return pltpu.make_async_copy(front_ref.at[:, 0, :, s, 0, :], acc_ref.at[s], fsem.at[s])
    def column(s):
        return pltpu.make_async_copy(bcol_ref.at[s % 8, s // 8], bc_ref.at[pl.ds(s * 128, 128)], bsem.at[s])
    def put(s):
        return pltpu.make_async_copy(acc_ref.at[s], out_ref.at[:, 0, :, s, 0, :], osem.at[s])
    def each(low, high, f):
        def go(s, c):
            f(s)
            return c
        lax.fori_loop(low, high, go, 0)
    each(0, 32, lambda s: fetch(s).start())
    for c in range(8):
        arrive(c).start()
    each(2, 32, lambda s: column(s).start())
    for q in range(4):
        pair = [brow_ref[q * 128:(q + 1) * 128, pl.ds(pl.multiple_of((4 * s + land_ref[257]) * 128, 128), 128)] for s in range(2)]
        pout_ref[q] = jnp.stack([x.astype(F32) for x in pair], 1).astype(BF)
    each(0, 32, lambda s: fetch(s).wait())
    for c in range(8):
        arrive(c).wait()
        def add(k, carry):
            slot = land_ref[c * 32 + k]
            @pl.when(slot >= 0)
            def _():
                s, q = slot % 32, slot // 32
                acc_ref[s, q] = acc_ref[s, q] + buf_ref[c, k].astype(F32)
            return carry
        lax.fori_loop(0, 32, add, 0)
    for s in range(2):
        put(s).start()
    def update(g, carry):
        s = 2 * g
        column(s).wait()
        column(s + 1).wait()
        y = lax.dot_general(brow_ref[...], bc_ref[pl.ds(pl.multiple_of(g * 256, 256), 256), :],
                            (((1,), (1,)), ((), ())), preferred_element_type=F32)
        for u in range(2):
            z = y[:, u * 128:(u + 1) * 128].reshape(4, 128, 128)
            acc_ref[s + u, 0] = acc_ref[s + u, 0] - jnp.where(land_ref[256] > 0, z[0], 0.0)
            acc_ref[s + u, 1:4] = acc_ref[s + u, 1:4] - z[1:4]
            put(s + u).start()
        return carry
    lax.fori_loop(1, 16, update, 0)
    each(0, 32, lambda s: put(s).wait())


def fin(land, front, arrived, brow, bcol):
    D = pltpu.SemaphoreType.DMA
    return pl.pallas_call(
        fin_kernel,
        out_shape=(jax.ShapeDtypeStruct((4, 1, 128, 32, 1, 128), F32), jax.ShapeDtypeStruct((4, 128, 2, 128), BF)),
        grid_spec=pltpu.PrefetchScalarGridSpec(
            num_scalar_prefetch=1, grid=(1,),
            in_specs=[pl.BlockSpec(memory_space=ANY)] * 2
            + [pl.BlockSpec((512, 1024), lambda g, a: (0, 0), pipeline_mode=pl.Buffered(1)), pl.BlockSpec(memory_space=ANY)],
            out_specs=(pl.BlockSpec(memory_space=ANY), pl.BlockSpec((4, 128, 2, 128), lambda g, a: (0, 0, 0, 0))),
            scratch_shapes=[V((8, 32, 128, 128), BF), V((32, 4, 128, 128), F32), V((4096, 1024), BF),
                            D((32,)), D((8,)), D((32,)), D((32,))]),
        compiler_params=pltpu.CompilerParams(vmem_limit_bytes=60 << 20),
        name="fin",
    )(land, front, arrived, brow, bcol)


def panel_kernel(panel_ref, hi_hbm, lo_hbm, low_hbm, brow_ref, bcol_ref, arow, ah, al, hi, lo, low, xb, rl,
                 lsem, ps, pr, xs, xr, ws, wr, ys, yr, rs, rr, zs, zr, fs, fr, ms, mr):
    sub, row, col = lax.axis_index("sub"), lax.axis_index("row"), lax.axis_index("col")
    group = 4 * sub + row
    mate = sub + 1 - 2 * lax.rem(sub, 2)

    def n4(x, d):
        return lax.rem(x + 4 + d, 4)

    def n8(x, d):
        return lax.rem(x + 8 + d, 8)

    def remote(src, dst, send, recv, **where):
        return pltpu.make_async_remote_copy(src, dst, send, recv, device_id=where, device_id_type=MESH)

    loads = [pltpu.make_async_copy(hi_hbm, hi, lsem.at[0]), pltpu.make_async_copy(lo_hbm, lo, lsem.at[1]),
             pltpu.make_async_copy(low_hbm.at[pl.ds(pl.multiple_of(lax.min(group, 7) * 128, 128), 128)], low, lsem.at[2]),
             pltpu.make_async_copy(panel_ref.at[:, col], arow.at[col], lsem.at[3])]
    barrier = pltpu.get_barrier_semaphore()
    for d in (1, 3):
        pl.semaphore_signal(barrier, inc=1, device_id={"row": n4(row, d)}, device_id_type=MESH)
        pl.semaphore_signal(barrier, inc=1, device_id={"sub": n8(sub, 2 * d if d == 1 else -2)}, device_id_type=MESH)
    for d in (1, 2, 3):
        pl.semaphore_signal(barrier, inc=1, device_id={"col": n4(col, d)}, device_id_type=MESH)
    pl.semaphore_signal(barrier, inc=1, device_id={"sub": mate}, device_id_type=MESH)
    for copy in loads:
        copy.start()
    pl.semaphore_wait(barrier, 8)

    def take(d):
        return remote(panel_ref.at[:, n4(col, d)], arow.at[col], ps.at[d - 1], pr.at[d - 1], col=n4(col, d))
    def taken(d):
        return remote(panel_ref.at[:, n4(col, d)], arow.at[n4(col, -d)], ps.at[d - 1], pr.at[d - 1], col=n4(col, d))
    for d in (1, 3, 2):
        take(d).start()
    loads[3].wait()
    for d in (1, 3, 2):
        taken(d).wait_recv()
    for s in range(2):
        for t in range(4):
            a = arow[t, s]
            h = a.astype(BF)
            at = (4 * s + t) * 128
            ah[:, at:at + 128] = h
            al[:, at:at + 128] = (a - h.astype(F32)).astype(BF)
    for copy in loads[:3]:
        copy.wait()
    top = (group < 8) & (col == 0)

    def mm(x, y):
        return lax.dot_general(x, y, (((1,), (1,)), ((), ())), preferred_element_type=F32)
    for b in range(4):
        w = 256 * (b + 1)
        rows = pl.ds(256 * b, 256)
        y = mm(ah[:, 0:w], hi[rows, 0:w]) + (mm(ah[:, 0:w], lo[rows, 0:w]) + mm(al[:, 0:w], hi[rows, 0:w]))
        y = jnp.where(top, low[:, 256 * b:w], y.astype(BF))
        xb[row, :, 256 * b:w] = y
        brow_ref[col, :, 256 * b:w] = y

    half = [pl.ds(0, 64), pl.ds(64, 64)]
    step = [1, -1]
    def xsend(i):
        return remote(xb.at[row], xb.at[row], xs.at[i], xr.at[i], row=n4(row, step[i]))
    def xrecv(i):
        at = xb.at[n4(row, -step[i])]
        return remote(at, at, xs.at[i], xr.at[i], row=n4(row, step[i]))
    def xforward(i, r):
        at = xb.at[r, half[i]]
        return remote(at, at, xs.at[2 + i], xr.at[2 + i], row=n4(row, step[i]))
    def wsend(i):
        return remote(brow_ref.at[col], brow_ref.at[col], ws.at[i], wr.at[i], col=n4(col, step[i]))
    def wrecv(i):
        at = brow_ref.at[n4(col, -step[i])]
        return remote(at, at, ws.at[i], wr.at[i], col=n4(col, step[i]))
    def wforward(i, c):
        at = brow_ref.at[c, half[i]]
        return remote(at, at, ws.at[2 + i], wr.at[2 + i], col=n4(col, step[i]))

    def ynear(i):
        return remote(xb.at[n4(col, step[i])], bcol_ref.at[sub, col], ys.at[i], yr.at[i], col=n4(col, step[i]))
    def ynear_in(i):
        return remote(xb.at[0], bcol_ref.at[sub, n4(col, -step[i])], ys.at[i], yr.at[i], col=n4(col, step[i]))
    def yfar(i):
        return remote(xb.at[n4(col, 2), half[i]], rl.at[i], rs.at[i], rr.at[i], col=n4(col, step[i]))
    def yrelay(i):
        return remote(rl.at[i], bcol_ref.at[sub, n4(col, -step[i]), half[i]], ys.at[2 + i], yr.at[2 + i], col=n4(col, step[i]))
    def yfar_in(i):
        return remote(rl.at[i], bcol_ref.at[sub, n4(col, 2), half[i]], ys.at[2 + i], yr.at[2 + i], col=n4(col, step[i]))
    home = pltpu.make_async_copy(xb.at[col], bcol_ref.at[sub, col], lsem.at[4])

    def ysend(c):
        d = n4(c, -col)
        @pl.when(d == 0)
        def _():
            home.start()
        for i in range(2):
            @pl.when(d == (1, 3)[i])
            def _():
                ynear(i).start()
        @pl.when(d == 2)
        def _():
            yfar(0).start()
            yfar(1).start()

    def own(e, i):
        at = bcol_ref.at[sub, n4(col, e)]
        return remote(at if e else xb.at[col], at, zs.at[i, e], zr.at[i, e], sub=n8(sub, 2 * step[i]))
    def arrive(e, i):
        at = bcol_ref.at[n8(sub, -2 * step[i]), n4(col, e)]
        return remote(at, at, zs.at[i, e], zr.at[i, e], sub=n8(sub, 2 * step[i]))
    side = [0, 0, 1, 1]
    def onward(e, z):
        at = bcol_ref.at[n8(sub, z), n4(col, e)]
        return remote(at, at, fs.at[e], fr.at[e], sub=n8(sub, 2 * step[side[e]]))
    def swap(e, k, z):
        at = bcol_ref.at[n8(sub, z), n4(col, e)]
        return remote(at if e or k else xb.at[col], at, ms.at[k, e], mr.at[k, e], sub=mate)
    def swapped(e, k, z):
        at = bcol_ref.at[n8(mate, z), n4(col, e)]
        return remote(at, at, ms.at[k, e], mr.at[k, e], sub=mate)

    def launch(e):
        own(e, 0).start()
        own(e, 1).start()
        swap(e, 0, 0).start()
    apart = n4(col, -row)

    def near():
        ynear_in(1).wait_recv()
        launch(1)
        ynear_in(0).wait_recv()
        launch(3)

    def reach(d):
        ysend(n4(row, d))
        @pl.when(apart == d)
        def _():
            launch(0)

    for i in range(2):
        xsend(i).start()
    for i in range(2):
        wsend(i).start()
    reach(0)
    for i in range(2):
        xrecv(i).wait_recv()
        xforward(i, n4(row, -step[i])).start()
        reach(3 if i == 0 else 1)
    for i in range(2):
        wrecv(i).wait_recv()
        wforward(i, n4(col, -step[i])).start()
    @pl.when(apart == 0)
    def _():
        near()
    for i in range(2):
        xforward(i, n4(row, 2)).wait_recv()
    reach(2)
    for i in range(2):
        yfar(i).wait_recv()
        yrelay(i).start()
    @pl.when(apart != 0)
    def _():
        near()
    yfar_in(0).wait_recv()
    yfar_in(1).wait_recv()
    launch(2)
    for e in (0, 1, 3, 2):
        for i in range(2):
            arrive(e, i).wait_recv()
            if side[e] == i:
                onward(e, -2 * step[i]).start()
            swap(e, 1 + i, -2 * step[i]).start()
    for e in (0, 1, 3, 2):
        onward(e, 4).wait_recv()
        swap(e, 3, 4).start()
    for e in range(4):
        swapped(e, 0, 0).wait_recv()
        swapped(e, 1, -2).wait_recv()
        swapped(e, 2, 2).wait_recv()
        swapped(e, 3, 4).wait_recv()
    for i in range(2):
        wforward(i, n4(col, 2)).wait_recv()

    home.wait()

    for d in (1, 2, 3):
        take(d).wait_send()
    for i in range(2):
        xsend(i).wait_send()
        wsend(i).wait_send()
        xforward(i, n4(row, -step[i])).wait_send()
        wforward(i, n4(col, -step[i])).wait_send()
        ynear(i).wait_send()
        yfar(i).wait_send()
        yrelay(i).wait_send()
    for e in range(4):
        own(e, 0).wait_send()
        own(e, 1).wait_send()
        onward(e, -2 * step[side[e]]).wait_send()
        swap(e, 0, 0).wait_send()
        swap(e, 1, -2).wait_send()
        swap(e, 2, 2).wait_send()
        swap(e, 3, 4).wait_send()


def panel_exchange(panel, hi, lo, low):
    D = pltpu.SemaphoreType.DMA
    H = pltpu.HBM
    return pl.pallas_call(
        panel_kernel,
        out_shape=(jax.ShapeDtypeStruct((4, 128, 1024), BF), jax.ShapeDtypeStruct((8, 4, 128, 1024), BF)),
        in_specs=[pl.BlockSpec(memory_space=V)] + [pl.BlockSpec(memory_space=H)] * 3,
        out_specs=(pl.BlockSpec(memory_space=V), pl.BlockSpec(memory_space=H)),
        scratch_shapes=[V((4, 2, 128, 128), F32), V((128, 1024), BF), V((128, 1024), BF), V((1024, 1024), BF), V((1024, 1024), BF),
                        V((128, 1024), BF), V((4, 128, 1024), BF), V((2, 64, 1024), BF),
                        D((5,)), D((3,)), D((3,)), D((4,)), D((4,)), D((4,)), D((4,)), D((4,)), D((4,)), D((2,)), D((2,)),
                        D((2, 4)), D((2, 4)), D((4,)), D((4,)), D((4, 4)), D((4, 4))],
        compiler_params=pltpu.CompilerParams(vmem_limit_bytes=60 << 20, collective_id=2, has_side_effects=True),
        name="panel",
    )(panel, hi, lo, low)


def lead_kernel(front_ref, code_ref, lead_ref, codes_ref, own_ref, lsem, zs, zr, zls, zlr, xs, xr, ys, yr, as_, ar, bs, br, cs, cr):
    sub, row, col = lax.axis_index("sub"), lax.axis_index("row"), lax.axis_index("col")
    par = lax.rem(sub, 2)
    mate = sub + 1 - 2 * par
    line = 4 * par + row
    need = (par == 1) | (col <= row)

    def remote(src, dst, send, recv, **where):
        return pltpu.make_async_remote_copy(src, dst, send, recv, device_id=where, device_id_type=MESH)

    barrier = pltpu.get_barrier_semaphore()
    for d in range(1, 8):
        pl.semaphore_signal(barrier, inc=1, device_id={"sub": lax.rem(sub + d, 8)}, device_id_type=MESH)
    for d in range(1, 4):
        pl.semaphore_signal(barrier, inc=1, device_id={"row": lax.rem(row + d, 4)}, device_id_type=MESH)
        pl.semaphore_signal(barrier, inc=1, device_id={"col": lax.rem(col + d, 4)}, device_id_type=MESH)

    mine = [pltpu.make_async_copy(front_ref.at[0, 0, :, s, 0, :], own_ref.at[s], lsem.at[s]) for s in range(2)]
    code = pltpu.make_async_copy(code_ref, codes_ref.at[col, row, sub], lsem.at[2])
    code.start()
    mine[0].start()
    mine[1].start()
    mine[0].wait()
    mine[1].wait()
    keep = [pltpu.make_async_copy(own_ref.at[s], lead_ref.at[line, 4 * s + col], lsem.at[3 + s]) for s in range(2)]

    @pl.when(sub < 2)
    def _():
        keep[0].start()
        keep[1].start()
    pl.semaphore_wait(barrier, 13)

    def zcode(d):
        return remote(code_ref, codes_ref.at[col, row, sub], zs.at[d - 1], zr.at[d - 1], sub=lax.rem(sub + d, 8))
    def zcode_in(d):
        return remote(code_ref, codes_ref.at[col, row, lax.rem(sub + 8 - d, 8)], zs.at[d - 1], zr.at[d - 1], sub=lax.rem(sub + d, 8))
    need1 = (par == 1) & (col <= row)

    @pl.when(sub < 2)
    def _():
        for d in (1, 3, 2):
            @pl.when(need)
            def _():
                remote(own_ref.at[0], lead_ref.at[line, col], zls.at[d - 1, 0], zlr.at[0], sub=sub + 2 * d).start()
            @pl.when(need1)
            def _():
                remote(own_ref.at[1], lead_ref.at[line, 4 + col], zls.at[d - 1, 1], zlr.at[1], sub=sub + 2 * d).start()
    for d in range(1, 8):
        zcode(d).start()

    @pl.when(sub < 2)
    def _():
        keep[0].wait()
        keep[1].wait()

    @pl.when(sub >= 2)
    def _():
        @pl.when(need)
        def _():
            remote(own_ref.at[0], lead_ref.at[line, col], zls.at[0, 0], zlr.at[0], sub=par).wait_recv()
        @pl.when(need1)
        def _():
            remote(own_ref.at[1], lead_ref.at[line, 4 + col], zls.at[0, 1], zlr.at[1], sub=par).wait_recv()

    def ax(d, r):
        return remote(lead_ref.at[4 + r, col], lead_ref.at[4 + r, col], as_.at[0, d - 1], ar.at[0, d - 1], row=lax.rem(row + d, 4))
    def ay(d, c):
        return remote(lead_ref.at[pl.ds(4, 4), c], lead_ref.at[pl.ds(4, 4), c], as_.at[1, d - 1], ar.at[1, d - 1], col=lax.rem(col + d, 4))
    def by(d, c):
        at = lead_ref.at[line, 4 * par + c]
        return remote(at, at, bs.at[d - 1, 4], br.at[d - 1, 4], col=lax.rem(col + d, 4))
    def bx(d, r, c):
        at = lead_ref.at[4 * par + r, 4 * par + c]
        return remote(at, at, bs.at[d - 1, c], br.at[d - 1, c], row=lax.rem(row + d, 4))
    for d in (1, 3, 2):
        @pl.when(par == 1)
        def _():
            ax(d, row).start()
        @pl.when(col <= row)
        def _():
            by(d, col).start()
    code.wait()
    for d in range(1, 8):
        zcode_in(d).wait_recv()
    def cx(d, r):
        return remote(codes_ref.at[col, r], codes_ref.at[col, r], xs.at[d - 1], xr.at[d - 1], row=lax.rem(row + d, 4))
    def cy(d, c):
        return remote(codes_ref.at[c], codes_ref.at[c], ys.at[d - 1], yr.at[d - 1], col=lax.rem(col + d, 4))
    for d in range(1, 4):
        cx(d, row).start()
    for d in range(1, 4):
        @pl.when(par == 1)
        def _():
            ax(d, lax.rem(row + 4 - d, 4)).wait_recv()
        @pl.when(lax.rem(col + 4 - d, 4) <= row)
        def _():
            by(d, lax.rem(col + 4 - d, 4)).wait_recv()
    for d in (1, 3, 2):
        @pl.when(par == 1)
        def _():
            ay(d, col).start()
        for c in range(4):
            @pl.when(c <= row)
            def _():
                bx(d, row, c).start()
    for d in range(1, 4):
        cx(d, lax.rem(row + 4 - d, 4)).wait_recv()
    for d in range(1, 4):
        cy(d, col).start()
    for d in range(1, 4):
        @pl.when(par == 1)
        def _():
            ay(d, lax.rem(col + 4 - d, 4)).wait_recv()
        for c in range(4):
            r = lax.rem(row + 4 - d, 4)
            @pl.when(c <= r)
            def _():
                bx(d, r, c).wait_recv()

    def swap(i):
        at = lead_ref.at[i, pl.ds(0, i + 1)]
        return remote(at, at, cs.at[i % 4], cr.at[i % 4], sub=mate)
    for i in range(8):
        @pl.when(par == i // 4)
        def _():
            swap(i).start()
    for i in range(8):
        @pl.when(par != i // 4)
        def _():
            swap(i).wait_recv()
    for d in range(1, 4):
        cy(d, lax.rem(col + 4 - d, 4)).wait_recv()

    for d in range(1, 8):
        zcode(d).wait_send()
    @pl.when(sub < 2)
    def _():
        for d in (1, 2, 3):
            @pl.when(need)
            def _():
                remote(own_ref.at[0], lead_ref.at[line, col], zls.at[d - 1, 0], zlr.at[0], sub=sub + 2 * d).wait_send()
            @pl.when(need1)
            def _():
                remote(own_ref.at[1], lead_ref.at[line, 4 + col], zls.at[d - 1, 1], zlr.at[1], sub=sub + 2 * d).wait_send()
    for d in range(1, 4):
        cx(d, row).wait_send()
        cy(d, col).wait_send()
        @pl.when(par == 1)
        def _():
            ax(d, row).wait_send()
            ay(d, col).wait_send()
        @pl.when(col <= row)
        def _():
            by(d, col).wait_send()
        for c in range(4):
            @pl.when(c <= row)
            def _():
                bx(d, row, c).wait_send()
    for i in range(8):
        @pl.when(par == i // 4)
        def _():
            swap(i).wait_send()


def lead_gather(front, code):
    D = pltpu.SemaphoreType.DMA
    return pl.pallas_call(
        lead_kernel,
        out_shape=(jax.ShapeDtypeStruct((8, 8, 128, 128), F32), jax.ShapeDtypeStruct((4, 4, 8, 1, 128), jnp.int32)),
        in_specs=[pl.BlockSpec(memory_space=pltpu.HBM), pl.BlockSpec(memory_space=V)],
        out_specs=(pl.BlockSpec(memory_space=V), pl.BlockSpec(memory_space=V)),
        scratch_shapes=[V((2, 128, 128), F32), D((5,)), D((7,)), D((7,)), D((3, 2)), D((2,)), D((3,)), D((3,)), D((3,)), D((3,)),
                        D((2, 3)), D((2, 3)), D((3, 5)), D((3, 5)), D((4,)), D((4,))],
        compiler_params=pltpu.CompilerParams(vmem_limit_bytes=60 << 20, collective_id=1, has_side_effects=True),
        name="lead",
    )(front, code)


def landings(codes, me):
    codes = codes[:, :, :, 0, :].transpose(2, 1, 0, 3).reshape(128, 128)
    place = lax.broadcasted_iota(jnp.int32, (128, 128), 1) * 128 + codes % 128
    match = codes // 128 == me
    first = jnp.min(jnp.where(match, place, 1 << 20), 1)
    last = jnp.max(jnp.where(match, place, -1), 1)
    one = jnp.where(last >= 0, first % 128, -1)
    two = jnp.where(last > first, last % 128, -1)
    return jnp.stack([one, two], 1).reshape(256)


def local(front, child_tiles, tile_owner, tile_slot):
    sub = lax.axis_index("sub")
    row = lax.axis_index("row")
    col = lax.axis_index("col")
    group = sub * 4 + row
    owner = tile_owner[:, 0]
    outgoing = route(owner, child_tiles)
    lead, codes = lead_gather(front, (owner * 128 + tile_slot).reshape(1, 128))
    outgoing, lead = lax.optimization_barrier((outgoing, lead))
    arrived = lax.all_to_all(outgoing, ("sub", "row", "col"), split_axis=0, concat_axis=0, tiled=True)
    arrived = arrived.reshape(256, 128, 128)
    factor, hi, lo = chol(lead)
    landing = landings(codes, group * 4 + col)
    listed = plan(landing)
    panel = head(landing, listed, front, arrived)
    brow, bcol = panel_exchange(panel, hi, lo, factor)
    extra = jnp.stack([jnp.where(group < 8, 0, 1), col]).astype(jnp.int32)
    out, panel_out = fin(jnp.concatenate([landing, extra]), front, arrived, brow.reshape(512, 1024), bcol)
    return out, panel_out.reshape(4, 1, 128, 2, 1, 128)


def solution(mesh):
    return jax.shard_map(
        local,
        mesh=mesh,
        in_specs=(
            P(None, ("sub", "row"), None, None, "col", None),
            P(("sub", "row", "col"), None, None),
            P(("sub", "row", "col"), None),
            P(("sub", "row", "col")),
        ),
        out_specs=(
            P(None, ("sub", "row"), None, None, "col", None),
            P(None, ("sub", "row"), None, None, "col", None),
        ),
        check_vma=False,
    )
```

```python
import jax
import jax.numpy as jnp
from jax import lax
from jax.experimental import pallas as pl
from jax.experimental.pallas import tpu as pltpu
from jax.sharding import PartitionSpec as P

F32, BF = jnp.float32, jnp.bfloat16
HI = lax.Precision.HIGHEST
V = pltpu.VMEM
ANY = pl.ANY
MESH = pl.DeviceIdType.MESH


def nt(a, b):
    return lax.dot_general(a, b, (((1,), (1,)), ((), ())), precision=HI, preferred_element_type=F32)


def nn(a, b):
    return lax.dot_general(a, b, (((1,), (0,)), ((), ())), precision=HI, preferred_element_type=F32)


def split3(x):
    h = x.astype(BF).astype(F32)
    r = x - h
    m = r.astype(BF).astype(F32)
    return h, m, r - m


def diag_factor(d_ref, u_ref, x_ref, cb_ref, r_ref):
    def body(b, carry):
        r0 = pl.multiple_of(b * 8, 8)
        block = d_ref[pl.ds(r0, 8), 0:128]
        rolled = pltpu.roll(block, (128 - r0) % 128, 1)
        for j in range(8):
            cb_ref[j] = jnp.broadcast_to(rolled[:, j:j + 1], (8, 128))
        r_ref[:, 0:128] = block
        r_ref[:, 128:256] = d_ref[pl.ds(r0, 8), 128:256]
        e = {}
        for i in range(8):
            for j in range(i + 1):
                e[i, j] = cb_ref[j, i:i + 1, :]
        rows = []
        for i in range(8):
            rows.append([r_ref[i:i + 1, 0:128], r_ref[i:i + 1, 128:256]])
        for j in range(8):
            inv = lax.rsqrt(e[j, j])
            low = {}
            for i in range(j + 1, 8):
                low[i] = e[i, j] * inv
            for h in range(2):
                rows[j][h] = rows[j][h] * inv
            for i in range(j + 1, 8):
                for m in range(j + 1, i + 1):
                    e[i, m] = e[i, m] - low[i] * low[m]
                for h in range(2):
                    rows[i][h] = rows[i][h] - low[i] * rows[j][h]
        for i in range(8):
            r_ref[i:i + 1, 0:128] = rows[i][0]
            r_ref[i:i + 1, 128:256] = rows[i][1]
        r = r_ref[...]
        u_ref[pl.ds(r0, 8), :] = r[:, 0:128]
        x_ref[pl.ds(r0, 8), :] = r[:, 128:256]
        h, m, l = split3(r)
        left = jnp.concatenate([h, h, m, h, l, m], 0)[:, 0:128].astype(BF)
        right = jnp.concatenate([h, m, h, l, h, m], 0).astype(BF)
        d_ref[...] = d_ref[...] - lax.dot_general(left, right, (((0,), (0,)), ((), ())), preferred_element_type=F32)
        return carry
    lax.fori_loop(0, 16, body, 0)


def chol_kernel(lead_ref, l_ref, hi_ref, lo_ref, s_ref, w_ref, d_ref, u_ref, x_ref, cb_ref, r_ref):
    row = lax.broadcasted_iota(jnp.int32, (128, 128), 0)
    col = lax.broadcasted_iota(jnp.int32, (128, 128), 1)
    eye = (row == col).astype(F32)
    n = 8
    for i in range(n):
        for j in range(i + 1):
            t = lead_ref[i, j]
            if i == j:
                t = jnp.where(row >= col, t, t.T)
            s_ref[i * 128:(i + 1) * 128, j * 128:(j + 1) * 128] = t
    w_ref[...] = jnp.zeros_like(w_ref)
    l_ref[...] = jnp.zeros_like(l_ref)
    for k in range(n):
        a, b = k * 128, (k + 1) * 128
        d_ref[:, 0:128] = s_ref[a:b, a:b]
        d_ref[:, 128:256] = eye
        diag_factor(d_ref, u_ref, x_ref, cb_ref, r_ref)
        x = x_ref[...]
        l_ref[a:b, a:b] = jnp.where(row >= col, u_ref[...].T, 0.0).astype(BF)
        if k > 0:
            w_ref[a:b, 0:a] = nn(x, w_ref[a:b, 0:a])
        w_ref[a:b, a:b] = x
        if k < n - 1:
            p = nt(s_ref[b:, a:b], x)
            s_ref[b:, a:b] = p
            l_ref[b:, a:b] = p.astype(BF)
            for j in range(k + 1, n):
                c, d = j * 128, (j + 1) * 128
                s_ref[c:, c:d] = s_ref[c:, c:d] - nt(s_ref[c:, a:b], s_ref[c:d, a:b])
            w_ref[b:, 0:b] = w_ref[b:, 0:b] - nn(p, w_ref[a:b, 0:b])
    for k in range(n):
        a, b = k * 128, (k + 1) * 128
        y = w_ref[a:b, :]
        h = y.astype(BF)
        hi_ref[a:b, :] = h
        lo_ref[a:b, :] = (y - h.astype(F32)).astype(BF)


def chol(lead):
    return pl.pallas_call(
        chol_kernel,
        out_shape=[jax.ShapeDtypeStruct((1024, 1024), BF)] * 3,
        in_specs=[pl.BlockSpec(memory_space=V)],
        out_specs=[pl.BlockSpec(memory_space=V)] * 3,
        scratch_shapes=[V((1024, 1024), F32), V((1024, 1024), F32), V((128, 256), F32), V((128, 128), F32),
                        V((128, 128), F32), V((8, 8, 128), F32), V((8, 256), F32)],
        compiler_params=pltpu.CompilerParams(vmem_limit_bytes=30 << 20),
        name="chol",
    )(lead)


def route_kernel(own_ref, child_ref, out_ref, idx_ref, cnt_ref):
    step = pl.program_id(0)

    @pl.when(step == 0)
    def _():
        def clear(k, c):
            cnt_ref[k] = 0
            for u in range(2):
                idx_ref[2 * k + u] = 0
            return c
        lax.fori_loop(0, 128, clear, 0)

        def place(k, c):
            o = own_ref[k]
            n = cnt_ref[o]
            idx_ref[2 * o + n] = k
            cnt_ref[o] = n + 1
            return c
        lax.fori_loop(0, 128, place, 0)

    def copy(j, c):
        for u in range(2):
            out_ref[j, u] = child_ref[idx_ref[step * 32 + 2 * j + u]]
        return c
    lax.fori_loop(0, 16, copy, 0)


def route(owner, child):
    return pl.pallas_call(
        route_kernel,
        out_shape=jax.ShapeDtypeStruct((128, 2, 128, 128), BF),
        grid_spec=pltpu.PrefetchScalarGridSpec(
            num_scalar_prefetch=1, grid=(8,),
            in_specs=[pl.BlockSpec((128, 128, 128), lambda g, a: (0, 0, 0), pipeline_mode=pl.Buffered(1))],
            out_specs=pl.BlockSpec((16, 2, 128, 128), lambda g, a: (g, 0, 0, 0)),
            scratch_shapes=[pltpu.SMEM((256,), jnp.int32), pltpu.SMEM((128,), jnp.int32)]),
        compiler_params=pltpu.CompilerParams(vmem_limit_bytes=60 << 20),
        name="route",
    )(owner, child)


def plan_kernel(land_ref, list_ref, order_ref, cnt_ref, pos_ref):
    def clear(k, c):
        cnt_ref[k] = 0
        for u in range(4):
            order_ref[4 * k + u] = 0
        return c
    lax.fori_loop(0, 128, clear, 0)

    def look(k, n):
        slot = land_ref[k]
        @pl.when(slot >= 0)
        def _():
            cnt_ref[slot] = cnt_ref[slot] + 1
        hit = (slot >= 0) & (lax.rem(lax.max(slot, 0), 32) < 2)
        @pl.when(hit)
        def _():
            list_ref[n + 1] = k
        return n + hit.astype(jnp.int32)
    list_ref[0] = lax.fori_loop(0, 256, look, 0)

    def bounds(j, n):
        here = cnt_ref[j]
        pos_ref[j] = n
        order_ref[512 + j] = lax.max(n + here - 1, 0)
        order_ref[640 + j] = lax.min(here, 1)
        cnt_ref[j] = 0
        return n + here
    lax.fori_loop(0, 128, bounds, 0)

    def place(k, c):
        slot = land_ref[k]
        @pl.when(slot >= 0)
        def _():
            p = pos_ref[slot]
            order_ref[p] = k
            order_ref[256 + p] = cnt_ref[slot]
            cnt_ref[slot] = 1
            pos_ref[slot] = p + 1
        return c
    lax.fori_loop(0, 256, place, 0)


def plan(land):
    return pl.pallas_call(
        plan_kernel,
        out_shape=(jax.ShapeDtypeStruct((264,), jnp.int32), jax.ShapeDtypeStruct((768,), jnp.int32)),
        in_specs=[pl.BlockSpec(memory_space=pltpu.SMEM)],
        out_specs=(pl.BlockSpec(memory_space=pltpu.SMEM),) * 2,
        scratch_shapes=[pltpu.SMEM((128,), jnp.int32)] * 2,
        name="plan",
    )(land)


def head_kernel(land_ref, list_ref, front_ref, arr_ref, out_ref, buf_ref, acc_ref, fsem, asem):
    count = list_ref[0]
    def arrive(n, i):
        return pltpu.make_async_copy(arr_ref.at[list_ref[n + 1]], buf_ref.at[i], asem.at[i])
    def fetch(s):
        return pltpu.make_async_copy(front_ref.at[:, 0, :, s, 0, :], acc_ref.at[s], fsem.at[s])
    for s in range(2):
        fetch(s).start()
    def batch(b, carry):
        def begin(i, c):
            arrive(b * 16 + i, i).start()
            return c
        def end(i, c):
            n = b * 16 + i
            slot = land_ref[list_ref[n + 1]]
            s, q = slot % 32, slot // 32
            arrive(n, i).wait()
            acc_ref[s, q] = acc_ref[s, q] + buf_ref[i].astype(F32)
            return c
        here = lax.min(count - b * 16, 16)
        lax.fori_loop(0, here, begin, 0)
        @pl.when(b == 0)
        def _():
            for s in range(2):
                fetch(s).wait()
        lax.fori_loop(0, here, end, 0)
        return carry
    lax.fori_loop(0, lax.max((count + 15) // 16, 1), batch, 0)
    out_ref[...] = acc_ref[...]


def head(land, listed, front, arrived):
    return pl.pallas_call(
        head_kernel,
        out_shape=jax.ShapeDtypeStruct((2, 4, 128, 128), F32),
        grid_spec=pltpu.PrefetchScalarGridSpec(
            num_scalar_prefetch=2, grid=(1,),
            in_specs=[pl.BlockSpec(memory_space=ANY)] * 2,
            out_specs=pl.BlockSpec((2, 4, 128, 128), lambda g, a, b: (0, 0, 0, 0)),
            scratch_shapes=[V((16, 128, 128), BF), V((2, 4, 128, 128), F32),
                            pltpu.SemaphoreType.DMA((2,)), pltpu.SemaphoreType.DMA((16,))]),
        compiler_params=pltpu.CompilerParams(vmem_limit_bytes=60 << 20),
        name="head",
    )(land, listed, front, arrived)


def panel_kernel(order_ref, panel_ref, hi_hbm, lo_hbm, low_hbm, front_ref, arr_ref, out_ref, pout_ref,
                 brow_ref, bcol_ref, acc_ref, buf_ref, run_ref, arow, ah, al, hi, lo, low, xb, rl, fsem, asem, osem, lsem, ps, pr, xs, xr, ws, wr, ys, yr, rs, rr, zs, zr, fs, fr, ms, mr):
    sub, row, col = lax.axis_index("sub"), lax.axis_index("row"), lax.axis_index("col")
    group = 4 * sub + row
    mate = sub + 1 - 2 * lax.rem(sub, 2)

    def n4(x, d):
        return lax.rem(x + 4 + d, 4)

    def n8(x, d):
        return lax.rem(x + 8 + d, 8)

    def remote(src, dst, send, recv, **where):
        return pltpu.make_async_remote_copy(src, dst, send, recv, device_id=where, device_id_type=MESH)

    loads = [pltpu.make_async_copy(hi_hbm, hi, lsem.at[0]), pltpu.make_async_copy(lo_hbm, lo, lsem.at[1]),
             pltpu.make_async_copy(low_hbm.at[pl.ds(pl.multiple_of(lax.min(group, 7) * 128, 128), 128)], low, lsem.at[2]),
             pltpu.make_async_copy(panel_ref.at[:, col], arow.at[col], lsem.at[3])]
    barrier = pltpu.get_barrier_semaphore()
    for d in (1, 3):
        pl.semaphore_signal(barrier, inc=1, device_id={"row": n4(row, d)}, device_id_type=MESH)
        pl.semaphore_signal(barrier, inc=1, device_id={"sub": n8(sub, 2 * d if d == 1 else -2)}, device_id_type=MESH)
    for d in (1, 2, 3):
        pl.semaphore_signal(barrier, inc=1, device_id={"col": n4(col, d)}, device_id_type=MESH)
    pl.semaphore_signal(barrier, inc=1, device_id={"sub": mate}, device_id_type=MESH)
    for copy in loads:
        copy.start()
    pl.semaphore_wait(barrier, 8)

    def fetch(s):
        return pltpu.make_async_copy(front_ref.at[:, 0, :, s, 0, :], acc_ref.at[s], fsem.at[s])
    def arrived(c):
        return pltpu.make_async_copy(arr_ref.at[pl.ds(c * 32, 32)], buf_ref.at[pl.ds(c * 32, 32)], asem.at[c])
    def put(s):
        return pltpu.make_async_copy(acc_ref.at[s], out_ref.at[:, 0, :, s, 0, :], osem.at[s])
    def early(s):
        return pltpu.make_async_copy(panel_ref.at[s], out_ref.at[:, 0, :, s, 0, :], osem.at[s])
    def each(low, high, f):
        def go(s, c):
            f(s)
            return c
        lax.fori_loop(low, high, go, 0)

    def take(d):
        return remote(panel_ref.at[:, n4(col, d)], arow.at[col], ps.at[d - 1], pr.at[d - 1], col=n4(col, d))
    def taken(d):
        return remote(panel_ref.at[:, n4(col, d)], arow.at[n4(col, -d)], ps.at[d - 1], pr.at[d - 1], col=n4(col, d))
    for d in (1, 3, 2):
        take(d).start()
    each(0, 8, lambda c: arrived(c).start())
    each(2, 32, lambda s: fetch(s).start())
    loads[3].wait()
    for d in (1, 3, 2):
        taken(d).wait_recv()
    for s in range(2):
        for t in range(4):
            a = arow[t, s]
            h = a.astype(BF)
            at = (4 * s + t) * 128
            ah[:, at:at + 128] = h
            al[:, at:at + 128] = (a - h.astype(F32)).astype(BF)
    for copy in loads[:3]:
        copy.wait()
    top = (group < 8) & (col == 0)

    def mm(x, y):
        return lax.dot_general(x, y, (((1,), (1,)), ((), ())), preferred_element_type=F32)
    for b in range(4):
        w = 256 * (b + 1)
        rows = pl.ds(256 * b, 256)
        y = mm(ah[:, 0:w], hi[rows, 0:w]) + (mm(ah[:, 0:w], lo[rows, 0:w]) + mm(al[:, 0:w], hi[rows, 0:w]))
        y = jnp.where(top, low[:, 256 * b:w], y.astype(BF))
        xb[row, :, 256 * b:w] = y
        brow_ref[col, :, 256 * b:w] = y

    half = [pl.ds(0, 64), pl.ds(64, 64)]
    step = [1, -1]
    def xsend(i):
        return remote(xb.at[row], xb.at[row], xs.at[i], xr.at[i], row=n4(row, step[i]))
    def xrecv(i):
        at = xb.at[n4(row, -step[i])]
        return remote(at, at, xs.at[i], xr.at[i], row=n4(row, step[i]))
    def xforward(i, r):
        at = xb.at[r, half[i]]
        return remote(at, at, xs.at[2 + i], xr.at[2 + i], row=n4(row, step[i]))
    def wsend(i):
        return remote(brow_ref.at[col], brow_ref.at[col], ws.at[i], wr.at[i], col=n4(col, step[i]))
    def wrecv(i):
        at = brow_ref.at[n4(col, -step[i])]
        return remote(at, at, ws.at[i], wr.at[i], col=n4(col, step[i]))
    def wforward(i, c):
        at = brow_ref.at[c, half[i]]
        return remote(at, at, ws.at[2 + i], wr.at[2 + i], col=n4(col, step[i]))

    def ynear(i):
        return remote(xb.at[n4(col, step[i])], bcol_ref.at[col, sub], ys.at[i], yr.at[i], col=n4(col, step[i]))
    def ynear_in(i):
        return remote(xb.at[0], bcol_ref.at[n4(col, -step[i]), sub], ys.at[i], yr.at[i], col=n4(col, step[i]))
    def yfar(i):
        return remote(xb.at[n4(col, 2), half[i]], rl.at[i], rs.at[i], rr.at[i], col=n4(col, step[i]))
    def yrelay(i):
        return remote(rl.at[i], bcol_ref.at[n4(col, -step[i]), sub, half[i]], ys.at[2 + i], yr.at[2 + i], col=n4(col, step[i]))
    def yfar_in(i):
        return remote(rl.at[i], bcol_ref.at[n4(col, 2), sub, half[i]], ys.at[2 + i], yr.at[2 + i], col=n4(col, step[i]))
    home = pltpu.make_async_copy(xb.at[col], bcol_ref.at[col, sub], lsem.at[4])

    def ysend(c):
        d = n4(c, -col)
        @pl.when(d == 0)
        def _():
            home.start()
        for i in range(2):
            @pl.when(d == (1, 3)[i])
            def _():
                ynear(i).start()
        @pl.when(d == 2)
        def _():
            yfar(0).start()
            yfar(1).start()

    def own(e, i):
        at = bcol_ref.at[n4(col, e), sub]
        return remote(at if e else xb.at[col], at, zs.at[i, e], zr.at[i, e], sub=n8(sub, 2 * step[i]))
    def arrive(e, i):
        at = bcol_ref.at[n4(col, e), n8(sub, -2 * step[i])]
        return remote(at, at, zs.at[i, e], zr.at[i, e], sub=n8(sub, 2 * step[i]))
    side = [0, 0, 1, 1]
    def onward(e, i, z):
        at = bcol_ref.at[n4(col, e), n8(sub, z)]
        return remote(at, at, fs.at[e], fr.at[e], sub=n8(sub, 2 * step[i]))
    def swap(e, k, z):
        at = bcol_ref.at[n4(col, e), n8(sub, z)]
        return remote(at if k or e else xb.at[col], at, ms.at[k, e], mr.at[k, e], sub=mate)
    def swapped(e, k, z):
        at = bcol_ref.at[n4(col, e), n8(mate, z)]
        return remote(at, at, ms.at[k, e], mr.at[k, e], sub=mate)

    def launch(e):
        own(e, 0).start()
        own(e, 1).start()
        swap(e, 0, 0).start()
    apart = n4(col, -row)

    def gather(c):
        def go(k, total):
            i = c * 32 + k
            total = buf_ref[order_ref[i]].astype(F32) + order_ref[256 + i].astype(F32) * total
            run_ref[i] = total
            return total
        first = jnp.zeros((128, 128), F32) if c == 0 else run_ref[c * 32 - 1]
        lax.fori_loop(0, 32, go, first)

    def settle(s):
        for q in range(4):
            slot = q * 32 + s
            acc_ref[s, q] = acc_ref[s, q] + order_ref[640 + slot].astype(F32) * run_ref[order_ref[512 + slot]]

    keep = jnp.where(group < 8, 0.0, 1.0)
    pair0 = sub - lax.rem(sub, 2)

    def update(e, dz):
        q, z = n4(col, e), n8(pair0, dz)
        s = q * 8 + z
        @pl.when(s >= 2)
        def _():
            y = mm(brow_ref[...].reshape(512, 1024), bcol_ref[q, pl.ds(z, 2)].reshape(256, 1024))
            for u in range(2):
                t = y[:, u * 128:(u + 1) * 128].reshape(4, 128, 128)
                acc_ref[s + u, 0] = acc_ref[s + u, 0] - keep * t[0]
                acc_ref[s + u, 1:4] = acc_ref[s + u, 1:4] - t[1:4]
                put(s + u).start()

    def near():
        ynear_in(1).wait_recv()
        launch(1)
        ynear_in(0).wait_recv()
        launch(3)

    def reach(d):
        ysend(n4(row, d))
        @pl.when(apart == d)
        def _():
            launch(0)

    for i in range(2):
        xsend(i).start()
    for i in range(2):
        wsend(i).start()
    reach(0)
    early(0).start()
    early(1).start()
    each(0, 8, lambda c: arrived(c).wait())
    for c in range(5):
        gather(c)
    for i in range(2):
        xrecv(i).wait_recv()
        xforward(i, n4(row, -step[i])).start()
        reach(3 if i == 0 else 1)
    for i in range(2):
        wrecv(i).wait_recv()
        wforward(i, n4(col, -step[i])).start()
    @pl.when(apart == 0)
    def _():
        near()
    for c in range(5, 8):
        gather(c)
    for i in range(2):
        xforward(i, n4(row, 2)).wait_recv()
    reach(2)
    each(2, 32, lambda s: fetch(s).wait())
    each(2, 12, settle)
    for i in range(2):
        yfar(i).wait_recv()
        yrelay(i).start()
    @pl.when(apart != 0)
    def _():
        near()
    yfar_in(0).wait_recv()
    yfar_in(1).wait_recv()
    launch(2)
    for i in range(2):
        wforward(i, n4(col, 2)).wait_recv()
    each(12, 32, settle)
    for q in range(4):
        pair = [brow_ref[q, :, pl.ds(pl.multiple_of((4 * s + col) * 128, 128), 128)] for s in range(2)]
        pout_ref[q] = jnp.stack([x.astype(F32) for x in pair], 1).astype(BF)
    home.wait()

    def gray(k):
        return k + jnp.where(k == 2, 1, 0) - jnp.where(k == 3, 1, 0)

    def pass_on(k, carry):
        e = gray(k)
        for i in range(2):
            arrive(e, i).wait_recv()
            @pl.when((e < 2) if i == 0 else (e >= 2))
            def _():
                onward(e, i, -2 * step[i]).start()
            swap(e, 1 + i, -2 * step[i]).start()
        swapped(e, 0, 0).wait_recv()
        update(e, 0)
        return carry
    lax.fori_loop(0, 4, pass_on, 0)

    def last(k, carry):
        e = gray(k)
        onward(e, 0, 4).wait_recv()
        swap(e, 3, 4).start()
        def sides(j, c):
            swapped(e, 1 + j, 4 * j - 2).wait_recv()
            update(e, 4 * j - 2)
            return c
        lax.fori_loop(0, 2, sides, 0)
        return carry
    lax.fori_loop(0, 4, last, 0)

    def far(k, carry):
        e = gray(k)
        swapped(e, 3, 4).wait_recv()
        update(e, 4)
        return carry
    lax.fori_loop(0, 4, far, 0)
    early(0).wait()
    early(1).wait()
    each(2, 32, lambda s: put(s).wait())

    for d in (1, 2, 3):
        take(d).wait_send()
    for i in range(2):
        xsend(i).wait_send()
        wsend(i).wait_send()
        xforward(i, n4(row, -step[i])).wait_send()
        wforward(i, n4(col, -step[i])).wait_send()
        ynear(i).wait_send()
        yfar(i).wait_send()
        yrelay(i).wait_send()
    for e in range(4):
        own(e, 0).wait_send()
        own(e, 1).wait_send()
        onward(e, side[e], -2 * step[side[e]]).wait_send()
        swap(e, 0, 0).wait_send()
        swap(e, 1, -2).wait_send()
        swap(e, 2, 2).wait_send()
        swap(e, 3, 4).wait_send()


def panel_exchange(order, panel, hi, lo, low, front, arrived):
    D = pltpu.SemaphoreType.DMA
    H = pltpu.HBM
    return pl.pallas_call(
        panel_kernel,
        out_shape=(jax.ShapeDtypeStruct((4, 1, 128, 32, 1, 128), F32), jax.ShapeDtypeStruct((4, 128, 2, 128), BF)),
        in_specs=[pl.BlockSpec(memory_space=pltpu.SMEM), pl.BlockSpec(memory_space=V)] + [pl.BlockSpec(memory_space=H)] * 5,
        out_specs=(pl.BlockSpec(memory_space=H), pl.BlockSpec(memory_space=V)),
        scratch_shapes=[V((4, 128, 1024), BF), V((4, 8, 128, 1024), BF), V((32, 4, 128, 128), F32), V((256, 128, 128), BF),
                        V((256, 128, 128), F32), V((4, 2, 128, 128), F32), V((128, 1024), BF), V((128, 1024), BF),
                        V((1024, 1024), BF), V((1024, 1024), BF),
                        V((128, 1024), BF), V((4, 128, 1024), BF), V((2, 64, 1024), BF), D((32,)), D((8,)), D((32,)),
                        D((5,)), D((3,)), D((3,)), D((4,)), D((4,)), D((4,)), D((4,)), D((4,)), D((4,)), D((2,)), D((2,)),
                        D((2, 4)), D((2, 4)), D((4,)), D((4,)), D((4, 4)), D((4, 4))],
        compiler_params=pltpu.CompilerParams(vmem_limit_bytes=60 << 20, collective_id=2, has_side_effects=True),
        name="panel",
    )(order, panel, hi, lo, low, front, arrived)


def lead_kernel(front_ref, code_ref, lead_ref, codes_ref, own_ref, lsem, zs, zr, zls, zlr, xs, xr, ys, yr, as_, ar, bs, br, cs, cr):
    sub, row, col = lax.axis_index("sub"), lax.axis_index("row"), lax.axis_index("col")
    par = lax.rem(sub, 2)
    mate = sub + 1 - 2 * par
    line = 4 * par + row
    need = (par == 1) | (col <= row)

    def remote(src, dst, send, recv, **where):
        return pltpu.make_async_remote_copy(src, dst, send, recv, device_id=where, device_id_type=MESH)

    barrier = pltpu.get_barrier_semaphore()
    for d in range(1, 8):
        pl.semaphore_signal(barrier, inc=1, device_id={"sub": lax.rem(sub + d, 8)}, device_id_type=MESH)
    for d in range(1, 4):
        pl.semaphore_signal(barrier, inc=1, device_id={"row": lax.rem(row + d, 4)}, device_id_type=MESH)
        pl.semaphore_signal(barrier, inc=1, device_id={"col": lax.rem(col + d, 4)}, device_id_type=MESH)

    mine = [pltpu.make_async_copy(front_ref.at[0, 0, :, s, 0, :], own_ref.at[s], lsem.at[s]) for s in range(2)]
    code = pltpu.make_async_copy(code_ref, codes_ref.at[col, row, sub], lsem.at[2])
    code.start()
    mine[0].start()
    mine[1].start()
    mine[0].wait()
    mine[1].wait()
    keep = [pltpu.make_async_copy(own_ref.at[s], lead_ref.at[line, 4 * s + col], lsem.at[3 + s]) for s in range(2)]

    @pl.when(sub < 2)
    def _():
        keep[0].start()
        keep[1].start()
    pl.semaphore_wait(barrier, 13)

    def zcode(d):
        return remote(code_ref, codes_ref.at[col, row, sub], zs.at[d - 1], zr.at[d - 1], sub=lax.rem(sub + d, 8))
    def zcode_in(d):
        return remote(code_ref, codes_ref.at[col, row, lax.rem(sub + 8 - d, 8)], zs.at[d - 1], zr.at[d - 1], sub=lax.rem(sub + d, 8))
    need1 = (par == 1) & (col <= row)

    @pl.when(sub < 2)
    def _():
        for d in (1, 3, 2):
            @pl.when(need)
            def _():
                remote(own_ref.at[0], lead_ref.at[line, col], zls.at[d - 1, 0], zlr.at[0], sub=sub + 2 * d).start()
            @pl.when(need1)
            def _():
                remote(own_ref.at[1], lead_ref.at[line, 4 + col], zls.at[d - 1, 1], zlr.at[1], sub=sub + 2 * d).start()
    for d in range(1, 8):
        zcode(d).start()

    @pl.when(sub < 2)
    def _():
        keep[0].wait()
        keep[1].wait()

    @pl.when(sub >= 2)
    def _():
        @pl.when(need)
        def _():
            remote(own_ref.at[0], lead_ref.at[line, col], zls.at[0, 0], zlr.at[0], sub=par).wait_recv()
        @pl.when(need1)
        def _():
            remote(own_ref.at[1], lead_ref.at[line, 4 + col], zls.at[0, 1], zlr.at[1], sub=par).wait_recv()

    def ax(d, r):
        return remote(lead_ref.at[4 + r, col], lead_ref.at[4 + r, col], as_.at[0, d - 1], ar.at[0, d - 1], row=lax.rem(row + d, 4))
    def ay(d, c):
        return remote(lead_ref.at[pl.ds(4, 4), c], lead_ref.at[pl.ds(4, 4), c], as_.at[1, d - 1], ar.at[1, d - 1], col=lax.rem(col + d, 4))
    def by(d, c):
        at = lead_ref.at[line, 4 * par + c]
        return remote(at, at, bs.at[d - 1, 4], br.at[d - 1, 4], col=lax.rem(col + d, 4))
    def bx(d, r, c):
        at = lead_ref.at[4 * par + r, 4 * par + c]
        return remote(at, at, bs.at[d - 1, c], br.at[d - 1, c], row=lax.rem(row + d, 4))
    for d in (1, 3, 2):
        @pl.when(par == 1)
        def _():
            ax(d, row).start()
        @pl.when(col <= row)
        def _():
            by(d, col).start()
    code.wait()
    for d in range(1, 8):
        zcode_in(d).wait_recv()
    def cx(d, r):
        return remote(codes_ref.at[col, r], codes_ref.at[col, r], xs.at[d - 1], xr.at[d - 1], row=lax.rem(row + d, 4))
    def cy(d, c):
        return remote(codes_ref.at[c], codes_ref.at[c], ys.at[d - 1], yr.at[d - 1], col=lax.rem(col + d, 4))
    for d in range(1, 4):
        cx(d, row).start()
    for d in range(1, 4):
        @pl.when(par == 1)
        def _():
            ax(d, lax.rem(row + 4 - d, 4)).wait_recv()
        @pl.when(lax.rem(col + 4 - d, 4) <= row)
        def _():
            by(d, lax.rem(col + 4 - d, 4)).wait_recv()
    for d in (1, 3, 2):
        @pl.when(par == 1)
        def _():
            ay(d, col).start()
        for c in range(4):
            @pl.when(c <= row)
            def _():
                bx(d, row, c).start()
    for d in range(1, 4):
        cx(d, lax.rem(row + 4 - d, 4)).wait_recv()
    for d in range(1, 4):
        cy(d, col).start()
    for d in range(1, 4):
        @pl.when(par == 1)
        def _():
            ay(d, lax.rem(col + 4 - d, 4)).wait_recv()
        for c in range(4):
            r = lax.rem(row + 4 - d, 4)
            @pl.when(c <= r)
            def _():
                bx(d, r, c).wait_recv()

    def swap(i):
        at = lead_ref.at[i, pl.ds(0, i + 1)]
        return remote(at, at, cs.at[i % 4], cr.at[i % 4], sub=mate)
    for i in range(8):
        @pl.when(par == i // 4)
        def _():
            swap(i).start()
    for i in range(8):
        @pl.when(par != i // 4)
        def _():
            swap(i).wait_recv()
    for d in range(1, 4):
        cy(d, lax.rem(col + 4 - d, 4)).wait_recv()

    for d in range(1, 8):
        zcode(d).wait_send()
    @pl.when(sub < 2)
    def _():
        for d in (1, 2, 3):
            @pl.when(need)
            def _():
                remote(own_ref.at[0], lead_ref.at[line, col], zls.at[d - 1, 0], zlr.at[0], sub=sub + 2 * d).wait_send()
            @pl.when(need1)
            def _():
                remote(own_ref.at[1], lead_ref.at[line, 4 + col], zls.at[d - 1, 1], zlr.at[1], sub=sub + 2 * d).wait_send()
    for d in range(1, 4):
        cx(d, row).wait_send()
        cy(d, col).wait_send()
        @pl.when(par == 1)
        def _():
            ax(d, row).wait_send()
            ay(d, col).wait_send()
        @pl.when(col <= row)
        def _():
            by(d, col).wait_send()
        for c in range(4):
            @pl.when(c <= row)
            def _():
                bx(d, row, c).wait_send()
    for i in range(8):
        @pl.when(par == i // 4)
        def _():
            swap(i).wait_send()


def lead_gather(front, code):
    D = pltpu.SemaphoreType.DMA
    return pl.pallas_call(
        lead_kernel,
        out_shape=(jax.ShapeDtypeStruct((8, 8, 128, 128), F32), jax.ShapeDtypeStruct((4, 4, 8, 1, 128), jnp.int32)),
        in_specs=[pl.BlockSpec(memory_space=pltpu.HBM), pl.BlockSpec(memory_space=V)],
        out_specs=(pl.BlockSpec(memory_space=V), pl.BlockSpec(memory_space=V)),
        scratch_shapes=[V((2, 128, 128), F32), D((5,)), D((7,)), D((7,)), D((3, 2)), D((2,)), D((3,)), D((3,)), D((3,)), D((3,)),
                        D((2, 3)), D((2, 3)), D((3, 5)), D((3, 5)), D((4,)), D((4,))],
        compiler_params=pltpu.CompilerParams(vmem_limit_bytes=60 << 20, collective_id=1, has_side_effects=True),
        name="lead",
    )(front, code)


def landings(codes, me):
    codes = codes[:, :, :, 0, :].transpose(2, 1, 0, 3).reshape(128, 128)
    place = lax.broadcasted_iota(jnp.int32, (128, 128), 1) * 128 + codes % 128
    match = codes // 128 == me
    first = jnp.min(jnp.where(match, place, 1 << 20), 1)
    last = jnp.max(jnp.where(match, place, -1), 1)
    one = jnp.where(last >= 0, first % 128, -1)
    two = jnp.where(last > first, last % 128, -1)
    return jnp.stack([one, two], 1).reshape(256)


def local(front, child_tiles, tile_owner, tile_slot):
    sub = lax.axis_index("sub")
    row = lax.axis_index("row")
    col = lax.axis_index("col")
    group = sub * 4 + row
    owner = tile_owner[:, 0]
    outgoing = route(owner, child_tiles)
    lead, codes = lead_gather(front, (owner * 128 + tile_slot).reshape(1, 128))
    outgoing, lead = lax.optimization_barrier((outgoing, lead))
    arrived = lax.all_to_all(outgoing, ("sub", "row", "col"), split_axis=0, concat_axis=0, tiled=True)
    arrived = arrived.reshape(256, 128, 128)
    factor, hi, lo = chol(lead)
    landing = landings(codes, group * 4 + col)
    listed, order = plan(landing)
    panel = head(landing, listed, front, arrived)
    out, panel_out = panel_exchange(order, panel, hi, lo, factor, front, arrived)
    return out, panel_out.reshape(4, 1, 128, 2, 1, 128)


def solution(mesh):
    return jax.shard_map(
        local,
        mesh=mesh,
        in_specs=(
            P(None, ("sub", "row"), None, None, "col", None),
            P(("sub", "row", "col"), None, None),
            P(("sub", "row", "col"), None),
            P(("sub", "row", "col")),
        ),
        out_specs=(
            P(None, ("sub", "row"), None, None, "col", None),
            P(None, ("sub", "row"), None, None, "col", None),
        ),
        check_vma=False,
    )
```

```python
import jax
import jax.numpy as jnp
from jax import lax
from jax.experimental import pallas as pl
from jax.experimental.pallas import tpu as pltpu
from jax.sharding import PartitionSpec as P

F32, BF = jnp.float32, jnp.bfloat16
HI = lax.Precision.HIGHEST
V = pltpu.VMEM
ANY = pl.ANY
MESH = pl.DeviceIdType.MESH


def nt(a, b):
    return lax.dot_general(a, b, (((1,), (1,)), ((), ())), precision=HI, preferred_element_type=F32)


def nn(a, b):
    return lax.dot_general(a, b, (((1,), (0,)), ((), ())), precision=HI, preferred_element_type=F32)


def split3(x):
    h = x.astype(BF).astype(F32)
    r = x - h
    m = r.astype(BF).astype(F32)
    return h, m, r - m


def diag_factor(d_ref, u_ref, x_ref, cb_ref, r_ref):
    def body(b, carry):
        r0 = pl.multiple_of(b * 8, 8)
        block = d_ref[pl.ds(r0, 8), 0:128]
        rolled = pltpu.roll(block, (128 - r0) % 128, 1)
        for j in range(8):
            cb_ref[j] = jnp.broadcast_to(rolled[:, j:j + 1], (8, 128))
        r_ref[:, 0:128] = block
        r_ref[:, 128:256] = d_ref[pl.ds(r0, 8), 128:256]
        e = {}
        for i in range(8):
            for j in range(i + 1):
                e[i, j] = cb_ref[j, i:i + 1, :]
        rows = []
        for i in range(8):
            rows.append([r_ref[i:i + 1, 0:128], r_ref[i:i + 1, 128:256]])
        for j in range(8):
            inv = lax.rsqrt(e[j, j])
            low = {}
            for i in range(j + 1, 8):
                low[i] = e[i, j] * inv
            for h in range(2):
                rows[j][h] = rows[j][h] * inv
            for i in range(j + 1, 8):
                for m in range(j + 1, i + 1):
                    e[i, m] = e[i, m] - low[i] * low[m]
                for h in range(2):
                    rows[i][h] = rows[i][h] - low[i] * rows[j][h]
        for i in range(8):
            r_ref[i:i + 1, 0:128] = rows[i][0]
            r_ref[i:i + 1, 128:256] = rows[i][1]
        r = r_ref[...]
        u_ref[pl.ds(r0, 8), :] = r[:, 0:128]
        x_ref[pl.ds(r0, 8), :] = r[:, 128:256]
        h, m, l = split3(r)
        left = jnp.concatenate([h, h, m, h, l, m], 0)[:, 0:128].astype(BF)
        right = jnp.concatenate([h, m, h, l, h, m], 0).astype(BF)
        d_ref[...] = d_ref[...] - lax.dot_general(left, right, (((0,), (0,)), ((), ())), preferred_element_type=F32)
        return carry
    lax.fori_loop(0, 16, body, 0)


def chol_kernel(lead_ref, l_ref, hi_ref, lo_ref, s_ref, w_ref, d_ref, u_ref, x_ref, cb_ref, r_ref):
    row = lax.broadcasted_iota(jnp.int32, (128, 128), 0)
    col = lax.broadcasted_iota(jnp.int32, (128, 128), 1)
    eye = (row == col).astype(F32)
    n = 8
    for i in range(n):
        for j in range(i + 1):
            t = lead_ref[i, j]
            if i == j:
                t = jnp.where(row >= col, t, t.T)
            s_ref[i * 128:(i + 1) * 128, j * 128:(j + 1) * 128] = t
    w_ref[...] = jnp.zeros_like(w_ref)
    l_ref[...] = jnp.zeros_like(l_ref)
    for k in range(n):
        a, b = k * 128, (k + 1) * 128
        d_ref[:, 0:128] = s_ref[a:b, a:b]
        d_ref[:, 128:256] = eye
        diag_factor(d_ref, u_ref, x_ref, cb_ref, r_ref)
        x = x_ref[...]
        l_ref[a:b, a:b] = jnp.where(row >= col, u_ref[...].T, 0.0).astype(BF)
        if k > 0:
            w_ref[a:b, 0:a] = nn(x, w_ref[a:b, 0:a])
        w_ref[a:b, a:b] = x
        if k < n - 1:
            p = nt(s_ref[b:, a:b], x)
            s_ref[b:, a:b] = p
            l_ref[b:, a:b] = p.astype(BF)
            for j in range(k + 1, n):
                c, d = j * 128, (j + 1) * 128
                s_ref[c:, c:d] = s_ref[c:, c:d] - nt(s_ref[c:, a:b], s_ref[c:d, a:b])
            w_ref[b:, 0:b] = w_ref[b:, 0:b] - nn(p, w_ref[a:b, 0:b])
    for k in range(n):
        a, b = k * 128, (k + 1) * 128
        y = w_ref[a:b, :]
        h = y.astype(BF)
        hi_ref[a:b, :] = h
        lo_ref[a:b, :] = (y - h.astype(F32)).astype(BF)


def chol(lead):
    return pl.pallas_call(
        chol_kernel,
        out_shape=[jax.ShapeDtypeStruct((1024, 1024), BF)] * 3,
        in_specs=[pl.BlockSpec(memory_space=V)],
        out_specs=[pl.BlockSpec(memory_space=V)] * 3,
        scratch_shapes=[V((1024, 1024), F32), V((1024, 1024), F32), V((128, 256), F32), V((128, 128), F32),
                        V((128, 128), F32), V((8, 8, 128), F32), V((8, 256), F32)],
        compiler_params=pltpu.CompilerParams(vmem_limit_bytes=30 << 20),
        name="chol",
    )(lead)


def index_kernel(owner_ref, slot_ref, idx_ref, code_ref):
    owner = owner_ref[...]
    code_ref[...] = owner * 128 + slot_ref[...]
    wide = jnp.broadcast_to(owner.astype(F32), (128, 128)).T
    k = lax.broadcasted_iota(jnp.int32, (128, 128), 0).astype(F32)
    match = wide == lax.broadcasted_iota(jnp.int32, (128, 128), 1).astype(F32)
    first = jnp.min(jnp.where(match, k, 127.0), 0, keepdims=True)
    last = jnp.max(jnp.where(match, k, 0.0), 0, keepdims=True)
    idx_ref[0:1, :] = first.astype(jnp.int32)
    idx_ref[1:2, :] = last.astype(jnp.int32)


def index(owner, slot):
    return pl.pallas_call(
        index_kernel,
        out_shape=(jax.ShapeDtypeStruct((2, 128), jnp.int32), jax.ShapeDtypeStruct((1, 128), jnp.int32)),
        in_specs=[pl.BlockSpec(memory_space=V)] * 2,
        out_specs=[pl.BlockSpec(memory_space=V)] * 2,
        name="index",
    )(owner, slot)


def plan_kernel(col_ref, row_ref, out_ref):
    def at(shape, axis):
        return lax.broadcasted_iota(jnp.int32, shape, axis).astype(F32)
    square = (256, 256)
    own = jnp.broadcast_to(col_ref[...], square).astype(F32)
    other = jnp.broadcast_to(row_ref[...], square).astype(F32)
    k, j = at(square, 0), at(square, 1)
    one = jnp.ones(square, F32)
    zero = jnp.zeros(square, F32)
    key, other_key = jnp.where(own < 0, 1000.0, own), jnp.where(other < 0, 1000.0, other)
    before = (other_key < key) | ((other_key == key) & (j < k))
    rank = jnp.sum(jnp.where(before, one, zero), 1, keepdims=True)
    here = jnp.broadcast_to(rank, square) == j
    order = jnp.sum(jnp.where(here, k, zero), 0, keepdims=True)
    slots = jnp.sum(jnp.where(here, key, zero), 0, keepdims=True)
    lane = at((1, 256), 1)
    same = jnp.where((slots == pltpu.roll(slots, 1, 1)) & (lane > 0) & (slots < 1000.0), 1.0, 0.0)
    half = (256, 128)
    slot = at(half, 1)
    own_key = key[:, 0:128]
    last = jnp.sum(jnp.where(own_key <= slot, 1.0, 0.0), 0, keepdims=True) - 1.0
    some = jnp.max(jnp.where(own_key == slot, 1.0, 0.0), 0, keepdims=True)

    def panel_column(x):
        return (x >= 0) & (x - 32.0 * jnp.floor(x * (1 / 32)) < 2.0)
    hit, other_hit = panel_column(own), panel_column(other)
    turn = jnp.sum(jnp.where(other_hit & (j < k), one, zero), 1, keepdims=True)
    listed = jnp.sum(jnp.where(hit & (jnp.broadcast_to(turn, square) == j), k, zero), 0, keepdims=True)
    count = jnp.sum(jnp.where(hit, one, zero), 0, keepdims=True)
    rows = [order, same, jnp.concatenate([jnp.maximum(last, 0.0), some], 1), listed, count]
    for r in range(5):
        out_ref[r:r + 1, :] = rows[r].astype(jnp.int32)


def plan(land):
    return pl.pallas_call(
        plan_kernel,
        out_shape=jax.ShapeDtypeStruct((5, 256), jnp.int32),
        in_specs=[pl.BlockSpec(memory_space=V)] * 2,
        out_specs=pl.BlockSpec(memory_space=V),
        name="plan",
    )(land.reshape(256, 1), land.reshape(1, 256))


def head_kernel(land_ref, list_ref, front_ref, arr_ref, out_ref, buf_ref, acc_ref, fsem, asem):
    count = list_ref[4, 0]
    def arrive(n, i):
        return pltpu.make_async_copy(arr_ref.at[list_ref[3, n]], buf_ref.at[i], asem.at[i])
    def fetch(s):
        return pltpu.make_async_copy(front_ref.at[:, 0, :, s, 0, :], acc_ref.at[s], fsem.at[s])
    for s in range(2):
        fetch(s).start()
    def batch(b, carry):
        def begin(i, c):
            arrive(b * 16 + i, i).start()
            return c
        def end(i, c):
            n = b * 16 + i
            slot = land_ref[list_ref[3, n]]
            s, q = slot % 32, slot // 32
            arrive(n, i).wait()
            acc_ref[s, q] = acc_ref[s, q] + buf_ref[i].astype(F32)
            return c
        here = lax.min(count - b * 16, 16)
        lax.fori_loop(0, here, begin, 0)
        @pl.when(b == 0)
        def _():
            for s in range(2):
                fetch(s).wait()
        lax.fori_loop(0, here, end, 0)
        return carry
    lax.fori_loop(0, lax.max((count + 15) // 16, 1), batch, 0)
    out_ref[...] = acc_ref[...]


def head(land, listed, front, arrived):
    return pl.pallas_call(
        head_kernel,
        out_shape=jax.ShapeDtypeStruct((2, 4, 128, 128), F32),
        grid_spec=pltpu.PrefetchScalarGridSpec(
            num_scalar_prefetch=2, grid=(1,),
            in_specs=[pl.BlockSpec(memory_space=ANY)] * 2,
            out_specs=pl.BlockSpec((2, 4, 128, 128), lambda g, a, b: (0, 0, 0, 0)),
            scratch_shapes=[V((16, 128, 128), BF), V((2, 4, 128, 128), F32),
                            pltpu.SemaphoreType.DMA((2,)), pltpu.SemaphoreType.DMA((16,))]),
        compiler_params=pltpu.CompilerParams(vmem_limit_bytes=60 << 20),
        name="head",
    )(land, listed, front, arrived)


def panel_kernel(order_ref, panel_ref, hi_hbm, lo_hbm, low_hbm, front_ref, arr_ref, out_ref, pout_ref,
                 brow_ref, bcol_ref, acc_ref, buf_ref, run_ref, arow, ah, al, hi, lo, low, xb, rl, fsem, asem, osem, lsem, ps, pr, xs, xr, ws, wr, ys, yr, rs, rr, zs, zr, fs, fr, ms, mr):
    sub, row, col = lax.axis_index("sub"), lax.axis_index("row"), lax.axis_index("col")
    group = 4 * sub + row
    mate = sub + 1 - 2 * lax.rem(sub, 2)

    def n4(x, d):
        return lax.rem(x + 4 + d, 4)

    def n8(x, d):
        return lax.rem(x + 8 + d, 8)

    def remote(src, dst, send, recv, **where):
        return pltpu.make_async_remote_copy(src, dst, send, recv, device_id=where, device_id_type=MESH)

    loads = [pltpu.make_async_copy(hi_hbm, hi, lsem.at[0]), pltpu.make_async_copy(lo_hbm, lo, lsem.at[1]),
             pltpu.make_async_copy(low_hbm.at[pl.ds(pl.multiple_of(lax.min(group, 7) * 128, 128), 128)], low, lsem.at[2]),
             pltpu.make_async_copy(panel_ref.at[:, col], arow.at[col], lsem.at[3])]
    barrier = pltpu.get_barrier_semaphore()
    for d in (1, 3):
        pl.semaphore_signal(barrier, inc=1, device_id={"row": n4(row, d)}, device_id_type=MESH)
        pl.semaphore_signal(barrier, inc=1, device_id={"sub": n8(sub, 2 * d if d == 1 else -2)}, device_id_type=MESH)
    for d in (1, 2, 3):
        pl.semaphore_signal(barrier, inc=1, device_id={"col": n4(col, d)}, device_id_type=MESH)
    pl.semaphore_signal(barrier, inc=1, device_id={"sub": mate}, device_id_type=MESH)
    for copy in loads:
        copy.start()
    pl.semaphore_wait(barrier, 8)

    def fetch(s):
        return pltpu.make_async_copy(front_ref.at[:, 0, :, s, 0, :], acc_ref.at[s], fsem.at[s])
    def arrived(c):
        return pltpu.make_async_copy(arr_ref.at[pl.ds(c * 32, 32)], buf_ref.at[pl.ds(c * 32, 32)], asem.at[c])
    def put(s):
        return pltpu.make_async_copy(acc_ref.at[s], out_ref.at[:, 0, :, s, 0, :], osem.at[s])
    def early(s):
        return pltpu.make_async_copy(panel_ref.at[s], out_ref.at[:, 0, :, s, 0, :], osem.at[s])
    def each(low, high, f):
        def go(s, c):
            f(s)
            return c
        lax.fori_loop(low, high, go, 0)

    def take(d):
        return remote(panel_ref.at[:, n4(col, d)], arow.at[col], ps.at[d - 1], pr.at[d - 1], col=n4(col, d))
    def taken(d):
        return remote(panel_ref.at[:, n4(col, d)], arow.at[n4(col, -d)], ps.at[d - 1], pr.at[d - 1], col=n4(col, d))
    for d in (1, 3, 2):
        take(d).start()
    each(0, 8, lambda c: arrived(c).start())
    each(2, 32, lambda s: fetch(s).start())
    loads[3].wait()
    for d in (1, 3, 2):
        taken(d).wait_recv()
    for s in range(2):
        for t in range(4):
            a = arow[t, s]
            h = a.astype(BF)
            at = (4 * s + t) * 128
            ah[:, at:at + 128] = h
            al[:, at:at + 128] = (a - h.astype(F32)).astype(BF)
    for copy in loads[:3]:
        copy.wait()
    top = (group < 8) & (col == 0)

    def mm(x, y):
        return lax.dot_general(x, y, (((1,), (1,)), ((), ())), preferred_element_type=F32)
    for b in range(4):
        w = 256 * (b + 1)
        rows = pl.ds(256 * b, 256)
        y = mm(ah[:, 0:w], hi[rows, 0:w]) + (mm(ah[:, 0:w], lo[rows, 0:w]) + mm(al[:, 0:w], hi[rows, 0:w]))
        y = jnp.where(top, low[:, 256 * b:w], y.astype(BF))
        xb[row, :, 256 * b:w] = y
        brow_ref[col, :, 256 * b:w] = y

    half = [pl.ds(0, 64), pl.ds(64, 64)]
    step = [1, -1]
    def xsend(i):
        return remote(xb.at[row], xb.at[row], xs.at[i], xr.at[i], row=n4(row, step[i]))
    def xrecv(i):
        at = xb.at[n4(row, -step[i])]
        return remote(at, at, xs.at[i], xr.at[i], row=n4(row, step[i]))
    def xforward(i, r):
        at = xb.at[r, half[i]]
        return remote(at, at, xs.at[2 + i], xr.at[2 + i], row=n4(row, step[i]))
    def wsend(i):
        return remote(brow_ref.at[col], brow_ref.at[col], ws.at[i], wr.at[i], col=n4(col, step[i]))
    def wrecv(i):
        at = brow_ref.at[n4(col, -step[i])]
        return remote(at, at, ws.at[i], wr.at[i], col=n4(col, step[i]))
    def wforward(i, c):
        at = brow_ref.at[c, half[i]]
        return remote(at, at, ws.at[2 + i], wr.at[2 + i], col=n4(col, step[i]))

    def ynear(i):
        return remote(xb.at[n4(col, step[i])], bcol_ref.at[col, sub], ys.at[i], yr.at[i], col=n4(col, step[i]))
    def ynear_in(i):
        return remote(xb.at[0], bcol_ref.at[n4(col, -step[i]), sub], ys.at[i], yr.at[i], col=n4(col, step[i]))
    def yfar(i):
        return remote(xb.at[n4(col, 2), half[i]], rl.at[i], rs.at[i], rr.at[i], col=n4(col, step[i]))
    def yrelay(i):
        return remote(rl.at[i], bcol_ref.at[n4(col, -step[i]), sub, half[i]], ys.at[2 + i], yr.at[2 + i], col=n4(col, step[i]))
    def yfar_in(i):
        return remote(rl.at[i], bcol_ref.at[n4(col, 2), sub, half[i]], ys.at[2 + i], yr.at[2 + i], col=n4(col, step[i]))
    home = pltpu.make_async_copy(xb.at[col], bcol_ref.at[col, sub], lsem.at[4])

    def ysend(c):
        d = n4(c, -col)
        @pl.when(d == 0)
        def _():
            home.start()
        for i in range(2):
            @pl.when(d == (1, 3)[i])
            def _():
                ynear(i).start()
        @pl.when(d == 2)
        def _():
            yfar(0).start()
            yfar(1).start()

    def own(e, i):
        at = bcol_ref.at[n4(col, e), sub]
        return remote(at if e else xb.at[col], at, zs.at[i, e], zr.at[i, e], sub=n8(sub, 2 * step[i]))
    def arrive(e, i):
        at = bcol_ref.at[n4(col, e), n8(sub, -2 * step[i])]
        return remote(at, at, zs.at[i, e], zr.at[i, e], sub=n8(sub, 2 * step[i]))
    side = [0, 0, 1, 1]
    def onward(e, i, z):
        at = bcol_ref.at[n4(col, e), n8(sub, z)]
        return remote(at, at, fs.at[e], fr.at[e], sub=n8(sub, 2 * step[i]))
    def swap(e, k, z):
        at = bcol_ref.at[n4(col, e), n8(sub, z)]
        return remote(at if k or e else xb.at[col], at, ms.at[k, e], mr.at[k, e], sub=mate)
    def swapped(e, k, z):
        at = bcol_ref.at[n4(col, e), n8(mate, z)]
        return remote(at, at, ms.at[k, e], mr.at[k, e], sub=mate)

    def launch(e):
        own(e, 0).start()
        own(e, 1).start()
        swap(e, 0, 0).start()
    apart = n4(col, -row)

    def gather(c):
        def go(k, total):
            i = c * 32 + k
            total = buf_ref[order_ref[0, i]].astype(F32) + order_ref[1, i].astype(F32) * total
            run_ref[i] = total
            return total
        first = jnp.zeros((128, 128), F32) if c == 0 else run_ref[c * 32 - 1]
        lax.fori_loop(0, 32, go, first)

    def settle(s):
        for q in range(4):
            slot = q * 32 + s
            acc_ref[s, q] = acc_ref[s, q] + order_ref[2, 128 + slot].astype(F32) * run_ref[order_ref[2, slot]]

    keep = jnp.where(group < 8, 0.0, 1.0)
    pair0 = sub - lax.rem(sub, 2)

    def update(e, dz):
        q, z = n4(col, e), n8(pair0, dz)
        s = q * 8 + z
        @pl.when(s >= 2)
        def _():
            y = mm(brow_ref[...].reshape(512, 1024), bcol_ref[q, pl.ds(z, 2)].reshape(256, 1024))
            for u in range(2):
                t = y[:, u * 128:(u + 1) * 128].reshape(4, 128, 128)
                acc_ref[s + u, 0] = acc_ref[s + u, 0] - keep * t[0]
                acc_ref[s + u, 1:4] = acc_ref[s + u, 1:4] - t[1:4]
                put(s + u).start()

    def near():
        ynear_in(1).wait_recv()
        launch(1)
        ynear_in(0).wait_recv()
        launch(3)

    def reach(d):
        ysend(n4(row, d))
        @pl.when(apart == d)
        def _():
            launch(0)

    for i in range(2):
        xsend(i).start()
    for i in range(2):
        wsend(i).start()
    reach(0)
    early(0).start()
    early(1).start()
    each(0, 8, lambda c: arrived(c).wait())
    for c in range(5):
        gather(c)
    for i in range(2):
        xrecv(i).wait_recv()
        xforward(i, n4(row, -step[i])).start()
        reach(3 if i == 0 else 1)
    for i in range(2):
        wrecv(i).wait_recv()
        wforward(i, n4(col, -step[i])).start()
    @pl.when(apart == 0)
    def _():
        near()
    for c in range(5, 8):
        gather(c)
    for i in range(2):
        xforward(i, n4(row, 2)).wait_recv()
    reach(2)
    each(2, 32, lambda s: fetch(s).wait())
    each(2, 12, settle)
    for i in range(2):
        yfar(i).wait_recv()
        yrelay(i).start()
    @pl.when(apart != 0)
    def _():
        near()
    yfar_in(0).wait_recv()
    yfar_in(1).wait_recv()
    launch(2)
    for i in range(2):
        wforward(i, n4(col, 2)).wait_recv()
    each(12, 32, settle)
    for q in range(4):
        pair = [brow_ref[q, :, pl.ds(pl.multiple_of((4 * s + col) * 128, 128), 128)] for s in range(2)]
        pout_ref[q] = jnp.stack([x.astype(F32) for x in pair], 1).astype(BF)
    home.wait()

    def gray(k):
        return k + jnp.where(k == 2, 1, 0) - jnp.where(k == 3, 1, 0)

    def pass_on(k, carry):
        e = gray(k)
        for i in range(2):
            arrive(e, i).wait_recv()
            @pl.when((e < 2) if i == 0 else (e >= 2))
            def _():
                onward(e, i, -2 * step[i]).start()
            swap(e, 1 + i, -2 * step[i]).start()
        swapped(e, 0, 0).wait_recv()
        update(e, 0)
        return carry
    lax.fori_loop(0, 4, pass_on, 0)

    def last(k, carry):
        e = gray(k)
        onward(e, 0, 4).wait_recv()
        swap(e, 3, 4).start()
        def sides(j, c):
            swapped(e, 1 + j, 4 * j - 2).wait_recv()
            update(e, 4 * j - 2)
            return c
        lax.fori_loop(0, 2, sides, 0)
        return carry
    lax.fori_loop(0, 4, last, 0)

    def far(k, carry):
        e = gray(k)
        swapped(e, 3, 4).wait_recv()
        update(e, 4)
        return carry
    lax.fori_loop(0, 4, far, 0)
    early(0).wait()
    early(1).wait()
    each(2, 32, lambda s: put(s).wait())

    for d in (1, 2, 3):
        take(d).wait_send()
    for i in range(2):
        xsend(i).wait_send()
        wsend(i).wait_send()
        xforward(i, n4(row, -step[i])).wait_send()
        wforward(i, n4(col, -step[i])).wait_send()
        ynear(i).wait_send()
        yfar(i).wait_send()
        yrelay(i).wait_send()
    for e in range(4):
        own(e, 0).wait_send()
        own(e, 1).wait_send()
        onward(e, side[e], -2 * step[side[e]]).wait_send()
        swap(e, 0, 0).wait_send()
        swap(e, 1, -2).wait_send()
        swap(e, 2, 2).wait_send()
        swap(e, 3, 4).wait_send()


def panel_exchange(order, panel, hi, lo, low, front, arrived):
    D = pltpu.SemaphoreType.DMA
    H = pltpu.HBM
    return pl.pallas_call(
        panel_kernel,
        out_shape=(jax.ShapeDtypeStruct((4, 1, 128, 32, 1, 128), F32), jax.ShapeDtypeStruct((4, 128, 2, 128), BF)),
        in_specs=[pl.BlockSpec(memory_space=pltpu.SMEM), pl.BlockSpec(memory_space=V)] + [pl.BlockSpec(memory_space=H)] * 5,
        out_specs=(pl.BlockSpec(memory_space=H), pl.BlockSpec(memory_space=V)),
        scratch_shapes=[V((4, 128, 1024), BF), V((4, 8, 128, 1024), BF), V((32, 4, 128, 128), F32), V((256, 128, 128), BF),
                        V((256, 128, 128), F32), V((4, 2, 128, 128), F32), V((128, 1024), BF), V((128, 1024), BF),
                        V((1024, 1024), BF), V((1024, 1024), BF),
                        V((128, 1024), BF), V((4, 128, 1024), BF), V((2, 64, 1024), BF), D((32,)), D((8,)), D((32,)),
                        D((5,)), D((3,)), D((3,)), D((4,)), D((4,)), D((4,)), D((4,)), D((4,)), D((4,)), D((2,)), D((2,)),
                        D((2, 4)), D((2, 4)), D((4,)), D((4,)), D((4, 4)), D((4, 4))],
        compiler_params=pltpu.CompilerParams(vmem_limit_bytes=60 << 20, collective_id=2, has_side_effects=True),
        name="panel",
    )(order, panel, hi, lo, low, front, arrived)


def lead_kernel(idx_ref, front_ref, code_ref, child_ref, lead_ref, codes_ref, sent_ref, own_ref, tile_ref, pack_ref, tsem, psem, lsem, zs, zr, zls, zlr, xs, xr, ys, yr, as_, ar, bs, br, cas, car, cbs, cbr):
    sub, row, col = lax.axis_index("sub"), lax.axis_index("row"), lax.axis_index("col")
    par = lax.rem(sub, 2)
    mate = sub + 1 - 2 * par
    line = 4 * par + row
    need = (par == 1) | (col <= row)

    def remote(src, dst, send, recv, **where):
        return pltpu.make_async_remote_copy(src, dst, send, recv, device_id=where, device_id_type=MESH)

    barrier = pltpu.get_barrier_semaphore()
    for d in range(1, 8):
        pl.semaphore_signal(barrier, inc=1, device_id={"sub": lax.rem(sub + d, 8)}, device_id_type=MESH)
    for d in range(1, 4):
        pl.semaphore_signal(barrier, inc=1, device_id={"row": lax.rem(row + d, 4)}, device_id_type=MESH)
        pl.semaphore_signal(barrier, inc=1, device_id={"col": lax.rem(col + d, 4)}, device_id_type=MESH)

    mine = [pltpu.make_async_copy(front_ref.at[0, 0, :, s, 0, :], own_ref.at[s], lsem.at[s]) for s in range(2)]
    code = pltpu.make_async_copy(code_ref, codes_ref.at[col, row, sub], lsem.at[2])
    tiles = [pltpu.make_async_copy(child_ref.at[pl.ds(32 * g, 32)], tile_ref.at[pl.ds(32 * g, 32)], tsem.at[g]) for g in range(4)]
    packs = [pltpu.make_async_copy(pack_ref.at[pl.ds(16 * g, 16)], sent_ref.at[pl.ds(16 * g, 16)], psem.at[g]) for g in range(8)]

    def pack(g):
        def go(j, c):
            for u in range(2):
                pack_ref[16 * g + j, u] = tile_ref[idx_ref[u, 16 * g + j]]
            return c
        lax.fori_loop(0, 16, go, 0)
        packs[g].start()

    code.start()
    mine[0].start()
    mine[1].start()
    for copy in tiles:
        copy.start()
    mine[0].wait()
    mine[1].wait()
    keep = [pltpu.make_async_copy(own_ref.at[s], lead_ref.at[line, 4 * s + col], lsem.at[3 + s]) for s in range(2)]

    @pl.when(sub < 2)
    def _():
        keep[0].start()
        keep[1].start()
    pl.semaphore_wait(barrier, 13)

    def zcode(d):
        return remote(code_ref, codes_ref.at[col, row, sub], zs.at[d - 1], zr.at[d - 1], sub=lax.rem(sub + d, 8))
    def zcode_in(d):
        return remote(code_ref, codes_ref.at[col, row, lax.rem(sub + 8 - d, 8)], zs.at[d - 1], zr.at[d - 1], sub=lax.rem(sub + d, 8))
    need1 = (par == 1) & (col <= row)

    @pl.when(sub < 2)
    def _():
        for d in (1, 3, 2):
            @pl.when(need)
            def _():
                remote(own_ref.at[0], lead_ref.at[line, col], zls.at[d - 1, 0], zlr.at[0], sub=sub + 2 * d).start()
            @pl.when(need1)
            def _():
                remote(own_ref.at[1], lead_ref.at[line, 4 + col], zls.at[d - 1, 1], zlr.at[1], sub=sub + 2 * d).start()
    for d in range(1, 8):
        zcode(d).start()
    for copy in tiles:
        copy.wait()
    for g in range(4):
        pack(g)

    @pl.when(sub < 2)
    def _():
        keep[0].wait()
        keep[1].wait()

    @pl.when(sub >= 2)
    def _():
        @pl.when(need)
        def _():
            remote(own_ref.at[0], lead_ref.at[line, col], zls.at[0, 0], zlr.at[0], sub=par).wait_recv()
        @pl.when(need1)
        def _():
            remote(own_ref.at[1], lead_ref.at[line, 4 + col], zls.at[0, 1], zlr.at[1], sub=par).wait_recv()

    def ax(d, r):
        return remote(lead_ref.at[4 + r, col], lead_ref.at[4 + r, col], as_.at[0, d - 1], ar.at[0, d - 1], row=lax.rem(row + d, 4))
    def ay(d, c):
        return remote(lead_ref.at[pl.ds(4, 4), c], lead_ref.at[pl.ds(4, 4), c], as_.at[1, d - 1], ar.at[1, d - 1], col=lax.rem(col + d, 4))
    def by(d, c):
        at = lead_ref.at[line, 4 * par + c]
        return remote(at, at, bs.at[d - 1, 4], br.at[d - 1, 4], col=lax.rem(col + d, 4))
    def bx(d, r, c):
        at = lead_ref.at[4 * par + r, 4 * par + c]
        return remote(at, at, bs.at[d - 1, c], br.at[d - 1, c], row=lax.rem(row + d, 4))
    for d in (1, 3, 2):
        @pl.when(par == 1)
        def _():
            ax(d, row).start()
        @pl.when(col <= row)
        def _():
            by(d, col).start()
    code.wait()
    for d in range(1, 8):
        zcode_in(d).wait_recv()
    def cx(d, r):
        return remote(codes_ref.at[col, r], codes_ref.at[col, r], xs.at[d - 1], xr.at[d - 1], row=lax.rem(row + d, 4))
    def cy(d, c):
        return remote(codes_ref.at[c], codes_ref.at[c], ys.at[d - 1], yr.at[d - 1], col=lax.rem(col + d, 4))
    for d in range(1, 4):
        cx(d, row).start()
    for d in (1, 3, 2):
        @pl.when(par == 1)
        def _():
            ax(d, lax.rem(row + 4 - d, 4)).wait_recv()
        @pl.when(lax.rem(col + 4 - d, 4) <= row)
        def _():
            by(d, lax.rem(col + 4 - d, 4)).wait_recv()
    for d in (1, 3, 2):
        @pl.when(par == 1)
        def _():
            ay(d, col).start()
        for c in range(4):
            @pl.when(c <= row)
            def _():
                bx(d, row, c).start()

    def swap_a(c):
        at = lead_ref.at[pl.ds(4, 4), c]
        return remote(at, at, cas.at[c], car.at[c], sub=mate)
    def swap_b(p, r, c):
        at = lead_ref.at[4 * p + r, 4 * p + c]
        return remote(at, at, cbs.at[r, c], cbr.at[r, c], sub=mate)
    def hand(r, c):
        @pl.when(par == 1)
        def _():
            swap_a(c).start()
        for u in range(4):
            @pl.when(u <= r)
            def _():
                swap_b(par, r, u).start()
    hand(row, col)
    for g in range(4, 8):
        pack(g)
    for d in range(1, 4):
        cx(d, lax.rem(row + 4 - d, 4)).wait_recv()
    for d in range(1, 4):
        cy(d, col).start()
    for d in (1, 3, 2):
        r = lax.rem(row + 4 - d, 4)
        @pl.when(par == 1)
        def _():
            ay(d, lax.rem(col + 4 - d, 4)).wait_recv()
        for c in range(4):
            @pl.when(c <= r)
            def _():
                bx(d, r, c).wait_recv()
        hand(r, lax.rem(col + 4 - d, 4))
    @pl.when(par == 0)
    def _():
        for c in range(4):
            swap_a(c).wait_recv()
    for r in range(4):
        for c in range(r + 1):
            swap_b(1 - par, r, c).wait_recv()
    for d in range(1, 4):
        cy(d, lax.rem(col + 4 - d, 4)).wait_recv()

    for d in range(1, 8):
        zcode(d).wait_send()
    @pl.when(sub < 2)
    def _():
        for d in (1, 2, 3):
            @pl.when(need)
            def _():
                remote(own_ref.at[0], lead_ref.at[line, col], zls.at[d - 1, 0], zlr.at[0], sub=sub + 2 * d).wait_send()
            @pl.when(need1)
            def _():
                remote(own_ref.at[1], lead_ref.at[line, 4 + col], zls.at[d - 1, 1], zlr.at[1], sub=sub + 2 * d).wait_send()
    for d in range(1, 4):
        cx(d, row).wait_send()
        cy(d, col).wait_send()
        @pl.when(par == 1)
        def _():
            ax(d, row).wait_send()
            ay(d, col).wait_send()
        @pl.when(col <= row)
        def _():
            by(d, col).wait_send()
        for c in range(4):
            @pl.when(c <= row)
            def _():
                bx(d, row, c).wait_send()
    @pl.when(par == 1)
    def _():
        for c in range(4):
            swap_a(c).wait_send()
    for r in range(4):
        for c in range(r + 1):
            swap_b(par, r, c).wait_send()
    for copy in packs:
        copy.wait()


def lead_gather(idx, front, code, child):
    D = pltpu.SemaphoreType.DMA
    return pl.pallas_call(
        lead_kernel,
        out_shape=(jax.ShapeDtypeStruct((8, 8, 128, 128), F32), jax.ShapeDtypeStruct((4, 4, 8, 1, 128), jnp.int32),
                   jax.ShapeDtypeStruct((128, 2, 128, 128), BF)),
        in_specs=[pl.BlockSpec(memory_space=pltpu.SMEM), pl.BlockSpec(memory_space=pltpu.HBM), pl.BlockSpec(memory_space=V),
                  pl.BlockSpec(memory_space=pltpu.HBM)],
        out_specs=(pl.BlockSpec(memory_space=V), pl.BlockSpec(memory_space=V), pl.BlockSpec(memory_space=pltpu.HBM)),
        scratch_shapes=[V((2, 128, 128), F32), V((128, 128, 128), BF), V((128, 2, 128, 128), BF), D((4,)), D((8,)), D((5,)), D((7,)), D((7,)), D((3, 2)), D((2,)), D((3,)), D((3,)), D((3,)), D((3,)),
                        D((2, 3)), D((2, 3)), D((3, 5)), D((3, 5)), D((4,)), D((4,)), D((4, 4)), D((4, 4))],
        compiler_params=pltpu.CompilerParams(vmem_limit_bytes=60 << 20, collective_id=1, has_side_effects=True),
        name="lead",
    )(idx, front, code, child)


def landings(codes, me):
    codes = codes[:, :, :, 0, :].transpose(2, 1, 0, 3).reshape(128, 128)
    place = lax.broadcasted_iota(jnp.int32, (128, 128), 1) * 128 + codes % 128
    match = codes // 128 == me
    first = jnp.min(jnp.where(match, place, 1 << 20), 1)
    last = jnp.max(jnp.where(match, place, -1), 1)
    one = jnp.where(last >= 0, first % 128, -1)
    two = jnp.where(last > first, last % 128, -1)
    return jnp.stack([one, two], 1).reshape(256)


def local(front, child_tiles, tile_owner, tile_slot):
    sub = lax.axis_index("sub")
    row = lax.axis_index("row")
    col = lax.axis_index("col")
    group = sub * 4 + row
    idx, code = index(tile_owner.reshape(1, 128), tile_slot.reshape(1, 128))
    lead, codes, outgoing = lead_gather(idx, front, code, child_tiles)
    arrived = lax.all_to_all(outgoing, ("sub", "row", "col"), split_axis=0, concat_axis=0, tiled=True)
    arrived = arrived.reshape(256, 128, 128)
    factor, hi, lo = chol(lead)
    landing = landings(codes, group * 4 + col)
    order = plan(landing)
    panel = head(landing, order, front, arrived)
    out, panel_out = panel_exchange(order, panel, hi, lo, factor, front, arrived)
    return out, panel_out.reshape(4, 1, 128, 2, 1, 128)


def solution(mesh):
    return jax.shard_map(
        local,
        mesh=mesh,
        in_specs=(
            P(None, ("sub", "row"), None, None, "col", None),
            P(("sub", "row", "col"), None, None),
            P(("sub", "row", "col"), None),
            P(("sub", "row", "col")),
        ),
        out_specs=(
            P(None, ("sub", "row"), None, None, "col", None),
            P(None, ("sub", "row"), None, None, "col", None),
        ),
        check_vma=False,
    )
```

```python
import jax
import jax.numpy as jnp
from jax import lax
from jax.experimental import pallas as pl
from jax.experimental.pallas import tpu as pltpu
from jax.sharding import PartitionSpec as P

F32, BF = jnp.float32, jnp.bfloat16
HI = lax.Precision.HIGHEST
V = pltpu.VMEM
ANY = pl.ANY
MESH = pl.DeviceIdType.MESH


def nt(a, b):
    return lax.dot_general(a, b, (((1,), (1,)), ((), ())), precision=HI, preferred_element_type=F32)


def nn(a, b):
    return lax.dot_general(a, b, (((1,), (0,)), ((), ())), precision=HI, preferred_element_type=F32)


def split3(x):
    h = x.astype(BF).astype(F32)
    r = x - h
    m = r.astype(BF).astype(F32)
    return h, m, r - m


def diag_factor(d_ref, u_ref, x_ref, cb_ref, r_ref):
    def body(b, carry):
        r0 = pl.multiple_of(b * 8, 8)
        block = d_ref[pl.ds(r0, 8), 0:128]
        rolled = pltpu.roll(block, (128 - r0) % 128, 1)
        for j in range(8):
            cb_ref[j] = jnp.broadcast_to(rolled[:, j:j + 1], (8, 128))
        r_ref[:, 0:128] = block
        r_ref[:, 128:256] = d_ref[pl.ds(r0, 8), 128:256]
        e = {}
        for i in range(8):
            for j in range(i + 1):
                e[i, j] = cb_ref[j, i:i + 1, :]
        rows = []
        for i in range(8):
            rows.append([r_ref[i:i + 1, 0:128], r_ref[i:i + 1, 128:256]])
        for j in range(8):
            inv = lax.rsqrt(e[j, j])
            low = {}
            for i in range(j + 1, 8):
                low[i] = e[i, j] * inv
            for h in range(2):
                rows[j][h] = rows[j][h] * inv
            for i in range(j + 1, 8):
                for m in range(j + 1, i + 1):
                    e[i, m] = e[i, m] - low[i] * low[m]
                for h in range(2):
                    rows[i][h] = rows[i][h] - low[i] * rows[j][h]
        for i in range(8):
            r_ref[i:i + 1, 0:128] = rows[i][0]
            r_ref[i:i + 1, 128:256] = rows[i][1]
        r = r_ref[...]
        u_ref[pl.ds(r0, 8), :] = r[:, 0:128]
        x_ref[pl.ds(r0, 8), :] = r[:, 128:256]
        h, m, l = split3(r)
        left = jnp.concatenate([h, h, m, h, l, m], 0)[:, 0:128].astype(BF)
        right = jnp.concatenate([h, m, h, l, h, m], 0).astype(BF)
        d_ref[...] = d_ref[...] - lax.dot_general(left, right, (((0,), (0,)), ((), ())), preferred_element_type=F32)
        return carry
    lax.fori_loop(0, 16, body, 0)


def chol_kernel(lead_ref, l_ref, hi_ref, lo_ref, s_ref, w_ref, d_ref, u_ref, x_ref, cb_ref, r_ref):
    row = lax.broadcasted_iota(jnp.int32, (128, 128), 0)
    col = lax.broadcasted_iota(jnp.int32, (128, 128), 1)
    eye = (row == col).astype(F32)
    n = 8
    for i in range(n):
        for j in range(i + 1):
            t = lead_ref[i, j]
            if i == j:
                t = jnp.where(row >= col, t, t.T)
            s_ref[i * 128:(i + 1) * 128, j * 128:(j + 1) * 128] = t
    w_ref[...] = jnp.zeros_like(w_ref)
    l_ref[...] = jnp.zeros_like(l_ref)
    for k in range(n):
        a, b = k * 128, (k + 1) * 128
        d_ref[:, 0:128] = s_ref[a:b, a:b]
        d_ref[:, 128:256] = eye
        diag_factor(d_ref, u_ref, x_ref, cb_ref, r_ref)
        x = x_ref[...]
        l_ref[a:b, a:b] = jnp.where(row >= col, u_ref[...].T, 0.0).astype(BF)
        if k > 0:
            w_ref[a:b, 0:a] = nn(x, w_ref[a:b, 0:a])
        w_ref[a:b, a:b] = x
        if k < n - 1:
            p = nt(s_ref[b:, a:b], x)
            s_ref[b:, a:b] = p
            l_ref[b:, a:b] = p.astype(BF)
            for j in range(k + 1, n):
                c, d = j * 128, (j + 1) * 128
                s_ref[c:, c:d] = s_ref[c:, c:d] - nt(s_ref[c:, a:b], s_ref[c:d, a:b])
            w_ref[b:, 0:b] = w_ref[b:, 0:b] - nn(p, w_ref[a:b, 0:b])
    for k in range(n):
        a, b = k * 128, (k + 1) * 128
        y = w_ref[a:b, :]
        h = y.astype(BF)
        hi_ref[a:b, :] = h
        lo_ref[a:b, :] = (y - h.astype(F32)).astype(BF)


def chol(lead):
    return pl.pallas_call(
        chol_kernel,
        out_shape=[jax.ShapeDtypeStruct((1024, 1024), BF)] * 3,
        in_specs=[pl.BlockSpec(memory_space=V)],
        out_specs=[pl.BlockSpec(memory_space=V)] * 3,
        scratch_shapes=[V((1024, 1024), F32), V((1024, 1024), F32), V((128, 256), F32), V((128, 128), F32),
                        V((128, 128), F32), V((8, 8, 128), F32), V((8, 256), F32)],
        compiler_params=pltpu.CompilerParams(vmem_limit_bytes=30 << 20),
        name="chol",
    )(lead)


def index_kernel(owner_ref, slot_ref, idx_ref, code_ref):
    owner = owner_ref[...]
    code_ref[...] = owner * 128 + slot_ref[...]
    wide = jnp.broadcast_to(owner.astype(F32), (128, 128)).T
    k = lax.broadcasted_iota(jnp.int32, (128, 128), 0).astype(F32)
    match = wide == lax.broadcasted_iota(jnp.int32, (128, 128), 1).astype(F32)
    first = jnp.min(jnp.where(match, k, 127.0), 0, keepdims=True)
    last = jnp.max(jnp.where(match, k, 0.0), 0, keepdims=True)
    idx_ref[0:1, :] = first.astype(jnp.int32)
    idx_ref[1:2, :] = last.astype(jnp.int32)


def index(owner, slot):
    return pl.pallas_call(
        index_kernel,
        out_shape=(jax.ShapeDtypeStruct((2, 128), jnp.int32), jax.ShapeDtypeStruct((1, 128), jnp.int32)),
        in_specs=[pl.BlockSpec(memory_space=V)] * 2,
        out_specs=[pl.BlockSpec(memory_space=V)] * 2,
        name="index",
    )(owner, slot)


def plan_kernel(col_ref, row_ref, out_ref):
    def at(shape, axis):
        return lax.broadcasted_iota(jnp.int32, shape, axis).astype(F32)
    square = (256, 256)
    own = jnp.broadcast_to(col_ref[...], square).astype(F32)
    other = jnp.broadcast_to(row_ref[...], square).astype(F32)
    k, j = at(square, 0), at(square, 1)
    one = jnp.ones(square, F32)
    zero = jnp.zeros(square, F32)
    key, other_key = jnp.where(own < 0, 1000.0, own), jnp.where(other < 0, 1000.0, other)
    before = (other_key < key) | ((other_key == key) & (j < k))
    rank = jnp.sum(jnp.where(before, one, zero), 1, keepdims=True)
    here = jnp.broadcast_to(rank, square) == j
    order = jnp.sum(jnp.where(here, k, zero), 0, keepdims=True)
    slots = jnp.sum(jnp.where(here, key, zero), 0, keepdims=True)
    lane = at((1, 256), 1)
    same = jnp.where((slots == pltpu.roll(slots, 1, 1)) & (lane > 0) & (slots < 1000.0), 1.0, 0.0)
    half = (256, 128)
    slot = at(half, 1)
    own_key = key[:, 0:128]
    last = jnp.sum(jnp.where(own_key <= slot, 1.0, 0.0), 0, keepdims=True) - 1.0
    some = jnp.max(jnp.where(own_key == slot, 1.0, 0.0), 0, keepdims=True)

    def panel_column(x):
        return (x >= 0) & (x - 32.0 * jnp.floor(x * (1 / 32)) < 2.0)
    hit, other_hit = panel_column(own), panel_column(other)
    turn = jnp.sum(jnp.where(other_hit & (j < k), one, zero), 1, keepdims=True)
    listed = jnp.sum(jnp.where(hit & (jnp.broadcast_to(turn, square) == j), k, zero), 0, keepdims=True)
    count = jnp.sum(jnp.where(hit, one, zero), 0, keepdims=True)
    rows = [order, same, jnp.concatenate([jnp.maximum(last, 0.0), some], 1), listed, count]
    for r in range(5):
        out_ref[r:r + 1, :] = rows[r].astype(jnp.int32)


def plan(land):
    return pl.pallas_call(
        plan_kernel,
        out_shape=jax.ShapeDtypeStruct((5, 256), jnp.int32),
        in_specs=[pl.BlockSpec(memory_space=V)] * 2,
        out_specs=pl.BlockSpec(memory_space=V),
        name="plan",
    )(land.reshape(256, 1), land.reshape(1, 256))


def head_kernel(land_ref, list_ref, front_ref, arr_ref, out_ref, buf_ref, acc_ref, fsem, asem):
    count = list_ref[4, 0]
    def arrive(n, i):
        return pltpu.make_async_copy(arr_ref.at[list_ref[3, n]], buf_ref.at[i], asem.at[i])
    def fetch(s):
        return pltpu.make_async_copy(front_ref.at[:, 0, :, s, 0, :], acc_ref.at[s], fsem.at[s])
    for s in range(2):
        fetch(s).start()
    def batch(b, carry):
        def begin(i, c):
            arrive(b * 16 + i, i).start()
            return c
        def end(i, c):
            n = b * 16 + i
            slot = land_ref[list_ref[3, n]]
            s, q = slot % 32, slot // 32
            arrive(n, i).wait()
            acc_ref[s, q] = acc_ref[s, q] + buf_ref[i].astype(F32)
            return c
        here = lax.min(count - b * 16, 16)
        lax.fori_loop(0, here, begin, 0)
        @pl.when(b == 0)
        def _():
            for s in range(2):
                fetch(s).wait()
        lax.fori_loop(0, here, end, 0)
        return carry
    lax.fori_loop(0, lax.max((count + 15) // 16, 1), batch, 0)
    out_ref[...] = acc_ref[...]


def head(land, listed, front, arrived):
    return pl.pallas_call(
        head_kernel,
        out_shape=jax.ShapeDtypeStruct((2, 4, 128, 128), F32),
        grid_spec=pltpu.PrefetchScalarGridSpec(
            num_scalar_prefetch=2, grid=(1,),
            in_specs=[pl.BlockSpec(memory_space=ANY)] * 2,
            out_specs=pl.BlockSpec((2, 4, 128, 128), lambda g, a, b: (0, 0, 0, 0)),
            scratch_shapes=[V((16, 128, 128), BF), V((2, 4, 128, 128), F32),
                            pltpu.SemaphoreType.DMA((2,)), pltpu.SemaphoreType.DMA((16,))]),
        compiler_params=pltpu.CompilerParams(vmem_limit_bytes=60 << 20),
        name="head",
    )(land, listed, front, arrived)


def panel_kernel(order_ref, panel_ref, hi_hbm, lo_hbm, low_hbm, front_ref, arr_ref, out_ref, pout_ref,
                 brow_ref, bcol_ref, acc_ref, buf_ref, run_ref, arow, ah, al, hi, lo, low, xb, rl, fsem, asem, osem, lsem, ps, pr, xs, xr, ws, wr, ys, yr, rs, rr, zs, zr, fs, fr, ms, mr):
    sub, row, col = lax.axis_index("sub"), lax.axis_index("row"), lax.axis_index("col")
    group = 4 * sub + row
    mate = sub + 1 - 2 * lax.rem(sub, 2)

    def n4(x, d):
        return lax.rem(x + 4 + d, 4)

    def n8(x, d):
        return lax.rem(x + 8 + d, 8)

    def remote(src, dst, send, recv, **where):
        return pltpu.make_async_remote_copy(src, dst, send, recv, device_id=where, device_id_type=MESH)

    loads = [pltpu.make_async_copy(hi_hbm, hi, lsem.at[0]), pltpu.make_async_copy(lo_hbm, lo, lsem.at[1]),
             pltpu.make_async_copy(low_hbm.at[pl.ds(pl.multiple_of(lax.min(group, 7) * 128, 128), 128)], low, lsem.at[2]),
             pltpu.make_async_copy(panel_ref.at[:, col], arow.at[col], lsem.at[3])]
    barrier = pltpu.get_barrier_semaphore()
    for d in (1, 3):
        pl.semaphore_signal(barrier, inc=1, device_id={"row": n4(row, d)}, device_id_type=MESH)
        pl.semaphore_signal(barrier, inc=1, device_id={"sub": n8(sub, 2 * d if d == 1 else -2)}, device_id_type=MESH)
    for d in (1, 2, 3):
        pl.semaphore_signal(barrier, inc=1, device_id={"col": n4(col, d)}, device_id_type=MESH)
    pl.semaphore_signal(barrier, inc=1, device_id={"sub": mate}, device_id_type=MESH)
    for copy in loads:
        copy.start()
    pl.semaphore_wait(barrier, 8)

    def fetch(s):
        return pltpu.make_async_copy(front_ref.at[:, 0, :, s, 0, :], acc_ref.at[s], fsem.at[s])
    def arrived(c):
        return pltpu.make_async_copy(arr_ref.at[pl.ds(c * 32, 32)], buf_ref.at[pl.ds(c * 32, 32)], asem.at[c])
    def put(s):
        return pltpu.make_async_copy(acc_ref.at[s], out_ref.at[:, 0, :, s, 0, :], osem.at[s])
    def early(s):
        return pltpu.make_async_copy(panel_ref.at[s], out_ref.at[:, 0, :, s, 0, :], osem.at[s])
    def each(low, high, f):
        def go(s, c):
            f(s)
            return c
        lax.fori_loop(low, high, go, 0)

    def take(d):
        return remote(panel_ref.at[:, n4(col, d)], arow.at[col], ps.at[d - 1], pr.at[d - 1], col=n4(col, d))
    def taken(d):
        return remote(panel_ref.at[:, n4(col, d)], arow.at[n4(col, -d)], ps.at[d - 1], pr.at[d - 1], col=n4(col, d))
    for d in (1, 3, 2):
        take(d).start()
    each(0, 8, lambda c: arrived(c).start())
    each(2, 32, lambda s: fetch(s).start())
    loads[3].wait()
    for d in (1, 3, 2):
        taken(d).wait_recv()
    for s in range(2):
        for t in range(4):
            a = arow[t, s]
            h = a.astype(BF)
            at = (4 * s + t) * 128
            ah[:, at:at + 128] = h
            al[:, at:at + 128] = (a - h.astype(F32)).astype(BF)
    for copy in loads[:3]:
        copy.wait()
    top = (group < 8) & (col == 0)

    def mm(x, y):
        return lax.dot_general(x, y, (((1,), (1,)), ((), ())), preferred_element_type=F32)
    for b in range(4):
        w = 256 * (b + 1)
        rows = pl.ds(256 * b, 256)
        y = mm(ah[:, 0:w], hi[rows, 0:w]) + (mm(ah[:, 0:w], lo[rows, 0:w]) + mm(al[:, 0:w], hi[rows, 0:w]))
        y = jnp.where(top, low[:, 256 * b:w], y.astype(BF))
        xb[row, :, 256 * b:w] = y
        brow_ref[col, :, 256 * b:w] = y

    half = [pl.ds(0, 64), pl.ds(64, 64)]
    step = [1, -1]
    def xsend(i):
        return remote(xb.at[row], xb.at[row], xs.at[i], xr.at[i], row=n4(row, step[i]))
    def xrecv(i):
        at = xb.at[n4(row, -step[i])]
        return remote(at, at, xs.at[i], xr.at[i], row=n4(row, step[i]))
    def xforward(i, r):
        at = xb.at[r, half[i]]
        return remote(at, at, xs.at[2 + i], xr.at[2 + i], row=n4(row, step[i]))
    def wsend(i):
        return remote(brow_ref.at[col], brow_ref.at[col], ws.at[i], wr.at[i], col=n4(col, step[i]))
    def wrecv(i):
        at = brow_ref.at[n4(col, -step[i])]
        return remote(at, at, ws.at[i], wr.at[i], col=n4(col, step[i]))
    def wforward(i, c):
        at = brow_ref.at[c, half[i]]
        return remote(at, at, ws.at[2 + i], wr.at[2 + i], col=n4(col, step[i]))

    def ynear(i):
        return remote(xb.at[n4(col, step[i])], bcol_ref.at[col, sub], ys.at[i], yr.at[i], col=n4(col, step[i]))
    def ynear_in(i):
        return remote(xb.at[0], bcol_ref.at[n4(col, -step[i]), sub], ys.at[i], yr.at[i], col=n4(col, step[i]))
    def yfar(i):
        return remote(xb.at[n4(col, 2), half[i]], rl.at[i], rs.at[i], rr.at[i], col=n4(col, step[i]))
    def yrelay(i):
        return remote(rl.at[i], bcol_ref.at[n4(col, -step[i]), sub, half[i]], ys.at[2 + i], yr.at[2 + i], col=n4(col, step[i]))
    def yfar_in(i):
        return remote(rl.at[i], bcol_ref.at[n4(col, 2), sub, half[i]], ys.at[2 + i], yr.at[2 + i], col=n4(col, step[i]))
    home = pltpu.make_async_copy(xb.at[col], bcol_ref.at[col, sub], lsem.at[4])

    def ysend(c):
        d = n4(c, -col)
        @pl.when(d == 0)
        def _():
            home.start()
        for i in range(2):
            @pl.when(d == (1, 3)[i])
            def _():
                ynear(i).start()
        @pl.when(d == 2)
        def _():
            yfar(0).start()
            yfar(1).start()

    def own(e, i):
        at = bcol_ref.at[n4(col, e), sub]
        return remote(at if e else xb.at[col], at, zs.at[i, e], zr.at[i, e], sub=n8(sub, 2 * step[i]))
    def arrive(e, i):
        at = bcol_ref.at[n4(col, e), n8(sub, -2 * step[i])]
        return remote(at, at, zs.at[i, e], zr.at[i, e], sub=n8(sub, 2 * step[i]))
    side = [0, 0, 1, 1]
    def onward(e, i, z):
        at = bcol_ref.at[n4(col, e), n8(sub, z)]
        return remote(at, at, fs.at[e], fr.at[e], sub=n8(sub, 2 * step[i]))
    def swap(e, k, z):
        at = bcol_ref.at[n4(col, e), n8(sub, z)]
        return remote(at if k or e else xb.at[col], at, ms.at[k, e], mr.at[k, e], sub=mate)
    def swapped(e, k, z):
        at = bcol_ref.at[n4(col, e), n8(mate, z)]
        return remote(at, at, ms.at[k, e], mr.at[k, e], sub=mate)

    def launch(e):
        own(e, 0).start()
        own(e, 1).start()
        swap(e, 0, 0).start()
    apart = n4(col, -row)

    def gather(c):
        def go(k, total):
            i = c * 32 + k
            total = buf_ref[order_ref[0, i]].astype(F32) + order_ref[1, i].astype(F32) * total
            run_ref[i] = total
            return total
        first = jnp.zeros((128, 128), F32) if c == 0 else run_ref[c * 32 - 1]
        lax.fori_loop(0, 32, go, first)

    def settle(s):
        for q in range(4):
            slot = q * 32 + s
            acc_ref[s, q] = acc_ref[s, q] + order_ref[2, 128 + slot].astype(F32) * run_ref[order_ref[2, slot]]

    keep = jnp.where(group < 8, 0.0, 1.0)
    pair0 = sub - lax.rem(sub, 2)

    def update(e, dz):
        q, z = n4(col, e), n8(pair0, dz)
        s = q * 8 + z
        @pl.when(s >= 2)
        def _():
            settle(s)
            settle(s + 1)
            y = mm(brow_ref[...].reshape(512, 1024), bcol_ref[q, pl.ds(z, 2)].reshape(256, 1024))
            for u in range(2):
                t = y[:, u * 128:(u + 1) * 128].reshape(4, 128, 128)
                acc_ref[s + u, 0] = acc_ref[s + u, 0] - keep * t[0]
                acc_ref[s + u, 1:4] = acc_ref[s + u, 1:4] - t[1:4]
                put(s + u).start()

    def near():
        ynear_in(1).wait_recv()
        launch(1)
        ynear_in(0).wait_recv()
        launch(3)

    def reach(d):
        ysend(n4(row, d))
        @pl.when(apart == d)
        def _():
            launch(0)

    for i in range(2):
        xsend(i).start()
    for i in range(2):
        wsend(i).start()
    reach(0)
    early(0).start()
    early(1).start()
    each(0, 8, lambda c: arrived(c).wait())
    for c in range(5):
        gather(c)
    for i in range(2):
        xrecv(i).wait_recv()
        xforward(i, n4(row, -step[i])).start()
        reach(3 if i == 0 else 1)
    for i in range(2):
        wrecv(i).wait_recv()
        wforward(i, n4(col, -step[i])).start()
    @pl.when(apart == 0)
    def _():
        near()
    for c in range(5, 8):
        gather(c)
    for i in range(2):
        xforward(i, n4(row, 2)).wait_recv()
    reach(2)
    each(2, 32, lambda s: fetch(s).wait())
    for i in range(2):
        yfar(i).wait_recv()
        yrelay(i).start()
    @pl.when(apart != 0)
    def _():
        near()
    yfar_in(0).wait_recv()
    yfar_in(1).wait_recv()
    launch(2)
    for i in range(2):
        wforward(i, n4(col, 2)).wait_recv()
    home.wait()

    def gray(k):
        return k + jnp.where(k == 2, 1, 0) - jnp.where(k == 3, 1, 0)

    def product(e, k, z):
        swapped(e, k, z).wait_recv()
        update(e, z)

    def pass_on(k, carry):
        e = gray(k)
        for i in range(2):
            arrive(e, i).wait_recv()
            @pl.when((e < 2) if i == 0 else (e >= 2))
            def _():
                onward(e, i, -2 * step[i]).start()
            swap(e, 1 + i, -2 * step[i]).start()

        def three(j, c):
            @pl.when((j == 0) | (k > 0))
            def _():
                product(jnp.where(j == 0, e, gray(lax.max(k - 1, 0))), j, jnp.where(j == 0, 0, 4 * j - 6))
            return c
        lax.fori_loop(0, 3, three, 0)
        return carry
    lax.fori_loop(0, 4, pass_on, 0)

    for q in range(4):
        pair = [brow_ref[q, :, pl.ds(pl.multiple_of((4 * s + col) * 128, 128), 128)] for s in range(2)]
        pout_ref[q] = jnp.stack([x.astype(F32) for x in pair], 1).astype(BF)

    def last(k, carry):
        @pl.when(k < 4)
        def _():
            e = gray(k)
            onward(e, 0, 4).wait_recv()
            swap(e, 3, 4).start()

        def two(j, c):
            @pl.when((j == 0) | (k == 0))
            def _():
                product(jnp.where(k == 0, 2, gray(lax.max(k - 1, 0))), jnp.where(k == 0, 1 + j, 3), jnp.where(k == 0, 4 * j - 2, 4))
            return c
        lax.fori_loop(0, 2, two, 0)
        return carry
    lax.fori_loop(0, 5, last, 0)
    early(0).wait()
    early(1).wait()
    each(2, 32, lambda s: put(s).wait())

    for d in (1, 2, 3):
        take(d).wait_send()
    for i in range(2):
        xsend(i).wait_send()
        wsend(i).wait_send()
        xforward(i, n4(row, -step[i])).wait_send()
        wforward(i, n4(col, -step[i])).wait_send()
        ynear(i).wait_send()
        yfar(i).wait_send()
        yrelay(i).wait_send()
    for e in range(4):
        own(e, 0).wait_send()
        own(e, 1).wait_send()
        onward(e, side[e], -2 * step[side[e]]).wait_send()
        swap(e, 0, 0).wait_send()
        swap(e, 1, -2).wait_send()
        swap(e, 2, 2).wait_send()
        swap(e, 3, 4).wait_send()


def panel_exchange(order, panel, hi, lo, low, front, arrived):
    D = pltpu.SemaphoreType.DMA
    H = pltpu.HBM
    return pl.pallas_call(
        panel_kernel,
        out_shape=(jax.ShapeDtypeStruct((4, 1, 128, 32, 1, 128), F32), jax.ShapeDtypeStruct((4, 128, 2, 128), BF)),
        in_specs=[pl.BlockSpec(memory_space=pltpu.SMEM), pl.BlockSpec(memory_space=V)] + [pl.BlockSpec(memory_space=H)] * 5,
        out_specs=(pl.BlockSpec(memory_space=H), pl.BlockSpec(memory_space=V)),
        scratch_shapes=[V((4, 128, 1024), BF), V((4, 8, 128, 1024), BF), V((32, 4, 128, 128), F32), V((256, 128, 128), BF),
                        V((256, 128, 128), F32), V((4, 2, 128, 128), F32), V((128, 1024), BF), V((128, 1024), BF),
                        V((1024, 1024), BF), V((1024, 1024), BF),
                        V((128, 1024), BF), V((4, 128, 1024), BF), V((2, 64, 1024), BF), D((32,)), D((8,)), D((32,)),
                        D((5,)), D((3,)), D((3,)), D((4,)), D((4,)), D((4,)), D((4,)), D((4,)), D((4,)), D((2,)), D((2,)),
                        D((2, 4)), D((2, 4)), D((4,)), D((4,)), D((4, 4)), D((4, 4))],
        compiler_params=pltpu.CompilerParams(vmem_limit_bytes=60 << 20, collective_id=2, has_side_effects=True),
        name="panel",
    )(order, panel, hi, lo, low, front, arrived)


def lead_kernel(idx_ref, front_ref, code_ref, child_ref, lead_ref, codes_ref, sent_ref, own_ref, tile_ref, pack_ref, tsem, psem, lsem, zs, zr, zls, zlr, xs, xr, ys, yr, as_, ar, bs, br, cas, car, cbs, cbr):
    sub, row, col = lax.axis_index("sub"), lax.axis_index("row"), lax.axis_index("col")
    par = lax.rem(sub, 2)
    mate = sub + 1 - 2 * par
    line = 4 * par + row
    need = (par == 1) | (col <= row)

    def remote(src, dst, send, recv, **where):
        return pltpu.make_async_remote_copy(src, dst, send, recv, device_id=where, device_id_type=MESH)

    barrier = pltpu.get_barrier_semaphore()
    for d in range(1, 8):
        pl.semaphore_signal(barrier, inc=1, device_id={"sub": lax.rem(sub + d, 8)}, device_id_type=MESH)
    for d in range(1, 4):
        pl.semaphore_signal(barrier, inc=1, device_id={"row": lax.rem(row + d, 4)}, device_id_type=MESH)
        pl.semaphore_signal(barrier, inc=1, device_id={"col": lax.rem(col + d, 4)}, device_id_type=MESH)

    mine = [pltpu.make_async_copy(front_ref.at[0, 0, :, s, 0, :], own_ref.at[s], lsem.at[s]) for s in range(2)]
    code = pltpu.make_async_copy(code_ref, codes_ref.at[col, row, sub], lsem.at[2])
    tiles = [pltpu.make_async_copy(child_ref.at[pl.ds(32 * g, 32)], tile_ref.at[pl.ds(32 * g, 32)], tsem.at[g]) for g in range(4)]
    packs = [pltpu.make_async_copy(pack_ref.at[pl.ds(16 * g, 16)], sent_ref.at[pl.ds(16 * g, 16)], psem.at[g]) for g in range(8)]

    def pack(g):
        def go(j, c):
            for u in range(2):
                pack_ref[16 * g + j, u] = tile_ref[idx_ref[u, 16 * g + j]]
            return c
        lax.fori_loop(0, 16, go, 0)
        packs[g].start()

    code.start()
    mine[0].start()
    mine[1].start()
    for copy in tiles:
        copy.start()
    mine[0].wait()
    mine[1].wait()
    keep = [pltpu.make_async_copy(own_ref.at[s], lead_ref.at[line, 4 * s + col], lsem.at[3 + s]) for s in range(2)]

    @pl.when(sub < 2)
    def _():
        keep[0].start()
        keep[1].start()
    pl.semaphore_wait(barrier, 13)

    def zcode(d):
        return remote(code_ref, codes_ref.at[col, row, sub], zs.at[d - 1], zr.at[d - 1], sub=lax.rem(sub + d, 8))
    def zcode_in(d):
        return remote(code_ref, codes_ref.at[col, row, lax.rem(sub + 8 - d, 8)], zs.at[d - 1], zr.at[d - 1], sub=lax.rem(sub + d, 8))
    need1 = (par == 1) & (col <= row)

    @pl.when(sub < 2)
    def _():
        for d in (1, 3, 2):
            @pl.when(need)
            def _():
                remote(own_ref.at[0], lead_ref.at[line, col], zls.at[d - 1, 0], zlr.at[0], sub=sub + 2 * d).start()
            @pl.when(need1)
            def _():
                remote(own_ref.at[1], lead_ref.at[line, 4 + col], zls.at[d - 1, 1], zlr.at[1], sub=sub + 2 * d).start()
    for d in range(1, 8):
        zcode(d).start()
    for copy in tiles:
        copy.wait()
    for g in range(4):
        pack(g)

    @pl.when(sub < 2)
    def _():
        keep[0].wait()
        keep[1].wait()

    @pl.when(sub >= 2)
    def _():
        @pl.when(need)
        def _():
            remote(own_ref.at[0], lead_ref.at[line, col], zls.at[0, 0], zlr.at[0], sub=par).wait_recv()
        @pl.when(need1)
        def _():
            remote(own_ref.at[1], lead_ref.at[line, 4 + col], zls.at[0, 1], zlr.at[1], sub=par).wait_recv()

    def ax(d, r):
        return remote(lead_ref.at[4 + r, col], lead_ref.at[4 + r, col], as_.at[0, d - 1], ar.at[0, d - 1], row=lax.rem(row + d, 4))
    def ay(d, c):
        return remote(lead_ref.at[pl.ds(4, 4), c], lead_ref.at[pl.ds(4, 4), c], as_.at[1, d - 1], ar.at[1, d - 1], col=lax.rem(col + d, 4))
    def by(d, c):
        at = lead_ref.at[line, 4 * par + c]
        return remote(at, at, bs.at[d - 1, 4], br.at[d - 1, 4], col=lax.rem(col + d, 4))
    def bx(d, r, c):
        at = lead_ref.at[4 * par + r, 4 * par + c]
        return remote(at, at, bs.at[d - 1, c], br.at[d - 1, c], row=lax.rem(row + d, 4))
    for d in (1, 3, 2):
        @pl.when(par == 1)
        def _():
            ax(d, row).start()
        @pl.when(col <= row)
        def _():
            by(d, col).start()
    code.wait()
    for d in range(1, 8):
        zcode_in(d).wait_recv()
    def cx(d, r):
        return remote(codes_ref.at[col, r], codes_ref.at[col, r], xs.at[d - 1], xr.at[d - 1], row=lax.rem(row + d, 4))
    def cy(d, c):
        return remote(codes_ref.at[c], codes_ref.at[c], ys.at[d - 1], yr.at[d - 1], col=lax.rem(col + d, 4))
    for d in range(1, 4):
        cx(d, row).start()
    for d in (1, 3, 2):
        @pl.when(par == 1)
        def _():
            ax(d, lax.rem(row + 4 - d, 4)).wait_recv()
        @pl.when(lax.rem(col + 4 - d, 4) <= row)
        def _():
            by(d, lax.rem(col + 4 - d, 4)).wait_recv()
    for d in (1, 3, 2):
        @pl.when(par == 1)
        def _():
            ay(d, col).start()
        for c in range(4):
            @pl.when(c <= row)
            def _():
                bx(d, row, c).start()

    def swap_a(c):
        at = lead_ref.at[pl.ds(4, 4), c]
        return remote(at, at, cas.at[c], car.at[c], sub=mate)
    def swap_b(p, r, c):
        at = lead_ref.at[4 * p + r, 4 * p + c]
        return remote(at, at, cbs.at[r, c], cbr.at[r, c], sub=mate)
    def hand(r, c):
        @pl.when(par == 1)
        def _():
            swap_a(c).start()
        for u in range(4):
            @pl.when(u <= r)
            def _():
                swap_b(par, r, u).start()
    hand(row, col)
    for g in range(4, 8):
        pack(g)
    for d in range(1, 4):
        cx(d, lax.rem(row + 4 - d, 4)).wait_recv()
    for d in range(1, 4):
        cy(d, col).start()
    for d in (1, 3, 2):
        r = lax.rem(row + 4 - d, 4)
        @pl.when(par == 1)
        def _():
            ay(d, lax.rem(col + 4 - d, 4)).wait_recv()
        for c in range(4):
            @pl.when(c <= r)
            def _():
                bx(d, r, c).wait_recv()
        hand(r, lax.rem(col + 4 - d, 4))
    @pl.when(par == 0)
    def _():
        for c in range(4):
            swap_a(c).wait_recv()
    for r in range(4):
        for c in range(r + 1):
            swap_b(1 - par, r, c).wait_recv()
    for d in range(1, 4):
        cy(d, lax.rem(col + 4 - d, 4)).wait_recv()

    for d in range(1, 8):
        zcode(d).wait_send()
    @pl.when(sub < 2)
    def _():
        for d in (1, 2, 3):
            @pl.when(need)
            def _():
                remote(own_ref.at[0], lead_ref.at[line, col], zls.at[d - 1, 0], zlr.at[0], sub=sub + 2 * d).wait_send()
            @pl.when(need1)
            def _():
                remote(own_ref.at[1], lead_ref.at[line, 4 + col], zls.at[d - 1, 1], zlr.at[1], sub=sub + 2 * d).wait_send()
    for d in range(1, 4):
        cx(d, row).wait_send()
        cy(d, col).wait_send()
        @pl.when(par == 1)
        def _():
            ax(d, row).wait_send()
            ay(d, col).wait_send()
        @pl.when(col <= row)
        def _():
            by(d, col).wait_send()
        for c in range(4):
            @pl.when(c <= row)
            def _():
                bx(d, row, c).wait_send()
    @pl.when(par == 1)
    def _():
        for c in range(4):
            swap_a(c).wait_send()
    for r in range(4):
        for c in range(r + 1):
            swap_b(par, r, c).wait_send()
    for copy in packs:
        copy.wait()


def lead_gather(idx, front, code, child):
    D = pltpu.SemaphoreType.DMA
    return pl.pallas_call(
        lead_kernel,
        out_shape=(jax.ShapeDtypeStruct((8, 8, 128, 128), F32), jax.ShapeDtypeStruct((4, 4, 8, 1, 128), jnp.int32),
                   jax.ShapeDtypeStruct((128, 2, 128, 128), BF)),
        in_specs=[pl.BlockSpec(memory_space=pltpu.SMEM), pl.BlockSpec(memory_space=pltpu.HBM), pl.BlockSpec(memory_space=V),
                  pl.BlockSpec(memory_space=pltpu.HBM)],
        out_specs=(pl.BlockSpec(memory_space=V), pl.BlockSpec(memory_space=V), pl.BlockSpec(memory_space=pltpu.HBM)),
        scratch_shapes=[V((2, 128, 128), F32), V((128, 128, 128), BF), V((128, 2, 128, 128), BF), D((4,)), D((8,)), D((5,)), D((7,)), D((7,)), D((3, 2)), D((2,)), D((3,)), D((3,)), D((3,)), D((3,)),
                        D((2, 3)), D((2, 3)), D((3, 5)), D((3, 5)), D((4,)), D((4,)), D((4, 4)), D((4, 4))],
        compiler_params=pltpu.CompilerParams(vmem_limit_bytes=60 << 20, collective_id=1, has_side_effects=True),
        name="lead",
    )(idx, front, code, child)


def landings(codes, me):
    codes = codes[:, :, :, 0, :].transpose(2, 1, 0, 3).reshape(128, 128)
    place = lax.broadcasted_iota(jnp.int32, (128, 128), 1) * 128 + codes % 128
    match = codes // 128 == me
    first = jnp.min(jnp.where(match, place, 1 << 20), 1)
    last = jnp.max(jnp.where(match, place, -1), 1)
    one = jnp.where(last >= 0, first % 128, -1)
    two = jnp.where(last > first, last % 128, -1)
    return jnp.stack([one, two], 1).reshape(256)


def local(front, child_tiles, tile_owner, tile_slot):
    sub = lax.axis_index("sub")
    row = lax.axis_index("row")
    col = lax.axis_index("col")
    group = sub * 4 + row
    idx, code = index(tile_owner.reshape(1, 128), tile_slot.reshape(1, 128))
    lead, codes, outgoing = lead_gather(idx, front, code, child_tiles)
    arrived = lax.all_to_all(outgoing, ("sub", "row", "col"), split_axis=0, concat_axis=0, tiled=True)
    arrived = arrived.reshape(256, 128, 128)
    factor, hi, lo = chol(lead)
    landing = landings(codes, group * 4 + col)
    order = plan(landing)
    panel = head(landing, order, front, arrived)
    out, panel_out = panel_exchange(order, panel, hi, lo, factor, front, arrived)
    return out, panel_out.reshape(4, 1, 128, 2, 1, 128)


def solution(mesh):
    return jax.shard_map(
        local,
        mesh=mesh,
        in_specs=(
            P(None, ("sub", "row"), None, None, "col", None),
            P(("sub", "row", "col"), None, None),
            P(("sub", "row", "col"), None),
            P(("sub", "row", "col")),
        ),
        out_specs=(
            P(None, ("sub", "row"), None, None, "col", None),
            P(None, ("sub", "row"), None, None, "col", None),
        ),
        check_vma=False,
    )
```

```python
import jax
import jax.numpy as jnp
from jax import lax
from jax.experimental import pallas as pl
from jax.experimental.pallas import tpu as pltpu
from jax.sharding import PartitionSpec as P

F32, BF = jnp.float32, jnp.bfloat16
HI = lax.Precision.HIGHEST
V = pltpu.VMEM
ANY = pl.ANY
MESH = pl.DeviceIdType.MESH


def nt(a, b):
    return lax.dot_general(a, b, (((1,), (1,)), ((), ())), precision=HI, preferred_element_type=F32)


def nn(a, b):
    return lax.dot_general(a, b, (((1,), (0,)), ((), ())), precision=HI, preferred_element_type=F32)


def split3(x):
    h = x.astype(BF).astype(F32)
    r = x - h
    m = r.astype(BF).astype(F32)
    return h, m, r - m


def diag_factor(d_ref, u_ref, x_ref, cb_ref, r_ref):
    def body(b, carry):
        r0 = pl.multiple_of(b * 8, 8)
        block = d_ref[pl.ds(r0, 8), 0:128]
        rolled = pltpu.roll(block, (128 - r0) % 128, 1)
        for j in range(8):
            cb_ref[j] = jnp.broadcast_to(rolled[:, j:j + 1], (8, 128))
        r_ref[:, 0:128] = block
        r_ref[:, 128:256] = d_ref[pl.ds(r0, 8), 128:256]
        e = {}
        for i in range(8):
            for j in range(i + 1):
                e[i, j] = cb_ref[j, i:i + 1, :]
        rows = []
        for i in range(8):
            rows.append([r_ref[i:i + 1, 0:128], r_ref[i:i + 1, 128:256]])
        for j in range(8):
            inv = lax.rsqrt(e[j, j])
            low = {}
            for i in range(j + 1, 8):
                low[i] = e[i, j] * inv
            for h in range(2):
                rows[j][h] = rows[j][h] * inv
            for i in range(j + 1, 8):
                for m in range(j + 1, i + 1):
                    e[i, m] = e[i, m] - low[i] * low[m]
                for h in range(2):
                    rows[i][h] = rows[i][h] - low[i] * rows[j][h]
        for i in range(8):
            r_ref[i:i + 1, 0:128] = rows[i][0]
            r_ref[i:i + 1, 128:256] = rows[i][1]
        r = r_ref[...]
        u_ref[pl.ds(r0, 8), :] = r[:, 0:128]
        x_ref[pl.ds(r0, 8), :] = r[:, 128:256]
        h, m, l = split3(r)
        left = jnp.concatenate([h, h, m, h, l, m], 0)[:, 0:128].astype(BF)
        right = jnp.concatenate([h, m, h, l, h, m], 0).astype(BF)
        d_ref[...] = d_ref[...] - lax.dot_general(left, right, (((0,), (0,)), ((), ())), preferred_element_type=F32)
        return carry
    lax.fori_loop(0, 16, body, 0)


def chol_kernel(lead_ref, l_ref, hi_ref, lo_ref, s_ref, w_ref, d_ref, u_ref, x_ref, cb_ref, r_ref):
    row = lax.broadcasted_iota(jnp.int32, (128, 128), 0)
    col = lax.broadcasted_iota(jnp.int32, (128, 128), 1)
    eye = (row == col).astype(F32)
    n = 8
    for i in range(n):
        for j in range(i + 1):
            t = lead_ref[i, j]
            if i == j:
                t = jnp.where(row >= col, t, t.T)
            s_ref[i * 128:(i + 1) * 128, j * 128:(j + 1) * 128] = t
    w_ref[...] = jnp.zeros_like(w_ref)
    l_ref[...] = jnp.zeros_like(l_ref)
    for k in range(n):
        a, b = k * 128, (k + 1) * 128
        d_ref[:, 0:128] = s_ref[a:b, a:b]
        d_ref[:, 128:256] = eye
        diag_factor(d_ref, u_ref, x_ref, cb_ref, r_ref)
        x = x_ref[...]
        l_ref[a:b, a:b] = jnp.where(row >= col, u_ref[...].T, 0.0).astype(BF)
        if k > 0:
            w_ref[a:b, 0:a] = nn(x, w_ref[a:b, 0:a])
        w_ref[a:b, a:b] = x
        if k < n - 1:
            p = nt(s_ref[b:, a:b], x)
            s_ref[b:, a:b] = p
            l_ref[b:, a:b] = p.astype(BF)
            for j in range(k + 1, n):
                c, d = j * 128, (j + 1) * 128
                s_ref[c:, c:d] = s_ref[c:, c:d] - nt(s_ref[c:, a:b], s_ref[c:d, a:b])
            w_ref[b:, 0:b] = w_ref[b:, 0:b] - nn(p, w_ref[a:b, 0:b])
    for k in range(n):
        a, b = k * 128, (k + 1) * 128
        y = w_ref[a:b, :]
        h = y.astype(BF)
        hi_ref[a:b, :] = h
        lo_ref[a:b, :] = (y - h.astype(F32)).astype(BF)


def chol(lead):
    return pl.pallas_call(
        chol_kernel,
        out_shape=[jax.ShapeDtypeStruct((1024, 1024), BF)] * 3,
        in_specs=[pl.BlockSpec(memory_space=V)],
        out_specs=[pl.BlockSpec(memory_space=V)] * 3,
        scratch_shapes=[V((1024, 1024), F32), V((1024, 1024), F32), V((128, 256), F32), V((128, 128), F32),
                        V((128, 128), F32), V((8, 8, 128), F32), V((8, 256), F32)],
        compiler_params=pltpu.CompilerParams(vmem_limit_bytes=30 << 20),
        name="chol",
    )(lead)


def index_kernel(owner_ref, slot_ref, idx_ref, code_ref):
    owner = owner_ref[...]
    code_ref[...] = owner * 128 + slot_ref[...]
    wide = jnp.broadcast_to(owner.astype(F32), (128, 128)).T
    k = lax.broadcasted_iota(jnp.int32, (128, 128), 0).astype(F32)
    match = wide == lax.broadcasted_iota(jnp.int32, (128, 128), 1).astype(F32)
    first = jnp.min(jnp.where(match, k, 127.0), 0, keepdims=True)
    last = jnp.max(jnp.where(match, k, 0.0), 0, keepdims=True)
    idx_ref[0:1, :] = first.astype(jnp.int32)
    idx_ref[1:2, :] = last.astype(jnp.int32)


def index(owner, slot):
    return pl.pallas_call(
        index_kernel,
        out_shape=(jax.ShapeDtypeStruct((2, 128), jnp.int32), jax.ShapeDtypeStruct((1, 128), jnp.int32)),
        in_specs=[pl.BlockSpec(memory_space=V)] * 2,
        out_specs=[pl.BlockSpec(memory_space=V)] * 2,
        name="index",
    )(owner, slot)


def plan_kernel(col_ref, row_ref, out_ref):
    def at(shape, axis):
        return lax.broadcasted_iota(jnp.int32, shape, axis).astype(F32)
    square = (256, 256)
    own = jnp.broadcast_to(col_ref[...], square).astype(F32)
    other = jnp.broadcast_to(row_ref[...], square).astype(F32)
    k, j = at(square, 0), at(square, 1)
    one = jnp.ones(square, F32)
    zero = jnp.zeros(square, F32)
    key, other_key = jnp.where(own < 0, 1000.0, own), jnp.where(other < 0, 1000.0, other)
    before = (other_key < key) | ((other_key == key) & (j < k))
    rank = jnp.sum(jnp.where(before, one, zero), 1, keepdims=True)
    here = jnp.broadcast_to(rank, square) == j
    order = jnp.sum(jnp.where(here, k, zero), 0, keepdims=True)
    slots = jnp.sum(jnp.where(here, key, zero), 0, keepdims=True)
    lane = at((1, 256), 1)
    same = jnp.where((slots == pltpu.roll(slots, 1, 1)) & (lane > 0) & (slots < 1000.0), 1.0, 0.0)
    half = (256, 128)
    slot = at(half, 1)
    own_key = key[:, 0:128]
    last = jnp.sum(jnp.where(own_key <= slot, 1.0, 0.0), 0, keepdims=True) - 1.0
    some = jnp.max(jnp.where(own_key == slot, 1.0, 0.0), 0, keepdims=True)

    def panel_column(x):
        return (x >= 0) & (x - 32.0 * jnp.floor(x * (1 / 32)) < 2.0)
    hit, other_hit = panel_column(own), panel_column(other)
    turn = jnp.sum(jnp.where(other_hit & (j < k), one, zero), 1, keepdims=True)
    listed = jnp.sum(jnp.where(hit & (jnp.broadcast_to(turn, square) == j), k, zero), 0, keepdims=True)
    count = jnp.sum(jnp.where(hit, one, zero), 0, keepdims=True)
    rows = [order, same, jnp.concatenate([jnp.maximum(last, 0.0), some], 1), listed, count]
    for r in range(5):
        out_ref[r:r + 1, :] = rows[r].astype(jnp.int32)


def plan(land):
    return pl.pallas_call(
        plan_kernel,
        out_shape=jax.ShapeDtypeStruct((5, 256), jnp.int32),
        in_specs=[pl.BlockSpec(memory_space=V)] * 2,
        out_specs=pl.BlockSpec(memory_space=V),
        name="plan",
    )(land.reshape(256, 1), land.reshape(1, 256))


def head_kernel(land_ref, list_ref, front_ref, arr_ref, out_ref, buf_ref, acc_ref, fsem, asem):
    count = list_ref[4, 0]
    def arrive(n, i):
        return pltpu.make_async_copy(arr_ref.at[list_ref[3, n]], buf_ref.at[i], asem.at[i])
    def fetch(s):
        return pltpu.make_async_copy(front_ref.at[:, 0, :, s, 0, :], acc_ref.at[s], fsem.at[s])
    for s in range(2):
        fetch(s).start()
    def batch(b, carry):
        def begin(i, c):
            arrive(b * 16 + i, i).start()
            return c
        def end(i, c):
            n = b * 16 + i
            slot = land_ref[list_ref[3, n]]
            s, q = slot % 32, slot // 32
            arrive(n, i).wait()
            acc_ref[s, q] = acc_ref[s, q] + buf_ref[i].astype(F32)
            return c
        here = lax.min(count - b * 16, 16)
        lax.fori_loop(0, here, begin, 0)
        @pl.when(b == 0)
        def _():
            for s in range(2):
                fetch(s).wait()
        lax.fori_loop(0, here, end, 0)
        return carry
    lax.fori_loop(0, lax.max((count + 15) // 16, 1), batch, 0)
    out_ref[...] = acc_ref[...]


def head(land, listed, front, arrived):
    return pl.pallas_call(
        head_kernel,
        out_shape=jax.ShapeDtypeStruct((2, 4, 128, 128), F32),
        grid_spec=pltpu.PrefetchScalarGridSpec(
            num_scalar_prefetch=2, grid=(1,),
            in_specs=[pl.BlockSpec(memory_space=ANY)] * 2,
            out_specs=pl.BlockSpec((2, 4, 128, 128), lambda g, a, b: (0, 0, 0, 0)),
            scratch_shapes=[V((16, 128, 128), BF), V((2, 4, 128, 128), F32),
                            pltpu.SemaphoreType.DMA((2,)), pltpu.SemaphoreType.DMA((16,))]),
        compiler_params=pltpu.CompilerParams(vmem_limit_bytes=60 << 20),
        name="head",
    )(land, listed, front, arrived)


def panel_kernel(order_ref, panel_ref, hi_hbm, lo_hbm, low_hbm, front_ref, arr_ref, out_ref, pout_ref,
                 brow_ref, bcol_ref, acc_ref, buf_ref, run_ref, arow, ah, al, hi, lo, low, xb, rl, fsem, asem, osem, lsem, ps, pr, xs, xr, ws, wr, ys, yr, rs, rr, zs, zr, fs, fr, ms, mr):
    sub, row, col = lax.axis_index("sub"), lax.axis_index("row"), lax.axis_index("col")
    group = 4 * sub + row
    mate = sub + 1 - 2 * lax.rem(sub, 2)

    def n4(x, d):
        return lax.rem(x + 4 + d, 4)

    def n8(x, d):
        return lax.rem(x + 8 + d, 8)

    def remote(src, dst, send, recv, **where):
        return pltpu.make_async_remote_copy(src, dst, send, recv, device_id=where, device_id_type=MESH)

    loads = [pltpu.make_async_copy(hi_hbm, hi, lsem.at[0]), pltpu.make_async_copy(lo_hbm, lo, lsem.at[1]),
             pltpu.make_async_copy(low_hbm.at[pl.ds(pl.multiple_of(lax.min(group, 7) * 128, 128), 128)], low, lsem.at[2]),
             pltpu.make_async_copy(panel_ref.at[:, col], arow.at[col], lsem.at[3])]
    barrier = pltpu.get_barrier_semaphore()
    for d in (1, 3):
        pl.semaphore_signal(barrier, inc=1, device_id={"row": n4(row, d)}, device_id_type=MESH)
        pl.semaphore_signal(barrier, inc=1, device_id={"sub": n8(sub, 2 * d if d == 1 else -2)}, device_id_type=MESH)
    for d in (1, 2, 3):
        pl.semaphore_signal(barrier, inc=1, device_id={"col": n4(col, d)}, device_id_type=MESH)
    pl.semaphore_signal(barrier, inc=1, device_id={"sub": mate}, device_id_type=MESH)
    for copy in loads:
        copy.start()
    pl.semaphore_wait(barrier, 8)

    def fetch(s):
        return pltpu.make_async_copy(front_ref.at[:, 0, :, s, 0, :], acc_ref.at[s], fsem.at[s])
    def arrived(c):
        return pltpu.make_async_copy(arr_ref.at[pl.ds(c * 32, 32)], buf_ref.at[pl.ds(c * 32, 32)], asem.at[c])
    def put(s):
        return pltpu.make_async_copy(acc_ref.at[s], out_ref.at[:, 0, :, s, 0, :], osem.at[s])
    def early(s):
        return pltpu.make_async_copy(panel_ref.at[s], out_ref.at[:, 0, :, s, 0, :], osem.at[s])
    def each(low, high, f):
        def go(s, c):
            f(s)
            return c
        lax.fori_loop(low, high, go, 0)

    def take(h, d):
        return remote(panel_ref.at[h, n4(col, d)], arow.at[col, h], ps.at[h, d - 1], pr.at[h, d - 1], col=n4(col, d))
    def taken(h, d):
        return remote(panel_ref.at[h, n4(col, d)], arow.at[n4(col, -d), h], ps.at[h, d - 1], pr.at[h, d - 1], col=n4(col, d))
    for h in range(2):
        for d in (1, 3, 2):
            take(h, d).start()
    each(0, 8, lambda c: arrived(c).start())
    each(2, 32, lambda s: fetch(s).start())
    loads[3].wait()
    top = (group < 8) & (col == 0)

    def mm(x, y):
        return lax.dot_general(x, y, (((1,), (1,)), ((), ())), preferred_element_type=F32)

    def solve(h):
        for d in (1, 3, 2):
            taken(h, d).wait_recv()
        for t in range(4):
            v = arow[t, h]
            u = v.astype(BF)
            at = (4 * h + t) * 128
            ah[:, at:at + 128] = u
            al[:, at:at + 128] = (v - u.astype(F32)).astype(BF)
        if h == 0:
            for copy in loads[:3]:
                copy.wait()
        for b in (2 * h, 2 * h + 1):
            w = 256 * (b + 1)
            rows = pl.ds(256 * b, 256)
            y = mm(ah[:, 0:w], hi[rows, 0:w]) + (mm(ah[:, 0:w], lo[rows, 0:w]) + mm(al[:, 0:w], hi[rows, 0:w]))
            y = jnp.where(top, low[:, 256 * b:w], y.astype(BF))
            at = 256 * (b - 2 * h)
            xb[h, row, :, at:at + 256] = y
            brow_ref[h, col, :, at:at + 256] = y

    half = [pl.ds(0, 64), pl.ds(64, 64)]
    step = [1, -1]
    def xsend(h, i):
        return remote(xb.at[h, row], xb.at[h, row], xs.at[h, i], xr.at[h, i], row=n4(row, step[i]))
    def xrecv(h, i):
        at = xb.at[h, n4(row, -step[i])]
        return remote(at, at, xs.at[h, i], xr.at[h, i], row=n4(row, step[i]))
    def xforward(h, i, r):
        at = xb.at[h, r, half[i]]
        return remote(at, at, xs.at[h, 2 + i], xr.at[h, 2 + i], row=n4(row, step[i]))
    def wsend(h, i):
        return remote(brow_ref.at[h, col], brow_ref.at[h, col], ws.at[h, i], wr.at[h, i], col=n4(col, step[i]))
    def wrecv(h, i):
        at = brow_ref.at[h, n4(col, -step[i])]
        return remote(at, at, ws.at[h, i], wr.at[h, i], col=n4(col, step[i]))
    def wforward(h, i, c):
        at = brow_ref.at[h, c, half[i]]
        return remote(at, at, ws.at[h, 2 + i], wr.at[h, 2 + i], col=n4(col, step[i]))

    def ynear(h, i):
        return remote(xb.at[h, n4(col, step[i])], bcol_ref.at[h, col, sub], ys.at[h, i], yr.at[h, i], col=n4(col, step[i]))
    def ynear_in(h, i):
        return remote(xb.at[h, 0], bcol_ref.at[h, n4(col, -step[i]), sub], ys.at[h, i], yr.at[h, i], col=n4(col, step[i]))
    def yfar(h, i):
        return remote(xb.at[h, n4(col, 2), half[i]], rl.at[h, i], rs.at[h, i], rr.at[h, i], col=n4(col, step[i]))
    def yrelay(h, i):
        return remote(rl.at[h, i], bcol_ref.at[h, n4(col, -step[i]), sub, half[i]], ys.at[h, 2 + i], yr.at[h, 2 + i], col=n4(col, step[i]))
    def yfar_in(h, i):
        return remote(rl.at[h, i], bcol_ref.at[h, n4(col, 2), sub, half[i]], ys.at[h, 2 + i], yr.at[h, 2 + i], col=n4(col, step[i]))
    def home(h):
        return pltpu.make_async_copy(xb.at[h, col], bcol_ref.at[h, col, sub], lsem.at[4 + h])

    def ysend(h, c):
        d = n4(c, -col)
        @pl.when(d == 0)
        def _():
            home(h).start()
        for i in range(2):
            @pl.when(d == (1, 3)[i])
            def _():
                ynear(h, i).start()
        @pl.when(d == 2)
        def _():
            yfar(h, 0).start()
            yfar(h, 1).start()

    def own(h, e, i):
        at = bcol_ref.at[h, n4(col, e), sub]
        return remote(at if e else xb.at[h, col], at, zs.at[h, i, e], zr.at[h, i, e], sub=n8(sub, 2 * step[i]))
    def arrive(h, e, i):
        at = bcol_ref.at[h, n4(col, e), n8(sub, -2 * step[i])]
        return remote(at, at, zs.at[h, i, e], zr.at[h, i, e], sub=n8(sub, 2 * step[i]))
    side = [0, 0, 1, 1]
    def onward(h, e, i, z):
        at = bcol_ref.at[h, n4(col, e), n8(sub, z)]
        return remote(at, at, fs.at[h, e], fr.at[h, e], sub=n8(sub, 2 * step[i]))
    def swap(h, e, k, z):
        at = bcol_ref.at[h, n4(col, e), n8(sub, z)]
        return remote(at if k or e else xb.at[h, col], at, ms.at[h, k, e], mr.at[h, k, e], sub=mate)
    def swapped(h, e, k, z):
        at = bcol_ref.at[h, n4(col, e), n8(mate, z)]
        return remote(at, at, ms.at[h, k, e], mr.at[h, k, e], sub=mate)

    def launch(h, e):
        own(h, e, 0).start()
        own(h, e, 1).start()
        swap(h, e, 0, 0).start()
    apart = n4(col, -row)

    def gather(c):
        def go(k, total):
            i = c * 32 + k
            total = buf_ref[order_ref[0, i]].astype(F32) + order_ref[1, i].astype(F32) * total
            run_ref[i] = total
            return total
        first = jnp.zeros((128, 128), F32) if c == 0 else run_ref[c * 32 - 1]
        lax.fori_loop(0, 32, go, first)

    def settle(s):
        for q in range(4):
            slot = q * 32 + s
            acc_ref[s, q] = acc_ref[s, q] + order_ref[2, 128 + slot].astype(F32) * run_ref[order_ref[2, slot]]

    keep = jnp.where(group < 8, 0.0, 1.0)
    pair0 = sub - lax.rem(sub, 2)

    def update(e, dz):
        q, z = n4(col, e), n8(pair0, dz)
        s = q * 8 + z
        @pl.when(s >= 2)
        def _():
            settle(s)
            settle(s + 1)
            y = (mm(brow_ref[0].reshape(512, 512), bcol_ref[0, q, pl.ds(z, 2)].reshape(256, 512))
                 + mm(brow_ref[1].reshape(512, 512), bcol_ref[1, q, pl.ds(z, 2)].reshape(256, 512)))
            for u in range(2):
                t = y[:, u * 128:(u + 1) * 128].reshape(4, 128, 128)
                acc_ref[s + u, 0] = acc_ref[s + u, 0] - keep * t[0]
                acc_ref[s + u, 1:4] = acc_ref[s + u, 1:4] - t[1:4]
                put(s + u).start()

    def near(h):
        ynear_in(h, 1).wait_recv()
        launch(h, 1)
        ynear_in(h, 0).wait_recv()
        launch(h, 3)

    def reach(h, d):
        ysend(h, n4(row, d))
        @pl.when(apart == d)
        def _():
            launch(h, 0)

    for h in range(2):
        solve(h)
        for i in range(2):
            xsend(h, i).start()
        for i in range(2):
            wsend(h, i).start()
        reach(h, 0)
    early(0).start()
    early(1).start()
    each(0, 8, lambda c: arrived(c).wait())
    for c in range(3):
        gather(c)
    for h in range(2):
        for i in range(2):
            xrecv(h, i).wait_recv()
            xforward(h, i, n4(row, -step[i])).start()
            reach(h, 3 if i == 0 else 1)
        for i in range(2):
            wrecv(h, i).wait_recv()
            wforward(h, i, n4(col, -step[i])).start()
    @pl.when(apart == 0)
    def _():
        near(0)
        near(1)
    for c in range(3, 8):
        gather(c)
    for h in range(2):
        for i in range(2):
            xforward(h, i, n4(row, 2)).wait_recv()
        reach(h, 2)
    each(2, 32, lambda s: fetch(s).wait())
    for h in range(2):
        for i in range(2):
            yfar(h, i).wait_recv()
            yrelay(h, i).start()
    @pl.when(apart != 0)
    def _():
        near(0)
        near(1)
    for h in range(2):
        yfar_in(h, 0).wait_recv()
        yfar_in(h, 1).wait_recv()
        launch(h, 2)
    for h in range(2):
        for i in range(2):
            wforward(h, i, n4(col, 2)).wait_recv()
        home(h).wait()

    def gray(k):
        return k + jnp.where(k == 2, 1, 0) - jnp.where(k == 3, 1, 0)

    def product(e, k, z):
        for h in range(2):
            swapped(h, e, k, z).wait_recv()
        update(e, z)

    def pass_on(k, carry):
        e = gray(k)
        for h in range(2):
            for i in range(2):
                arrive(h, e, i).wait_recv()
                @pl.when((e < 2) if i == 0 else (e >= 2))
                def _():
                    onward(h, e, i, -2 * step[i]).start()
                swap(h, e, 1 + i, -2 * step[i]).start()

        def three(j, c):
            @pl.when((j == 0) | (k > 0))
            def _():
                product(jnp.where(j == 0, e, gray(lax.max(k - 1, 0))), j, jnp.where(j == 0, 0, 4 * j - 6))
            return c
        lax.fori_loop(0, 3, three, 0)
        return carry
    lax.fori_loop(0, 4, pass_on, 0)

    for q in range(4):
        pair = [brow_ref[s, q, :, pl.ds(pl.multiple_of(col * 128, 128), 128)] for s in range(2)]
        pout_ref[q] = jnp.stack([x.astype(F32) for x in pair], 1).astype(BF)

    def last(k, carry):
        @pl.when(k < 4)
        def _():
            e = gray(k)
            for h in range(2):
                onward(h, e, 0, 4).wait_recv()
                swap(h, e, 3, 4).start()

        def two(j, c):
            @pl.when((j == 0) | (k == 0))
            def _():
                product(jnp.where(k == 0, 2, gray(lax.max(k - 1, 0))), jnp.where(k == 0, 1 + j, 3), jnp.where(k == 0, 4 * j - 2, 4))
            return c
        lax.fori_loop(0, 2, two, 0)
        return carry
    lax.fori_loop(0, 5, last, 0)
    early(0).wait()
    early(1).wait()
    each(2, 32, lambda s: put(s).wait())

    for h in range(2):
        for d in (1, 2, 3):
            take(h, d).wait_send()
        for i in range(2):
            xsend(h, i).wait_send()
            wsend(h, i).wait_send()
            xforward(h, i, n4(row, -step[i])).wait_send()
            wforward(h, i, n4(col, -step[i])).wait_send()
            ynear(h, i).wait_send()
            yfar(h, i).wait_send()
            yrelay(h, i).wait_send()
        for e in range(4):
            own(h, e, 0).wait_send()
            own(h, e, 1).wait_send()
            onward(h, e, side[e], -2 * step[side[e]]).wait_send()
            swap(h, e, 0, 0).wait_send()
            swap(h, e, 1, -2).wait_send()
            swap(h, e, 2, 2).wait_send()
            swap(h, e, 3, 4).wait_send()


def panel_exchange(order, panel, hi, lo, low, front, arrived):
    D = pltpu.SemaphoreType.DMA
    H = pltpu.HBM
    return pl.pallas_call(
        panel_kernel,
        out_shape=(jax.ShapeDtypeStruct((4, 1, 128, 32, 1, 128), F32), jax.ShapeDtypeStruct((4, 128, 2, 128), BF)),
        in_specs=[pl.BlockSpec(memory_space=pltpu.SMEM), pl.BlockSpec(memory_space=V)] + [pl.BlockSpec(memory_space=H)] * 5,
        out_specs=(pl.BlockSpec(memory_space=H), pl.BlockSpec(memory_space=V)),
        scratch_shapes=[V((2, 4, 128, 512), BF), V((2, 4, 8, 128, 512), BF), V((32, 4, 128, 128), F32), V((256, 128, 128), BF),
                        V((256, 128, 128), F32), V((4, 2, 128, 128), F32), V((128, 1024), BF), V((128, 1024), BF),
                        V((1024, 1024), BF), V((1024, 1024), BF),
                        V((128, 1024), BF), V((2, 4, 128, 512), BF), V((2, 2, 64, 512), BF), D((32,)), D((8,)), D((32,)), D((6,))]
        + [D((2, 3))] * 2 + [D((2, 4))] * 6 + [D((2, 2))] * 2 + [D((2, 2, 4))] * 2 + [D((2, 4))] * 2 + [D((2, 4, 4))] * 2,
        compiler_params=pltpu.CompilerParams(vmem_limit_bytes=60 << 20, collective_id=2, has_side_effects=True),
        name="panel",
    )(order, panel, hi, lo, low, front, arrived)


def lead_kernel(idx_ref, front_ref, code_ref, child_ref, lead_ref, codes_ref, sent_ref, own_ref, tile_ref, pack_ref, tsem, psem, lsem, zs, zr, zls, zlr, xs, xr, ys, yr, as_, ar, bs, br, cas, car, cbs, cbr):
    sub, row, col = lax.axis_index("sub"), lax.axis_index("row"), lax.axis_index("col")
    par = lax.rem(sub, 2)
    mate = sub + 1 - 2 * par
    line = 4 * par + row
    need = (par == 1) | (col <= row)

    def remote(src, dst, send, recv, **where):
        return pltpu.make_async_remote_copy(src, dst, send, recv, device_id=where, device_id_type=MESH)

    barrier = pltpu.get_barrier_semaphore()
    for d in range(1, 8):
        pl.semaphore_signal(barrier, inc=1, device_id={"sub": lax.rem(sub + d, 8)}, device_id_type=MESH)
    for d in range(1, 4):
        pl.semaphore_signal(barrier, inc=1, device_id={"row": lax.rem(row + d, 4)}, device_id_type=MESH)
        pl.semaphore_signal(barrier, inc=1, device_id={"col": lax.rem(col + d, 4)}, device_id_type=MESH)

    mine = [pltpu.make_async_copy(front_ref.at[0, 0, :, s, 0, :], own_ref.at[s], lsem.at[s]) for s in range(2)]
    code = pltpu.make_async_copy(code_ref, codes_ref.at[col, row, sub], lsem.at[2])
    tiles = [pltpu.make_async_copy(child_ref.at[pl.ds(32 * g, 32)], tile_ref.at[pl.ds(32 * g, 32)], tsem.at[g]) for g in range(4)]
    packs = [pltpu.make_async_copy(pack_ref.at[pl.ds(16 * g, 16)], sent_ref.at[pl.ds(16 * g, 16)], psem.at[g]) for g in range(8)]

    def pack(g):
        def go(j, c):
            for u in range(2):
                pack_ref[16 * g + j, u] = tile_ref[idx_ref[u, 16 * g + j]]
            return c
        lax.fori_loop(0, 16, go, 0)
        packs[g].start()

    code.start()
    mine[0].start()
    mine[1].start()
    for copy in tiles:
        copy.start()
    mine[0].wait()
    mine[1].wait()
    keep = [pltpu.make_async_copy(own_ref.at[s], lead_ref.at[line, 4 * s + col], lsem.at[3 + s]) for s in range(2)]

    @pl.when(sub < 2)
    def _():
        keep[0].start()
        keep[1].start()
    pl.semaphore_wait(barrier, 13)

    def zcode(d):
        return remote(code_ref, codes_ref.at[col, row, sub], zs.at[d - 1], zr.at[d - 1], sub=lax.rem(sub + d, 8))
    def zcode_in(d):
        return remote(code_ref, codes_ref.at[col, row, lax.rem(sub + 8 - d, 8)], zs.at[d - 1], zr.at[d - 1], sub=lax.rem(sub + d, 8))
    need1 = (par == 1) & (col <= row)

    @pl.when(sub < 2)
    def _():
        for d in (1, 3, 2):
            @pl.when(need)
            def _():
                remote(own_ref.at[0], lead_ref.at[line, col], zls.at[d - 1, 0], zlr.at[0], sub=sub + 2 * d).start()
            @pl.when(need1)
            def _():
                remote(own_ref.at[1], lead_ref.at[line, 4 + col], zls.at[d - 1, 1], zlr.at[1], sub=sub + 2 * d).start()
    for d in range(1, 8):
        zcode(d).start()
    for copy in tiles:
        copy.wait()
    for g in range(4):
        pack(g)

    @pl.when(sub < 2)
    def _():
        keep[0].wait()
        keep[1].wait()

    @pl.when(sub >= 2)
    def _():
        @pl.when(need)
        def _():
            remote(own_ref.at[0], lead_ref.at[line, col], zls.at[0, 0], zlr.at[0], sub=par).wait_recv()
        @pl.when(need1)
        def _():
            remote(own_ref.at[1], lead_ref.at[line, 4 + col], zls.at[0, 1], zlr.at[1], sub=par).wait_recv()

    def ax(d, r):
        return remote(lead_ref.at[4 + r, col], lead_ref.at[4 + r, col], as_.at[0, d - 1], ar.at[0, d - 1], row=lax.rem(row + d, 4))
    def ay(d, c):
        return remote(lead_ref.at[pl.ds(4, 4), c], lead_ref.at[pl.ds(4, 4), c], as_.at[1, d - 1], ar.at[1, d - 1], col=lax.rem(col + d, 4))
    def by(d, c):
        at = lead_ref.at[line, 4 * par + c]
        return remote(at, at, bs.at[d - 1, 4], br.at[d - 1, 4], col=lax.rem(col + d, 4))
    def bx(d, r, c):
        at = lead_ref.at[4 * par + r, 4 * par + c]
        return remote(at, at, bs.at[d - 1, c], br.at[d - 1, c], row=lax.rem(row + d, 4))
    for d in (1, 3, 2):
        @pl.when(par == 1)
        def _():
            ax(d, row).start()
        @pl.when(col <= row)
        def _():
            by(d, col).start()
    code.wait()
    for d in range(1, 8):
        zcode_in(d).wait_recv()
    def cx(d, r):
        return remote(codes_ref.at[col, r], codes_ref.at[col, r], xs.at[d - 1], xr.at[d - 1], row=lax.rem(row + d, 4))
    def cy(d, c):
        return remote(codes_ref.at[c], codes_ref.at[c], ys.at[d - 1], yr.at[d - 1], col=lax.rem(col + d, 4))
    for d in range(1, 4):
        cx(d, row).start()
    for d in (1, 3, 2):
        @pl.when(par == 1)
        def _():
            ax(d, lax.rem(row + 4 - d, 4)).wait_recv()
        @pl.when(lax.rem(col + 4 - d, 4) <= row)
        def _():
            by(d, lax.rem(col + 4 - d, 4)).wait_recv()
    for d in (1, 3, 2):
        @pl.when(par == 1)
        def _():
            ay(d, col).start()
        for c in range(4):
            @pl.when(c <= row)
            def _():
                bx(d, row, c).start()

    def swap_a(c):
        at = lead_ref.at[pl.ds(4, 4), c]
        return remote(at, at, cas.at[c], car.at[c], sub=mate)
    def swap_b(p, r, c):
        at = lead_ref.at[4 * p + r, 4 * p + c]
        return remote(at, at, cbs.at[r, c], cbr.at[r, c], sub=mate)
    def hand(r, c):
        @pl.when(par == 1)
        def _():
            swap_a(c).start()
        for u in range(4):
            @pl.when(u <= r)
            def _():
                swap_b(par, r, u).start()
    hand(row, col)
    for g in range(4, 8):
        pack(g)
    for d in range(1, 4):
        cx(d, lax.rem(row + 4 - d, 4)).wait_recv()
    for d in range(1, 4):
        cy(d, col).start()
    for d in (1, 3, 2):
        r = lax.rem(row + 4 - d, 4)
        @pl.when(par == 1)
        def _():
            ay(d, lax.rem(col + 4 - d, 4)).wait_recv()
        for c in range(4):
            @pl.when(c <= r)
            def _():
                bx(d, r, c).wait_recv()
        hand(r, lax.rem(col + 4 - d, 4))
    @pl.when(par == 0)
    def _():
        for c in range(4):
            swap_a(c).wait_recv()
    for r in range(4):
        for c in range(r + 1):
            swap_b(1 - par, r, c).wait_recv()
    for d in range(1, 4):
        cy(d, lax.rem(col + 4 - d, 4)).wait_recv()

    for d in range(1, 8):
        zcode(d).wait_send()
    @pl.when(sub < 2)
    def _():
        for d in (1, 2, 3):
            @pl.when(need)
            def _():
                remote(own_ref.at[0], lead_ref.at[line, col], zls.at[d - 1, 0], zlr.at[0], sub=sub + 2 * d).wait_send()
            @pl.when(need1)
            def _():
                remote(own_ref.at[1], lead_ref.at[line, 4 + col], zls.at[d - 1, 1], zlr.at[1], sub=sub + 2 * d).wait_send()
    for d in range(1, 4):
        cx(d, row).wait_send()
        cy(d, col).wait_send()
        @pl.when(par == 1)
        def _():
            ax(d, row).wait_send()
            ay(d, col).wait_send()
        @pl.when(col <= row)
        def _():
            by(d, col).wait_send()
        for c in range(4):
            @pl.when(c <= row)
            def _():
                bx(d, row, c).wait_send()
    @pl.when(par == 1)
    def _():
        for c in range(4):
            swap_a(c).wait_send()
    for r in range(4):
        for c in range(r + 1):
            swap_b(par, r, c).wait_send()
    for copy in packs:
        copy.wait()


def lead_gather(idx, front, code, child):
    D = pltpu.SemaphoreType.DMA
    return pl.pallas_call(
        lead_kernel,
        out_shape=(jax.ShapeDtypeStruct((8, 8, 128, 128), F32), jax.ShapeDtypeStruct((4, 4, 8, 1, 128), jnp.int32),
                   jax.ShapeDtypeStruct((128, 2, 128, 128), BF)),
        in_specs=[pl.BlockSpec(memory_space=pltpu.SMEM), pl.BlockSpec(memory_space=pltpu.HBM), pl.BlockSpec(memory_space=V),
                  pl.BlockSpec(memory_space=pltpu.HBM)],
        out_specs=(pl.BlockSpec(memory_space=V), pl.BlockSpec(memory_space=V), pl.BlockSpec(memory_space=pltpu.HBM)),
        scratch_shapes=[V((2, 128, 128), F32), V((128, 128, 128), BF), V((128, 2, 128, 128), BF), D((4,)), D((8,)), D((5,)), D((7,)), D((7,)), D((3, 2)), D((2,)), D((3,)), D((3,)), D((3,)), D((3,)),
                        D((2, 3)), D((2, 3)), D((3, 5)), D((3, 5)), D((4,)), D((4,)), D((4, 4)), D((4, 4))],
        compiler_params=pltpu.CompilerParams(vmem_limit_bytes=60 << 20, collective_id=1, has_side_effects=True),
        name="lead",
    )(idx, front, code, child)


def landings(codes, me):
    codes = codes[:, :, :, 0, :].transpose(2, 1, 0, 3).reshape(128, 128)
    place = lax.broadcasted_iota(jnp.int32, (128, 128), 1) * 128 + codes % 128
    match = codes // 128 == me
    first = jnp.min(jnp.where(match, place, 1 << 20), 1)
    last = jnp.max(jnp.where(match, place, -1), 1)
    one = jnp.where(last >= 0, first % 128, -1)
    two = jnp.where(last > first, last % 128, -1)
    return jnp.stack([one, two], 1).reshape(256)


def local(front, child_tiles, tile_owner, tile_slot):
    sub = lax.axis_index("sub")
    row = lax.axis_index("row")
    col = lax.axis_index("col")
    group = sub * 4 + row
    idx, code = index(tile_owner.reshape(1, 128), tile_slot.reshape(1, 128))
    lead, codes, outgoing = lead_gather(idx, front, code, child_tiles)
    arrived = lax.all_to_all(outgoing, ("sub", "row", "col"), split_axis=0, concat_axis=0, tiled=True)
    arrived = arrived.reshape(256, 128, 128)
    factor, hi, lo = chol(lead)
    landing = landings(codes, group * 4 + col)
    order = plan(landing)
    panel = head(landing, order, front, arrived)
    out, panel_out = panel_exchange(order, panel, hi, lo, factor, front, arrived)
    return out, panel_out.reshape(4, 1, 128, 2, 1, 128)


def solution(mesh):
    return jax.shard_map(
        local,
        mesh=mesh,
        in_specs=(
            P(None, ("sub", "row"), None, None, "col", None),
            P(("sub", "row", "col"), None, None),
            P(("sub", "row", "col"), None),
            P(("sub", "row", "col")),
        ),
        out_specs=(
            P(None, ("sub", "row"), None, None, "col", None),
            P(None, ("sub", "row"), None, None, "col", None),
        ),
        check_vma=False,
    )
```

```python
import jax
import jax.numpy as jnp
from jax import lax
from jax.experimental import pallas as pl
from jax.experimental.pallas import tpu as pltpu
from jax.sharding import PartitionSpec as P

F32, BF = jnp.float32, jnp.bfloat16
HI = lax.Precision.HIGHEST
V = pltpu.VMEM
ANY = pl.ANY
MESH = pl.DeviceIdType.MESH


def nt(a, b):
    return lax.dot_general(a, b, (((1,), (1,)), ((), ())), precision=HI, preferred_element_type=F32)


def nn(a, b):
    return lax.dot_general(a, b, (((1,), (0,)), ((), ())), precision=HI, preferred_element_type=F32)


def split3(x):
    h = x.astype(BF).astype(F32)
    r = x - h
    m = r.astype(BF).astype(F32)
    return h, m, r - m


def diag_factor(d_ref, u_ref, x_ref, cb_ref, r_ref):
    def body(b, carry):
        r0 = pl.multiple_of(b * 8, 8)
        block = d_ref[pl.ds(r0, 8), 0:128]
        rolled = pltpu.roll(block, (128 - r0) % 128, 1)
        for j in range(8):
            cb_ref[j] = jnp.broadcast_to(rolled[:, j:j + 1], (8, 128))
        r_ref[:, 0:128] = block
        r_ref[:, 128:256] = d_ref[pl.ds(r0, 8), 128:256]
        e = {}
        for i in range(8):
            for j in range(i + 1):
                e[i, j] = cb_ref[j, i:i + 1, :]
        rows = []
        for i in range(8):
            rows.append([r_ref[i:i + 1, 0:128], r_ref[i:i + 1, 128:256]])
        for j in range(8):
            inv = lax.rsqrt(e[j, j])
            low = {}
            for i in range(j + 1, 8):
                low[i] = e[i, j] * inv
            for h in range(2):
                rows[j][h] = rows[j][h] * inv
            for i in range(j + 1, 8):
                for m in range(j + 1, i + 1):
                    e[i, m] = e[i, m] - low[i] * low[m]
                for h in range(2):
                    rows[i][h] = rows[i][h] - low[i] * rows[j][h]
        for i in range(8):
            r_ref[i:i + 1, 0:128] = rows[i][0]
            r_ref[i:i + 1, 128:256] = rows[i][1]
        r = r_ref[...]
        u_ref[pl.ds(r0, 8), :] = r[:, 0:128]
        x_ref[pl.ds(r0, 8), :] = r[:, 128:256]
        h, m, l = split3(r)
        left = jnp.concatenate([h, h, m, h, l, m], 0)[:, 0:128].astype(BF)
        right = jnp.concatenate([h, m, h, l, h, m], 0).astype(BF)
        d_ref[...] = d_ref[...] - lax.dot_general(left, right, (((0,), (0,)), ((), ())), preferred_element_type=F32)
        return carry
    lax.fori_loop(0, 16, body, 0)


def chol_kernel(lead_ref, l_ref, hi_ref, lo_ref, s_ref, w_ref, d_ref, u_ref, x_ref, cb_ref, r_ref):
    row = lax.broadcasted_iota(jnp.int32, (128, 128), 0)
    col = lax.broadcasted_iota(jnp.int32, (128, 128), 1)
    eye = (row == col).astype(F32)
    n = 8
    for i in range(n):
        for j in range(i + 1):
            t = lead_ref[i, j]
            if i == j:
                t = jnp.where(row >= col, t, t.T)
            s_ref[i * 128:(i + 1) * 128, j * 128:(j + 1) * 128] = t
    w_ref[...] = jnp.zeros_like(w_ref)
    l_ref[...] = jnp.zeros_like(l_ref)
    for k in range(n):
        a, b = k * 128, (k + 1) * 128
        d_ref[:, 0:128] = s_ref[a:b, a:b]
        d_ref[:, 128:256] = eye
        diag_factor(d_ref, u_ref, x_ref, cb_ref, r_ref)
        x = x_ref[...]
        l_ref[a:b, a:b] = jnp.where(row >= col, u_ref[...].T, 0.0).astype(BF)
        if k > 0:
            w_ref[a:b, 0:a] = nn(x, w_ref[a:b, 0:a])
        w_ref[a:b, a:b] = x
        if k < n - 1:
            p = nt(s_ref[b:, a:b], x)
            s_ref[b:, a:b] = p
            l_ref[b:, a:b] = p.astype(BF)
            for j in range(k + 1, n):
                c, d = j * 128, (j + 1) * 128
                s_ref[c:, c:d] = s_ref[c:, c:d] - nt(s_ref[c:, a:b], s_ref[c:d, a:b])
            w_ref[b:, 0:b] = w_ref[b:, 0:b] - nn(p, w_ref[a:b, 0:b])
    for k in range(n):
        a, b = k * 128, (k + 1) * 128
        y = w_ref[a:b, :]
        h = y.astype(BF)
        hi_ref[a:b, :] = h
        lo_ref[a:b, :] = (y - h.astype(F32)).astype(BF)


def chol(lead):
    return pl.pallas_call(
        chol_kernel,
        out_shape=[jax.ShapeDtypeStruct((1024, 1024), BF)] * 3,
        in_specs=[pl.BlockSpec(memory_space=V)],
        out_specs=[pl.BlockSpec(memory_space=V)] * 3,
        scratch_shapes=[V((1024, 1024), F32), V((1024, 1024), F32), V((128, 256), F32), V((128, 128), F32),
                        V((128, 128), F32), V((8, 8, 128), F32), V((8, 256), F32)],
        compiler_params=pltpu.CompilerParams(vmem_limit_bytes=30 << 20),
        name="chol",
    )(lead)


def index_kernel(owner_ref, slot_ref, idx_ref, code_ref):
    owner = owner_ref[...]
    code_ref[...] = owner * 128 + slot_ref[...]
    wide = jnp.broadcast_to(owner.astype(F32), (128, 128)).T
    k = lax.broadcasted_iota(jnp.int32, (128, 128), 0).astype(F32)
    match = wide == lax.broadcasted_iota(jnp.int32, (128, 128), 1).astype(F32)
    first = jnp.min(jnp.where(match, k, 127.0), 0, keepdims=True)
    last = jnp.max(jnp.where(match, k, 0.0), 0, keepdims=True)
    idx_ref[0:1, :] = first.astype(jnp.int32)
    idx_ref[1:2, :] = last.astype(jnp.int32)


def index(owner, slot):
    return pl.pallas_call(
        index_kernel,
        out_shape=(jax.ShapeDtypeStruct((2, 128), jnp.int32), jax.ShapeDtypeStruct((1, 128), jnp.int32)),
        in_specs=[pl.BlockSpec(memory_space=V)] * 2,
        out_specs=[pl.BlockSpec(memory_space=V)] * 2,
        name="index",
    )(owner, slot)


def plan_kernel(col_ref, row_ref, out_ref):
    def at(shape, axis):
        return lax.broadcasted_iota(jnp.int32, shape, axis).astype(F32)
    square = (256, 256)
    own = jnp.broadcast_to(col_ref[...], square).astype(F32)
    other = jnp.broadcast_to(row_ref[...], square).astype(F32)
    k, j = at(square, 0), at(square, 1)
    one = jnp.ones(square, F32)
    zero = jnp.zeros(square, F32)
    key, other_key = jnp.where(own < 0, 1000.0, own), jnp.where(other < 0, 1000.0, other)
    before = (other_key < key) | ((other_key == key) & (j < k))
    rank = jnp.sum(jnp.where(before, one, zero), 1, keepdims=True)
    here = jnp.broadcast_to(rank, square) == j
    order = jnp.sum(jnp.where(here, k, zero), 0, keepdims=True)
    slots = jnp.sum(jnp.where(here, key, zero), 0, keepdims=True)
    lane = at((1, 256), 1)
    same = jnp.where((slots == pltpu.roll(slots, 1, 1)) & (lane > 0) & (slots < 1000.0), 1.0, 0.0)
    half = (256, 128)
    slot = at(half, 1)
    own_key = key[:, 0:128]
    last = jnp.sum(jnp.where(own_key <= slot, 1.0, 0.0), 0, keepdims=True) - 1.0
    some = jnp.max(jnp.where(own_key == slot, 1.0, 0.0), 0, keepdims=True)

    def panel_column(x):
        return (x >= 0) & (x - 32.0 * jnp.floor(x * (1 / 32)) < 2.0)
    hit, other_hit = panel_column(own), panel_column(other)
    turn = jnp.sum(jnp.where(other_hit & (j < k), one, zero), 1, keepdims=True)
    listed = jnp.sum(jnp.where(hit & (jnp.broadcast_to(turn, square) == j), k, zero), 0, keepdims=True)
    count = jnp.sum(jnp.where(hit, one, zero), 0, keepdims=True)
    rows = [order, same, jnp.concatenate([jnp.maximum(last, 0.0), some], 1), listed, count]
    for r in range(5):
        out_ref[r:r + 1, :] = rows[r].astype(jnp.int32)


def plan(land):
    return pl.pallas_call(
        plan_kernel,
        out_shape=jax.ShapeDtypeStruct((5, 256), jnp.int32),
        in_specs=[pl.BlockSpec(memory_space=V)] * 2,
        out_specs=pl.BlockSpec(memory_space=V),
        name="plan",
    )(land.reshape(256, 1), land.reshape(1, 256))


def head_kernel(land_ref, list_ref, front_ref, arr_ref, out_ref, buf_ref, acc_ref, fsem, asem):
    count = list_ref[4, 0]
    def arrive(n, i):
        return pltpu.make_async_copy(arr_ref.at[list_ref[3, n]], buf_ref.at[i], asem.at[i])
    def fetch(s):
        return pltpu.make_async_copy(front_ref.at[:, 0, :, s, 0, :], acc_ref.at[s], fsem.at[s])
    for s in range(2):
        fetch(s).start()
    def batch(b, carry):
        def begin(i, c):
            arrive(b * 16 + i, i).start()
            return c
        def end(i, c):
            n = b * 16 + i
            slot = land_ref[list_ref[3, n]]
            s, q = slot % 32, slot // 32
            arrive(n, i).wait()
            acc_ref[s, q] = acc_ref[s, q] + buf_ref[i].astype(F32)
            return c
        here = lax.min(count - b * 16, 16)
        lax.fori_loop(0, here, begin, 0)
        @pl.when(b == 0)
        def _():
            for s in range(2):
                fetch(s).wait()
        lax.fori_loop(0, here, end, 0)
        return carry
    lax.fori_loop(0, lax.max((count + 15) // 16, 1), batch, 0)
    out_ref[...] = acc_ref[...]


def head(land, listed, front, arrived):
    return pl.pallas_call(
        head_kernel,
        out_shape=jax.ShapeDtypeStruct((2, 4, 128, 128), F32),
        grid_spec=pltpu.PrefetchScalarGridSpec(
            num_scalar_prefetch=2, grid=(1,),
            in_specs=[pl.BlockSpec(memory_space=ANY)] * 2,
            out_specs=pl.BlockSpec((2, 4, 128, 128), lambda g, a, b: (0, 0, 0, 0)),
            scratch_shapes=[V((16, 128, 128), BF), V((2, 4, 128, 128), F32),
                            pltpu.SemaphoreType.DMA((2,)), pltpu.SemaphoreType.DMA((16,))]),
        compiler_params=pltpu.CompilerParams(vmem_limit_bytes=60 << 20),
        name="head",
    )(land, listed, front, arrived)


def panel_kernel(order_ref, panel_ref, hi_hbm, lo_hbm, low_hbm, front_ref, arr_ref, out_ref, pout_ref,
                 brow_ref, bcol_ref, acc_ref, buf_ref, run_ref, arow, ah, al, hi, lo, low, xb, rl, fsem, asem, osem, lsem, ps, pr, xs, xr, ws, wr, ys, yr, rs, rr, zs, zr, fs, fr, ms, mr):
    sub, row, col = lax.axis_index("sub"), lax.axis_index("row"), lax.axis_index("col")
    group = 4 * sub + row
    mate = sub + 1 - 2 * lax.rem(sub, 2)

    def n4(x, d):
        return lax.rem(x + 4 + d, 4)

    def n8(x, d):
        return lax.rem(x + 8 + d, 8)

    def remote(src, dst, send, recv, **where):
        return pltpu.make_async_remote_copy(src, dst, send, recv, device_id=where, device_id_type=MESH)

    loads = [pltpu.make_async_copy(hi_hbm, hi, lsem.at[0]), pltpu.make_async_copy(lo_hbm, lo, lsem.at[1]),
             pltpu.make_async_copy(low_hbm.at[pl.ds(pl.multiple_of(lax.min(group, 7) * 128, 128), 128)], low, lsem.at[2]),
             pltpu.make_async_copy(panel_ref.at[:, col], arow.at[col], lsem.at[3])]
    barrier = pltpu.get_barrier_semaphore()
    for d in (1, 3):
        pl.semaphore_signal(barrier, inc=1, device_id={"row": n4(row, d)}, device_id_type=MESH)
        pl.semaphore_signal(barrier, inc=1, device_id={"sub": n8(sub, 2 * d if d == 1 else -2)}, device_id_type=MESH)
    for d in (1, 2, 3):
        pl.semaphore_signal(barrier, inc=1, device_id={"col": n4(col, d)}, device_id_type=MESH)
    pl.semaphore_signal(barrier, inc=1, device_id={"sub": mate}, device_id_type=MESH)
    for copy in loads:
        copy.start()
    pl.semaphore_wait(barrier, 8)

    def fetch(s):
        return pltpu.make_async_copy(front_ref.at[:, 0, :, s, 0, :], acc_ref.at[s], fsem.at[s])
    def arrived(c):
        return pltpu.make_async_copy(arr_ref.at[pl.ds(c * 32, 32)], buf_ref.at[pl.ds(c * 32, 32)], asem.at[c])
    def put(s):
        return pltpu.make_async_copy(acc_ref.at[s], out_ref.at[:, 0, :, s, 0, :], osem.at[s])
    def early(s):
        return pltpu.make_async_copy(panel_ref.at[s], out_ref.at[:, 0, :, s, 0, :], osem.at[s])
    def each(low, high, f):
        def go(s, c):
            f(s)
            return c
        lax.fori_loop(low, high, go, 0)

    def take(h, d):
        return remote(panel_ref.at[h, n4(col, d)], arow.at[col, h], ps.at[h, d - 1], pr.at[h, d - 1], col=n4(col, d))
    def taken(h, d):
        return remote(panel_ref.at[h, n4(col, d)], arow.at[n4(col, -d), h], ps.at[h, d - 1], pr.at[h, d - 1], col=n4(col, d))
    for h in range(2):
        for d in (1, 3, 2):
            take(h, d).start()
    each(0, 8, lambda c: arrived(c).start())
    each(2, 32, lambda s: fetch(s).start())
    loads[3].wait()
    top = (group < 8) & (col == 0)

    def mm(x, y):
        return lax.dot_general(x, y, (((1,), (1,)), ((), ())), preferred_element_type=F32)

    def solve(h):
        for d in (1, 3, 2):
            taken(h, d).wait_recv()
        for t in range(4):
            v = arow[t, h]
            u = v.astype(BF)
            at = (4 * h + t) * 128
            ah[:, at:at + 128] = u
            al[:, at:at + 128] = (v - u.astype(F32)).astype(BF)
        if h == 0:
            for copy in loads[:3]:
                copy.wait()
        for b in (2 * h, 2 * h + 1):
            w = 256 * (b + 1)
            rows = pl.ds(256 * b, 256)
            y = mm(ah[:, 0:w], hi[rows, 0:w]) + (mm(ah[:, 0:w], lo[rows, 0:w]) + mm(al[:, 0:w], hi[rows, 0:w]))
            y = jnp.where(top, low[:, 256 * b:w], y.astype(BF))
            at = 256 * (b - 2 * h)
            xb[h, row, :, at:at + 256] = y
            brow_ref[h, col, :, at:at + 256] = y

    half = [pl.ds(0, 64), pl.ds(64, 64)]
    step = [1, -1]
    def xsend(h, i):
        return remote(xb.at[h, row], xb.at[h, row], xs.at[h, i], xr.at[h, i], row=n4(row, step[i]))
    def xrecv(h, i):
        at = xb.at[h, n4(row, -step[i])]
        return remote(at, at, xs.at[h, i], xr.at[h, i], row=n4(row, step[i]))
    def xforward(h, i, r):
        at = xb.at[h, r, half[i]]
        return remote(at, at, xs.at[h, 2 + i], xr.at[h, 2 + i], row=n4(row, step[i]))
    def wsend(h, i):
        return remote(brow_ref.at[h, col], brow_ref.at[h, col], ws.at[h, i], wr.at[h, i], col=n4(col, step[i]))
    def wrecv(h, i):
        at = brow_ref.at[h, n4(col, -step[i])]
        return remote(at, at, ws.at[h, i], wr.at[h, i], col=n4(col, step[i]))
    def wforward(h, i, c):
        at = brow_ref.at[h, c, half[i]]
        return remote(at, at, ws.at[h, 2 + i], wr.at[h, 2 + i], col=n4(col, step[i]))

    def ynear(h, i):
        return remote(xb.at[h, n4(col, step[i])], bcol_ref.at[h, col, sub], ys.at[h, i], yr.at[h, i], col=n4(col, step[i]))
    def ynear_in(h, i):
        return remote(xb.at[h, 0], bcol_ref.at[h, n4(col, -step[i]), sub], ys.at[h, i], yr.at[h, i], col=n4(col, step[i]))
    def yfar(h, i):
        return remote(xb.at[h, n4(col, 2), half[i]], rl.at[h, i], rs.at[h, i], rr.at[h, i], col=n4(col, step[i]))
    def yrelay(h, i):
        return remote(rl.at[h, i], bcol_ref.at[h, n4(col, -step[i]), sub, half[i]], ys.at[h, 2 + i], yr.at[h, 2 + i], col=n4(col, step[i]))
    def yfar_in(h, i):
        return remote(rl.at[h, i], bcol_ref.at[h, n4(col, 2), sub, half[i]], ys.at[h, 2 + i], yr.at[h, 2 + i], col=n4(col, step[i]))
    def home(h):
        return pltpu.make_async_copy(xb.at[h, col], bcol_ref.at[h, col, sub], lsem.at[4 + h])

    def ysend(h, c):
        d = n4(c, -col)
        @pl.when(d == 0)
        def _():
            home(h).start()
        for i in range(2):
            @pl.when(d == (1, 3)[i])
            def _():
                ynear(h, i).start()
        @pl.when(d == 2)
        def _():
            yfar(h, 0).start()
            yfar(h, 1).start()

    def own(h, e, i):
        at = bcol_ref.at[h, n4(col, e), sub]
        return remote(at if e else xb.at[h, col], at, zs.at[h, i, e], zr.at[h, i, e], sub=n8(sub, 2 * step[i]))
    def arrive(h, e, i):
        at = bcol_ref.at[h, n4(col, e), n8(sub, -2 * step[i])]
        return remote(at, at, zs.at[h, i, e], zr.at[h, i, e], sub=n8(sub, 2 * step[i]))
    side = [0, 0, 1, 1]
    def onward(h, e, i, z):
        at = bcol_ref.at[h, n4(col, e), n8(sub, z)]
        return remote(at, at, fs.at[h, e], fr.at[h, e], sub=n8(sub, 2 * step[i]))
    def swap(h, e, k, z):
        at = bcol_ref.at[h, n4(col, e), n8(sub, z)]
        return remote(at if k or e else xb.at[h, col], at, ms.at[h, k, e], mr.at[h, k, e], sub=mate)
    def swapped(h, e, k, z):
        at = bcol_ref.at[h, n4(col, e), n8(mate, z)]
        return remote(at, at, ms.at[h, k, e], mr.at[h, k, e], sub=mate)

    def launch(h, e):
        own(h, e, 0).start()
        own(h, e, 1).start()
        swap(h, e, 0, 0).start()
    apart = n4(col, -row)

    def gather(c):
        def go(k, total):
            i = c * 32 + k
            total = buf_ref[order_ref[0, i]].astype(F32) + order_ref[1, i].astype(F32) * total
            run_ref[i] = total
            return total
        first = jnp.zeros((128, 128), F32) if c == 0 else run_ref[c * 32 - 1]
        lax.fori_loop(0, 32, go, first)

    def settle(s):
        for q in range(4):
            slot = q * 32 + s
            acc_ref[s, q] = acc_ref[s, q] + order_ref[2, 128 + slot].astype(F32) * run_ref[order_ref[2, slot]]

    keep = jnp.where(group < 8, 0.0, 1.0)
    pair0 = sub - lax.rem(sub, 2)

    def update(e, dz):
        q, z = n4(col, e), n8(pair0, dz)
        s = q * 8 + z
        @pl.when(s >= 2)
        def _():
            settle(s)
            settle(s + 1)
            y = (mm(brow_ref[0].reshape(512, 512), bcol_ref[0, q, pl.ds(z, 2)].reshape(256, 512))
                 + mm(brow_ref[1].reshape(512, 512), bcol_ref[1, q, pl.ds(z, 2)].reshape(256, 512)))
            for u in range(2):
                t = y[:, u * 128:(u + 1) * 128].reshape(4, 128, 128)
                acc_ref[s + u, 0] = acc_ref[s + u, 0] - keep * t[0]
                acc_ref[s + u, 1:4] = acc_ref[s + u, 1:4] - t[1:4]
                put(s + u).start()

    def near(h):
        ynear_in(h, 1).wait_recv()
        launch(h, 1)
        ynear_in(h, 0).wait_recv()
        launch(h, 3)

    def reach(h, d):
        ysend(h, n4(row, d))
        @pl.when(apart == d)
        def _():
            launch(h, 0)

    for h in range(2):
        solve(h)
        for i in range(2):
            xsend(h, i).start()
        for i in range(2):
            wsend(h, i).start()
        reach(h, 0)
    early(0).start()
    early(1).start()
    each(0, 8, lambda c: arrived(c).wait())
    for c in range(3):
        gather(c)
    for h in range(2):
        for i in range(2):
            xrecv(h, i).wait_recv()
            xforward(h, i, n4(row, -step[i])).start()
            reach(h, 3 if i == 0 else 1)
        for i in range(2):
            wrecv(h, i).wait_recv()
            wforward(h, i, n4(col, -step[i])).start()
    @pl.when(apart == 0)
    def _():
        near(0)
        near(1)
    for c in range(3, 8):
        gather(c)
    for h in range(2):
        for i in range(2):
            xforward(h, i, n4(row, 2)).wait_recv()
        reach(h, 2)
    each(2, 32, lambda s: fetch(s).wait())
    for h in range(2):
        for i in range(2):
            yfar(h, i).wait_recv()
            yrelay(h, i).start()
    @pl.when(apart != 0)
    def _():
        near(0)
        near(1)
    for h in range(2):
        yfar_in(h, 0).wait_recv()
        yfar_in(h, 1).wait_recv()
        launch(h, 2)
    for h in range(2):
        for i in range(2):
            wforward(h, i, n4(col, 2)).wait_recv()
        home(h).wait()

    def gray(k):
        return k + jnp.where(k == 2, 1, 0) - jnp.where(k == 3, 1, 0)

    def product(e, k, z):
        for h in range(2):
            swapped(h, e, k, z).wait_recv()
        update(e, z)

    def pass_on(k, carry):
        e = gray(k)
        for h in range(2):
            for i in range(2):
                arrive(h, e, i).wait_recv()
                @pl.when((e < 2) if i == 0 else (e >= 2))
                def _():
                    onward(h, e, i, -2 * step[i]).start()
                swap(h, e, 1 + i, -2 * step[i]).start()

        def three(j, c):
            @pl.when((j == 0) | (k > 0))
            def _():
                product(jnp.where(j == 0, e, gray(lax.max(k - 1, 0))), j, jnp.where(j == 0, 0, 4 * j - 6))
            return c
        lax.fori_loop(0, 3, three, 0)
        return carry
    lax.fori_loop(0, 4, pass_on, 0)

    for q in range(4):
        pair = [brow_ref[s, q, :, pl.ds(pl.multiple_of(col * 128, 128), 128)] for s in range(2)]
        pout_ref[q] = jnp.stack([x.astype(F32) for x in pair], 1).astype(BF)

    def last(k, carry):
        @pl.when(k < 4)
        def _():
            e = gray(k)
            for h in range(2):
                onward(h, e, 0, 4).wait_recv()
                swap(h, e, 3, 4).start()

        def two(j, c):
            @pl.when((j == 0) | (k == 0))
            def _():
                product(jnp.where(k == 0, 2, gray(lax.max(k - 1, 0))), jnp.where(k == 0, 1 + j, 3), jnp.where(k == 0, 4 * j - 2, 4))
            return c
        lax.fori_loop(0, 2, two, 0)
        return carry
    lax.fori_loop(0, 5, last, 0)
    early(0).wait()
    early(1).wait()
    each(2, 32, lambda s: put(s).wait())

    for h in range(2):
        for d in (1, 2, 3):
            take(h, d).wait_send()
        for i in range(2):
            xsend(h, i).wait_send()
            wsend(h, i).wait_send()
            xforward(h, i, n4(row, -step[i])).wait_send()
            wforward(h, i, n4(col, -step[i])).wait_send()
            ynear(h, i).wait_send()
            yfar(h, i).wait_send()
            yrelay(h, i).wait_send()
        for e in range(4):
            own(h, e, 0).wait_send()
            own(h, e, 1).wait_send()
            onward(h, e, side[e], -2 * step[side[e]]).wait_send()
            swap(h, e, 0, 0).wait_send()
            swap(h, e, 1, -2).wait_send()
            swap(h, e, 2, 2).wait_send()
            swap(h, e, 3, 4).wait_send()


def panel_exchange(order, panel, hi, lo, low, front, arrived):
    D = pltpu.SemaphoreType.DMA
    H = pltpu.HBM
    return pl.pallas_call(
        panel_kernel,
        out_shape=(jax.ShapeDtypeStruct((4, 1, 128, 32, 1, 128), F32), jax.ShapeDtypeStruct((4, 128, 2, 128), BF)),
        in_specs=[pl.BlockSpec(memory_space=pltpu.SMEM), pl.BlockSpec(memory_space=V)] + [pl.BlockSpec(memory_space=H)] * 5,
        out_specs=(pl.BlockSpec(memory_space=H), pl.BlockSpec(memory_space=V)),
        scratch_shapes=[V((2, 4, 128, 512), BF), V((2, 4, 8, 128, 512), BF), V((32, 4, 128, 128), F32), V((256, 128, 128), BF),
                        V((256, 128, 128), F32), V((4, 2, 128, 128), F32), V((128, 1024), BF), V((128, 1024), BF),
                        V((1024, 1024), BF), V((1024, 1024), BF),
                        V((128, 1024), BF), V((2, 4, 128, 512), BF), V((2, 2, 64, 512), BF), D((32,)), D((8,)), D((32,)), D((6,))]
        + [D((2, 3))] * 2 + [D((2, 4))] * 6 + [D((2, 2))] * 2 + [D((2, 2, 4))] * 2 + [D((2, 4))] * 2 + [D((2, 4, 4))] * 2,
        compiler_params=pltpu.CompilerParams(vmem_limit_bytes=60 << 20, collective_id=2, has_side_effects=True),
        name="panel",
    )(order, panel, hi, lo, low, front, arrived)


def lead_kernel(idx_ref, front_ref, code_ref, child_ref, lead_ref, codes_ref, sent_ref, own_ref, tile_ref, pack_ref, tsem, psem, lsem, zs, zr, zls, zlr, xs, xr, ys, yr, as_, ar, bs, br, cas, car, cbs, cbr, afs, afr, bfs, bfr):
    sub, row, col = lax.axis_index("sub"), lax.axis_index("row"), lax.axis_index("col")
    par = lax.rem(sub, 2)
    mate = sub + 1 - 2 * par
    line = 4 * par + row
    need = (par == 1) | (col <= row)

    def remote(src, dst, send, recv, **where):
        return pltpu.make_async_remote_copy(src, dst, send, recv, device_id=where, device_id_type=MESH)

    barrier = pltpu.get_barrier_semaphore()
    for d in range(1, 8):
        pl.semaphore_signal(barrier, inc=1, device_id={"sub": lax.rem(sub + d, 8)}, device_id_type=MESH)
    for d in range(1, 4):
        pl.semaphore_signal(barrier, inc=1, device_id={"row": lax.rem(row + d, 4)}, device_id_type=MESH)
        pl.semaphore_signal(barrier, inc=1, device_id={"col": lax.rem(col + d, 4)}, device_id_type=MESH)

    mine = [pltpu.make_async_copy(front_ref.at[0, 0, :, s, 0, :], own_ref.at[s], lsem.at[s]) for s in range(2)]
    code = pltpu.make_async_copy(code_ref, codes_ref.at[col, row, sub], lsem.at[2])
    tiles = [pltpu.make_async_copy(child_ref.at[pl.ds(32 * g, 32)], tile_ref.at[pl.ds(32 * g, 32)], tsem.at[g]) for g in range(4)]
    packs = [pltpu.make_async_copy(pack_ref.at[pl.ds(16 * g, 16)], sent_ref.at[pl.ds(16 * g, 16)], psem.at[g]) for g in range(8)]

    def pack(g):
        def go(j, c):
            for u in range(2):
                pack_ref[16 * g + j, u] = tile_ref[idx_ref[u, 16 * g + j]]
            return c
        lax.fori_loop(0, 16, go, 0)
        packs[g].start()

    code.start()
    mine[0].start()
    mine[1].start()
    for copy in tiles:
        copy.start()
    mine[0].wait()
    mine[1].wait()
    keep = [pltpu.make_async_copy(own_ref.at[s], lead_ref.at[line, 4 * s + col], lsem.at[3 + s]) for s in range(2)]

    @pl.when(sub < 2)
    def _():
        keep[0].start()
        keep[1].start()
    pl.semaphore_wait(barrier, 13)

    def zcode(d):
        return remote(code_ref, codes_ref.at[col, row, sub], zs.at[d - 1], zr.at[d - 1], sub=lax.rem(sub + d, 8))
    def zcode_in(d):
        return remote(code_ref, codes_ref.at[col, row, lax.rem(sub + 8 - d, 8)], zs.at[d - 1], zr.at[d - 1], sub=lax.rem(sub + d, 8))
    need1 = (par == 1) & (col <= row)

    @pl.when(sub < 2)
    def _():
        for d in (1, 3, 2):
            @pl.when(need)
            def _():
                remote(own_ref.at[0], lead_ref.at[line, col], zls.at[d - 1, 0], zlr.at[0], sub=sub + 2 * d).start()
            @pl.when(need1)
            def _():
                remote(own_ref.at[1], lead_ref.at[line, 4 + col], zls.at[d - 1, 1], zlr.at[1], sub=sub + 2 * d).start()
    for d in range(1, 8):
        zcode(d).start()
    for copy in tiles:
        copy.wait()
    for g in range(4):
        pack(g)

    @pl.when(sub < 2)
    def _():
        keep[0].wait()
        keep[1].wait()

    @pl.when(sub >= 2)
    def _():
        @pl.when(need)
        def _():
            remote(own_ref.at[0], lead_ref.at[line, col], zls.at[0, 0], zlr.at[0], sub=par).wait_recv()
        @pl.when(need1)
        def _():
            remote(own_ref.at[1], lead_ref.at[line, 4 + col], zls.at[0, 1], zlr.at[1], sub=par).wait_recv()

    def ax(d, r):
        return remote(lead_ref.at[4 + r, col], lead_ref.at[4 + r, col], as_.at[0, d - 1], ar.at[0, d - 1], row=lax.rem(row + d, 4))
    def ay(d, c):
        return remote(lead_ref.at[pl.ds(4, 4), c], lead_ref.at[pl.ds(4, 4), c], as_.at[1, d - 1], ar.at[1, d - 1], col=lax.rem(col + d, 4))
    def by(d, c):
        at = lead_ref.at[line, 4 * par + c]
        return remote(at, at, bs.at[d - 1, 4], br.at[d - 1, 4], col=lax.rem(col + d, 4))
    def bx(d, r, c):
        at = lead_ref.at[4 * par + r, 4 * par + c]
        return remote(at, at, bs.at[d - 1, c], br.at[d - 1, c], row=lax.rem(row + d, 4))
    for d in (1, 3, 2):
        @pl.when(par == 1)
        def _():
            ax(d, row).start()
        @pl.when(col <= row)
        def _():
            by(d, col).start()
    code.wait()
    for d in range(1, 8):
        zcode_in(d).wait_recv()
    def cx(d, r):
        return remote(codes_ref.at[col, r], codes_ref.at[col, r], xs.at[d - 1], xr.at[d - 1], row=lax.rem(row + d, 4))
    def cy(d, c):
        return remote(codes_ref.at[c], codes_ref.at[c], ys.at[d - 1], yr.at[d - 1], col=lax.rem(col + d, 4))
    for d in range(1, 4):
        cx(d, row).start()
    for d in (1, 3, 2):
        @pl.when(par == 1)
        def _():
            ax(d, lax.rem(row + 4 - d, 4)).wait_recv()
        @pl.when(lax.rem(col + 4 - d, 4) <= row)
        def _():
            by(d, lax.rem(col + 4 - d, 4)).wait_recv()
    for d in (1, 3):
        @pl.when(par == 1)
        def _():
            ay(d, col).start()
        for c in range(4):
            @pl.when(c <= row)
            def _():
                bx(d, row, c).start()
    def ay2(i, c):
        at = lead_ref.at[pl.ds(4 + 2 * i, 2), c]
        return remote(at, at, afs.at[i], afr.at[i], col=lax.rem(col + (1, 3)[i], 4))
    def bx2(r, c):
        at = lead_ref.at[4 * par + r, 4 * par + c]
        return remote(at, at, bfs.at[c], bfr.at[c], row=lax.rem(row + (1, 3)[c // 2], 4))

    def swap_a(c):
        at = lead_ref.at[pl.ds(4, 4), c]
        return remote(at, at, cas.at[c], car.at[c], sub=mate)
    def swap_b(p, r, c):
        at = lead_ref.at[4 * p + r, 4 * p + c]
        return remote(at, at, cbs.at[r, c], cbr.at[r, c], sub=mate)
    def hand(r, c):
        @pl.when(par == 1)
        def _():
            swap_a(c).start()
        for u in range(4):
            @pl.when(u <= r)
            def _():
                swap_b(par, r, u).start()
    hand(row, col)
    for g in range(4, 8):
        pack(g)
    for d in range(1, 4):
        cx(d, lax.rem(row + 4 - d, 4)).wait_recv()
    for d in range(1, 4):
        cy(d, col).start()
    for i in range(2):
        d = (1, 3)[i]
        r = lax.rem(row + 4 - d, 4)
        @pl.when(par == 1)
        def _():
            ay(d, lax.rem(col + 4 - d, 4)).wait_recv()
            ay2(i, lax.rem(col + 4 - d, 4)).start()
        for c in range(4):
            @pl.when(c <= r)
            def _():
                bx(d, r, c).wait_recv()
                if c // 2 == i:
                    bx2(r, c).start()
        hand(r, lax.rem(col + 4 - d, 4))
    across, beyond = lax.rem(row + 2, 4), lax.rem(col + 2, 4)
    @pl.when(par == 1)
    def _():
        for i in range(2):
            ay2(i, beyond).wait_recv()
    for c in range(4):
        @pl.when(c <= across)
        def _():
            bx2(across, c).wait_recv()
    hand(across, beyond)
    @pl.when(par == 0)
    def _():
        for c in range(4):
            swap_a(c).wait_recv()
    for r in range(4):
        for c in range(r + 1):
            swap_b(1 - par, r, c).wait_recv()
    for d in range(1, 4):
        cy(d, lax.rem(col + 4 - d, 4)).wait_recv()

    for d in range(1, 8):
        zcode(d).wait_send()
    @pl.when(sub < 2)
    def _():
        for d in (1, 2, 3):
            @pl.when(need)
            def _():
                remote(own_ref.at[0], lead_ref.at[line, col], zls.at[d - 1, 0], zlr.at[0], sub=sub + 2 * d).wait_send()
            @pl.when(need1)
            def _():
                remote(own_ref.at[1], lead_ref.at[line, 4 + col], zls.at[d - 1, 1], zlr.at[1], sub=sub + 2 * d).wait_send()
    for d in range(1, 4):
        cx(d, row).wait_send()
        cy(d, col).wait_send()
        @pl.when(par == 1)
        def _():
            ax(d, row).wait_send()
        @pl.when(col <= row)
        def _():
            by(d, col).wait_send()
    for i in range(2):
        d = (1, 3)[i]
        r = lax.rem(row + 4 - d, 4)
        @pl.when(par == 1)
        def _():
            ay(d, col).wait_send()
            ay2(i, lax.rem(col + 4 - d, 4)).wait_send()
        for c in range(4):
            @pl.when(c <= row)
            def _():
                bx(d, row, c).wait_send()
        for c in (2 * i, 2 * i + 1):
            @pl.when(c <= r)
            def _():
                bx2(r, c).wait_send()
    @pl.when(par == 1)
    def _():
        for c in range(4):
            swap_a(c).wait_send()
    for r in range(4):
        for c in range(r + 1):
            swap_b(par, r, c).wait_send()
    for copy in packs:
        copy.wait()


def lead_gather(idx, front, code, child):
    D = pltpu.SemaphoreType.DMA
    return pl.pallas_call(
        lead_kernel,
        out_shape=(jax.ShapeDtypeStruct((8, 8, 128, 128), F32), jax.ShapeDtypeStruct((4, 4, 8, 1, 128), jnp.int32),
                   jax.ShapeDtypeStruct((128, 2, 128, 128), BF)),
        in_specs=[pl.BlockSpec(memory_space=pltpu.SMEM), pl.BlockSpec(memory_space=pltpu.HBM), pl.BlockSpec(memory_space=V),
                  pl.BlockSpec(memory_space=pltpu.HBM)],
        out_specs=(pl.BlockSpec(memory_space=V), pl.BlockSpec(memory_space=V), pl.BlockSpec(memory_space=pltpu.HBM)),
        scratch_shapes=[V((2, 128, 128), F32), V((128, 128, 128), BF), V((128, 2, 128, 128), BF), D((4,)), D((8,)), D((5,)), D((7,)), D((7,)), D((3, 2)), D((2,)), D((3,)), D((3,)), D((3,)), D((3,)),
                        D((2, 3)), D((2, 3)), D((3, 5)), D((3, 5)), D((4,)), D((4,)), D((4, 4)), D((4, 4)), D((2,)), D((2,)), D((4,)), D((4,))],
        compiler_params=pltpu.CompilerParams(vmem_limit_bytes=60 << 20, collective_id=1, has_side_effects=True),
        name="lead",
    )(idx, front, code, child)


def landings(codes, me):
    codes = codes[:, :, :, 0, :].transpose(2, 1, 0, 3).reshape(128, 128)
    place = lax.broadcasted_iota(jnp.int32, (128, 128), 1) * 128 + codes % 128
    match = codes // 128 == me
    first = jnp.min(jnp.where(match, place, 1 << 20), 1)
    last = jnp.max(jnp.where(match, place, -1), 1)
    one = jnp.where(last >= 0, first % 128, -1)
    two = jnp.where(last > first, last % 128, -1)
    return jnp.stack([one, two], 1).reshape(256)


def local(front, child_tiles, tile_owner, tile_slot):
    sub = lax.axis_index("sub")
    row = lax.axis_index("row")
    col = lax.axis_index("col")
    group = sub * 4 + row
    idx, code = index(tile_owner.reshape(1, 128), tile_slot.reshape(1, 128))
    lead, codes, outgoing = lead_gather(idx, front, code, child_tiles)
    arrived = lax.all_to_all(outgoing, ("sub", "row", "col"), split_axis=0, concat_axis=0, tiled=True)
    arrived = arrived.reshape(256, 128, 128)
    factor, hi, lo = chol(lead)
    landing = landings(codes, group * 4 + col)
    order = plan(landing)
    panel = head(landing, order, front, arrived)
    out, panel_out = panel_exchange(order, panel, hi, lo, factor, front, arrived)
    return out, panel_out.reshape(4, 1, 128, 2, 1, 128)


def solution(mesh):
    return jax.shard_map(
        local,
        mesh=mesh,
        in_specs=(
            P(None, ("sub", "row"), None, None, "col", None),
            P(("sub", "row", "col"), None, None),
            P(("sub", "row", "col"), None),
            P(("sub", "row", "col")),
        ),
        out_specs=(
            P(None, ("sub", "row"), None, None, "col", None),
            P(None, ("sub", "row"), None, None, "col", None),
        ),
        check_vma=False,
    )
```

```python
import jax
import jax.numpy as jnp
from jax import lax
from jax.experimental import pallas as pl
from jax.experimental.pallas import tpu as pltpu
from jax.sharding import PartitionSpec as P

F32, BF = jnp.float32, jnp.bfloat16
HI = lax.Precision.HIGHEST
V = pltpu.VMEM
ANY = pl.ANY
MESH = pl.DeviceIdType.MESH


def nt(a, b):
    return lax.dot_general(a, b, (((1,), (1,)), ((), ())), precision=HI, preferred_element_type=F32)


def nn(a, b):
    return lax.dot_general(a, b, (((1,), (0,)), ((), ())), precision=HI, preferred_element_type=F32)


def split3(x):
    h = x.astype(BF).astype(F32)
    r = x - h
    m = r.astype(BF).astype(F32)
    return h, m, r - m


def diag_factor(d_ref, u_ref, x_ref, cb_ref, r_ref):
    def body(b, carry):
        r0 = pl.multiple_of(b * 8, 8)
        block = d_ref[pl.ds(r0, 8), 0:128]
        rolled = pltpu.roll(block, (128 - r0) % 128, 1)
        for j in range(8):
            cb_ref[j] = jnp.broadcast_to(rolled[:, j:j + 1], (8, 128))
        r_ref[:, 0:128] = block
        r_ref[:, 128:256] = d_ref[pl.ds(r0, 8), 128:256]
        e = {}
        for i in range(8):
            for j in range(i + 1):
                e[i, j] = cb_ref[j, i:i + 1, :]
        rows = []
        for i in range(8):
            rows.append([r_ref[i:i + 1, 0:128], r_ref[i:i + 1, 128:256]])
        for j in range(8):
            inv = lax.rsqrt(e[j, j])
            low = {}
            for i in range(j + 1, 8):
                low[i] = e[i, j] * inv
            for h in range(2):
                rows[j][h] = rows[j][h] * inv
            for i in range(j + 1, 8):
                for m in range(j + 1, i + 1):
                    e[i, m] = e[i, m] - low[i] * low[m]
                for h in range(2):
                    rows[i][h] = rows[i][h] - low[i] * rows[j][h]
        for i in range(8):
            r_ref[i:i + 1, 0:128] = rows[i][0]
            r_ref[i:i + 1, 128:256] = rows[i][1]
        r = r_ref[...]
        u_ref[pl.ds(r0, 8), :] = r[:, 0:128]
        x_ref[pl.ds(r0, 8), :] = r[:, 128:256]
        h, m, l = split3(r)
        left = jnp.concatenate([h, h, m, h, l, m], 0)[:, 0:128].astype(BF)
        right = jnp.concatenate([h, m, h, l, h, m], 0).astype(BF)
        d_ref[...] = d_ref[...] - lax.dot_general(left, right, (((0,), (0,)), ((), ())), preferred_element_type=F32)
        return carry
    lax.fori_loop(0, 16, body, 0)


def chol_kernel(lead_ref, l_ref, hi_ref, lo_ref, s_ref, w_ref, d_ref, u_ref, x_ref, cb_ref, r_ref):
    row = lax.broadcasted_iota(jnp.int32, (128, 128), 0)
    col = lax.broadcasted_iota(jnp.int32, (128, 128), 1)
    eye = (row == col).astype(F32)
    n = 8
    for i in range(n):
        for j in range(i + 1):
            t = lead_ref[i, j]
            if i == j:
                t = jnp.where(row >= col, t, t.T)
            s_ref[i * 128:(i + 1) * 128, j * 128:(j + 1) * 128] = t
    w_ref[...] = jnp.zeros_like(w_ref)
    l_ref[...] = jnp.zeros_like(l_ref)
    for k in range(n):
        a, b = k * 128, (k + 1) * 128
        d_ref[:, 0:128] = s_ref[a:b, a:b]
        d_ref[:, 128:256] = eye
        diag_factor(d_ref, u_ref, x_ref, cb_ref, r_ref)
        x = x_ref[...]
        l_ref[a:b, a:b] = jnp.where(row >= col, u_ref[...].T, 0.0).astype(BF)
        if k > 0:
            w_ref[a:b, 0:a] = nn(x, w_ref[a:b, 0:a])
        w_ref[a:b, a:b] = x
        if k < n - 1:
            p = nt(s_ref[b:, a:b], x)
            s_ref[b:, a:b] = p
            l_ref[b:, a:b] = p.astype(BF)
            for j in range(k + 1, n):
                c, d = j * 128, (j + 1) * 128
                s_ref[c:, c:d] = s_ref[c:, c:d] - nt(s_ref[c:, a:b], s_ref[c:d, a:b])
            w_ref[b:, 0:b] = w_ref[b:, 0:b] - nn(p, w_ref[a:b, 0:b])
    for k in range(n):
        a, b = k * 128, (k + 1) * 128
        y = w_ref[a:b, :]
        h = y.astype(BF)
        hi_ref[a:b, :] = h
        lo_ref[a:b, :] = (y - h.astype(F32)).astype(BF)


def chol(lead):
    return pl.pallas_call(
        chol_kernel,
        out_shape=[jax.ShapeDtypeStruct((1024, 1024), BF)] * 3,
        in_specs=[pl.BlockSpec(memory_space=V)],
        out_specs=[pl.BlockSpec(memory_space=V)] * 3,
        scratch_shapes=[V((1024, 1024), F32), V((1024, 1024), F32), V((128, 256), F32), V((128, 128), F32),
                        V((128, 128), F32), V((8, 8, 128), F32), V((8, 256), F32)],
        compiler_params=pltpu.CompilerParams(vmem_limit_bytes=30 << 20),
        name="chol",
    )(lead)


def index_kernel(owner_ref, slot_ref, idx_ref, code_ref):
    owner = owner_ref[...]
    code_ref[...] = owner * 128 + slot_ref[...]
    wide = jnp.broadcast_to(owner.astype(F32), (128, 128)).T
    k = lax.broadcasted_iota(jnp.int32, (128, 128), 0).astype(F32)
    match = wide == lax.broadcasted_iota(jnp.int32, (128, 128), 1).astype(F32)
    first = jnp.min(jnp.where(match, k, 127.0), 0, keepdims=True)
    last = jnp.max(jnp.where(match, k, 0.0), 0, keepdims=True)
    idx_ref[0:1, :] = first.astype(jnp.int32)
    idx_ref[1:2, :] = last.astype(jnp.int32)


def index(owner, slot):
    return pl.pallas_call(
        index_kernel,
        out_shape=(jax.ShapeDtypeStruct((2, 128), jnp.int32), jax.ShapeDtypeStruct((1, 128), jnp.int32)),
        in_specs=[pl.BlockSpec(memory_space=V)] * 2,
        out_specs=[pl.BlockSpec(memory_space=V)] * 2,
        name="index",
    )(owner, slot)


def plan_kernel(col_ref, row_ref, out_ref):
    def at(shape, axis):
        return lax.broadcasted_iota(jnp.int32, shape, axis).astype(F32)
    square = (256, 256)
    own = jnp.broadcast_to(col_ref[...], square).astype(F32)
    other = jnp.broadcast_to(row_ref[...], square).astype(F32)
    k, j = at(square, 0), at(square, 1)
    one = jnp.ones(square, F32)
    zero = jnp.zeros(square, F32)
    key, other_key = jnp.where(own < 0, 1000.0, own), jnp.where(other < 0, 1000.0, other)
    before = (other_key < key) | ((other_key == key) & (j < k))
    rank = jnp.sum(jnp.where(before, one, zero), 1, keepdims=True)
    here = jnp.broadcast_to(rank, square) == j
    order = jnp.sum(jnp.where(here, k, zero), 0, keepdims=True)
    slots = jnp.sum(jnp.where(here, key, zero), 0, keepdims=True)
    lane = at((1, 256), 1)
    same = jnp.where((slots == pltpu.roll(slots, 1, 1)) & (lane > 0) & (slots < 1000.0), 1.0, 0.0)
    half = (256, 128)
    slot = at(half, 1)
    own_key = key[:, 0:128]
    last = jnp.sum(jnp.where(own_key <= slot, 1.0, 0.0), 0, keepdims=True) - 1.0
    some = jnp.max(jnp.where(own_key == slot, 1.0, 0.0), 0, keepdims=True)

    def panel_column(x):
        return (x >= 0) & (x - 32.0 * jnp.floor(x * (1 / 32)) < 2.0)
    hit, other_hit = panel_column(own), panel_column(other)
    turn = jnp.sum(jnp.where(other_hit & (j < k), one, zero), 1, keepdims=True)
    listed = jnp.sum(jnp.where(hit & (jnp.broadcast_to(turn, square) == j), k, zero), 0, keepdims=True)
    count = jnp.sum(jnp.where(hit, one, zero), 0, keepdims=True)
    rows = [order, same, jnp.concatenate([jnp.maximum(last, 0.0), some], 1), listed, count]
    for r in range(5):
        out_ref[r:r + 1, :] = rows[r].astype(jnp.int32)


def plan(land):
    return pl.pallas_call(
        plan_kernel,
        out_shape=jax.ShapeDtypeStruct((5, 256), jnp.int32),
        in_specs=[pl.BlockSpec(memory_space=V)] * 2,
        out_specs=pl.BlockSpec(memory_space=V),
        name="plan",
    )(land.reshape(256, 1), land.reshape(1, 256))


def head_kernel(land_ref, list_ref, front_ref, arr_ref, out_ref, buf_ref, acc_ref, fsem, asem):
    count = list_ref[4, 0]
    def arrive(n, i):
        return pltpu.make_async_copy(arr_ref.at[list_ref[3, n]], buf_ref.at[i], asem.at[i])
    def fetch(s):
        return pltpu.make_async_copy(front_ref.at[:, 0, :, s, 0, :], acc_ref.at[s], fsem.at[s])
    for s in range(2):
        fetch(s).start()
    def batch(b, carry):
        def begin(i, c):
            arrive(b * 16 + i, i).start()
            return c
        def end(i, c):
            n = b * 16 + i
            slot = land_ref[list_ref[3, n]]
            s, q = slot % 32, slot // 32
            arrive(n, i).wait()
            acc_ref[s, q] = acc_ref[s, q] + buf_ref[i].astype(F32)
            return c
        here = lax.min(count - b * 16, 16)
        lax.fori_loop(0, here, begin, 0)
        @pl.when(b == 0)
        def _():
            for s in range(2):
                fetch(s).wait()
        lax.fori_loop(0, here, end, 0)
        return carry
    lax.fori_loop(0, lax.max((count + 15) // 16, 1), batch, 0)
    out_ref[...] = acc_ref[...]


def head(land, listed, front, arrived):
    return pl.pallas_call(
        head_kernel,
        out_shape=jax.ShapeDtypeStruct((2, 4, 128, 128), F32),
        grid_spec=pltpu.PrefetchScalarGridSpec(
            num_scalar_prefetch=2, grid=(1,),
            in_specs=[pl.BlockSpec(memory_space=ANY)] * 2,
            out_specs=pl.BlockSpec((2, 4, 128, 128), lambda g, a, b: (0, 0, 0, 0)),
            scratch_shapes=[V((16, 128, 128), BF), V((2, 4, 128, 128), F32),
                            pltpu.SemaphoreType.DMA((2,)), pltpu.SemaphoreType.DMA((16,))]),
        compiler_params=pltpu.CompilerParams(vmem_limit_bytes=60 << 20),
        name="head",
    )(land, listed, front, arrived)


def panel_kernel(order_ref, panel_ref, hi_hbm, lo_hbm, low_hbm, front_ref, arr_ref, out_ref, pout_ref,
                 brow_ref, bcol_ref, acc_ref, buf_ref, run_ref, arow, ah, al, hi, lo, low, xb, rl, fsem, asem, osem, lsem, ps, pr, xs, xr, ws, wr, ys, yr, rs, rr, zs, zr, fs, fr, ms, mr):
    sub, row, col = lax.axis_index("sub"), lax.axis_index("row"), lax.axis_index("col")
    group = 4 * sub + row
    mate = sub + 1 - 2 * lax.rem(sub, 2)

    def n4(x, d):
        return lax.rem(x + 4 + d, 4)

    def n8(x, d):
        return lax.rem(x + 8 + d, 8)

    def remote(src, dst, send, recv, **where):
        return pltpu.make_async_remote_copy(src, dst, send, recv, device_id=where, device_id_type=MESH)

    loads = [pltpu.make_async_copy(hi_hbm, hi, lsem.at[0]), pltpu.make_async_copy(lo_hbm, lo, lsem.at[1]),
             pltpu.make_async_copy(low_hbm.at[pl.ds(pl.multiple_of(lax.min(group, 7) * 128, 128), 128)], low, lsem.at[2]),
             pltpu.make_async_copy(panel_ref.at[:, col], arow.at[col], lsem.at[3])]
    barrier = pltpu.get_barrier_semaphore()
    for d in (1, 3):
        pl.semaphore_signal(barrier, inc=1, device_id={"row": n4(row, d)}, device_id_type=MESH)
        pl.semaphore_signal(barrier, inc=1, device_id={"sub": n8(sub, 2 * d if d == 1 else -2)}, device_id_type=MESH)
    for d in (1, 2, 3):
        pl.semaphore_signal(barrier, inc=1, device_id={"col": n4(col, d)}, device_id_type=MESH)
    pl.semaphore_signal(barrier, inc=1, device_id={"sub": mate}, device_id_type=MESH)
    for copy in loads:
        copy.start()
    pl.semaphore_wait(barrier, 8)

    def fetch(s):
        return pltpu.make_async_copy(front_ref.at[:, 0, :, s, 0, :], acc_ref.at[s], fsem.at[s])
    def arrived(c):
        return pltpu.make_async_copy(arr_ref.at[pl.ds(c * 32, 32)], buf_ref.at[pl.ds(c * 32, 32)], asem.at[c])
    def put(s):
        return pltpu.make_async_copy(acc_ref.at[s], out_ref.at[:, 0, :, s, 0, :], osem.at[s])
    def early(s):
        return pltpu.make_async_copy(panel_ref.at[s], out_ref.at[:, 0, :, s, 0, :], osem.at[s])
    def each(low, high, f):
        def go(s, c):
            f(s)
            return c
        lax.fori_loop(low, high, go, 0)

    def take(h, d):
        return remote(panel_ref.at[h, n4(col, d)], arow.at[col, h], ps.at[h, d - 1], pr.at[h, d - 1], col=n4(col, d))
    def taken(h, d):
        return remote(panel_ref.at[h, n4(col, d)], arow.at[n4(col, -d), h], ps.at[h, d - 1], pr.at[h, d - 1], col=n4(col, d))
    for h in range(2):
        for d in (1, 3, 2):
            take(h, d).start()
    each(0, 8, lambda c: arrived(c).start())
    each(2, 32, lambda s: fetch(s).start())
    loads[3].wait()
    top = (group < 8) & (col == 0)

    def mm(x, y):
        return lax.dot_general(x, y, (((1,), (1,)), ((), ())), preferred_element_type=F32)

    def solve(h):
        for d in (1, 3, 2):
            taken(h, d).wait_recv()
        for t in range(4):
            v = arow[t, h]
            u = v.astype(BF)
            at = (4 * h + t) * 128
            ah[:, at:at + 128] = u
            al[:, at:at + 128] = (v - u.astype(F32)).astype(BF)
        if h == 0:
            for copy in loads[:3]:
                copy.wait()
        for b in (2 * h, 2 * h + 1):
            w = 256 * (b + 1)
            rows = pl.ds(256 * b, 256)
            y = mm(ah[:, 0:w], hi[rows, 0:w]) + (mm(ah[:, 0:w], lo[rows, 0:w]) + mm(al[:, 0:w], hi[rows, 0:w]))
            y = jnp.where(top, low[:, 256 * b:w], y.astype(BF))
            at = 256 * (b - 2 * h)
            xb[h, row, :, at:at + 256] = y
            brow_ref[h, col, :, at:at + 256] = y

    half = [pl.ds(0, 64), pl.ds(64, 64)]
    step = [1, -1]
    def xsend(h, i):
        return remote(xb.at[h, row], xb.at[h, row], xs.at[h, i], xr.at[h, i], row=n4(row, step[i]))
    def xrecv(h, i):
        at = xb.at[h, n4(row, -step[i])]
        return remote(at, at, xs.at[h, i], xr.at[h, i], row=n4(row, step[i]))
    def xforward(h, i, r):
        at = xb.at[h, r, half[i]]
        return remote(at, at, xs.at[h, 2 + i], xr.at[h, 2 + i], row=n4(row, step[i]))
    def wsend(h, i):
        return remote(brow_ref.at[h, col], brow_ref.at[h, col], ws.at[h, i], wr.at[h, i], col=n4(col, step[i]))
    def wrecv(h, i):
        at = brow_ref.at[h, n4(col, -step[i])]
        return remote(at, at, ws.at[h, i], wr.at[h, i], col=n4(col, step[i]))
    def wforward(h, i, c):
        at = brow_ref.at[h, c, half[i]]
        return remote(at, at, ws.at[h, 2 + i], wr.at[h, 2 + i], col=n4(col, step[i]))

    def ynear(h, i):
        return remote(xb.at[h, n4(col, step[i])], bcol_ref.at[h, col, sub], ys.at[h, i], yr.at[h, i], col=n4(col, step[i]))
    def ynear_in(h, i):
        return remote(xb.at[h, 0], bcol_ref.at[h, n4(col, -step[i]), sub], ys.at[h, i], yr.at[h, i], col=n4(col, step[i]))
    def yfar(h, i):
        return remote(xb.at[h, n4(col, 2), half[i]], rl.at[h, i], rs.at[h, i], rr.at[h, i], col=n4(col, step[i]))
    def yrelay(h, i):
        return remote(rl.at[h, i], bcol_ref.at[h, n4(col, -step[i]), sub, half[i]], ys.at[h, 2 + i], yr.at[h, 2 + i], col=n4(col, step[i]))
    def yfar_in(h, i):
        return remote(rl.at[h, i], bcol_ref.at[h, n4(col, 2), sub, half[i]], ys.at[h, 2 + i], yr.at[h, 2 + i], col=n4(col, step[i]))
    def home(h):
        return pltpu.make_async_copy(xb.at[h, col], bcol_ref.at[h, col, sub], lsem.at[4 + h])

    def ysend(h, c):
        d = n4(c, -col)
        @pl.when(d == 0)
        def _():
            home(h).start()
        for i in range(2):
            @pl.when(d == (1, 3)[i])
            def _():
                ynear(h, i).start()
        @pl.when(d == 2)
        def _():
            yfar(h, 0).start()
            yfar(h, 1).start()

    def own(h, e, i):
        at = bcol_ref.at[h, n4(col, e), sub]
        return remote(at if e else xb.at[h, col], at, zs.at[h, i, e], zr.at[h, i, e], sub=n8(sub, 2 * step[i]))
    def arrive(h, e, i):
        at = bcol_ref.at[h, n4(col, e), n8(sub, -2 * step[i])]
        return remote(at, at, zs.at[h, i, e], zr.at[h, i, e], sub=n8(sub, 2 * step[i]))
    side = [0, 0, 1, 1]
    def onward(h, e, i, z):
        at = bcol_ref.at[h, n4(col, e), n8(sub, z)]
        return remote(at, at, fs.at[h, e], fr.at[h, e], sub=n8(sub, 2 * step[i]))
    def swap(h, e, k, z):
        at = bcol_ref.at[h, n4(col, e), n8(sub, z)]
        return remote(at if k or e else xb.at[h, col], at, ms.at[h, k, e], mr.at[h, k, e], sub=mate)
    def swapped(h, e, k, z):
        at = bcol_ref.at[h, n4(col, e), n8(mate, z)]
        return remote(at, at, ms.at[h, k, e], mr.at[h, k, e], sub=mate)

    def launch(h, e):
        own(h, e, 0).start()
        own(h, e, 1).start()
        swap(h, e, 0, 0).start()
    apart = n4(col, -row)

    def gather(c):
        def go(k, total):
            i = c * 32 + k
            total = buf_ref[order_ref[0, i]].astype(F32) + order_ref[1, i].astype(F32) * total
            run_ref[i] = total
            return total
        first = jnp.zeros((128, 128), F32) if c == 0 else run_ref[c * 32 - 1]
        lax.fori_loop(0, 32, go, first)

    def settle(s):
        for q in range(4):
            slot = q * 32 + s
            acc_ref[s, q] = acc_ref[s, q] + order_ref[2, 128 + slot].astype(F32) * run_ref[order_ref[2, slot]]

    keep = jnp.where(group < 8, 0.0, 1.0)
    pair0 = sub - lax.rem(sub, 2)

    def update(e, dz):
        q, z = n4(col, e), n8(pair0, dz)
        s = q * 8 + z
        @pl.when(s >= 2)
        def _():
            settle(s)
            settle(s + 1)
            y = (mm(brow_ref[0].reshape(512, 512), bcol_ref[0, q, pl.ds(z, 2)].reshape(256, 512))
                 + mm(brow_ref[1].reshape(512, 512), bcol_ref[1, q, pl.ds(z, 2)].reshape(256, 512)))
            for u in range(2):
                t = y[:, u * 128:(u + 1) * 128].reshape(4, 128, 128)
                acc_ref[s + u, 0] = acc_ref[s + u, 0] - keep * t[0]
                acc_ref[s + u, 1:4] = acc_ref[s + u, 1:4] - t[1:4]
                put(s + u).start()

    def near(h):
        ynear_in(h, 1).wait_recv()
        launch(h, 1)
        ynear_in(h, 0).wait_recv()
        launch(h, 3)

    def reach(h, d):
        ysend(h, n4(row, d))
        @pl.when(apart == d)
        def _():
            launch(h, 0)

    for h in range(2):
        solve(h)
        for i in range(2):
            xsend(h, i).start()
        for i in range(2):
            wsend(h, i).start()
        reach(h, 0)
    early(0).start()
    early(1).start()
    for h in range(2):
        for i in range(2):
            xrecv(h, i).wait_recv()
            xforward(h, i, n4(row, -step[i])).start()
            reach(h, 3 if i == 0 else 1)
        if h == 0:
            each(0, 8, lambda c: arrived(c).wait())
            gather(0)
    for h in range(2):
        for i in range(2):
            wrecv(h, i).wait_recv()
            wforward(h, i, n4(col, -step[i])).start()
    gather(1)
    @pl.when(apart == 0)
    def _():
        near(0)
        near(1)
    for h in range(2):
        for i in range(2):
            xforward(h, i, n4(row, 2)).wait_recv()
        reach(h, 2)
        gather(2 + h)
    for h in range(2):
        for i in range(2):
            yfar(h, i).wait_recv()
            yrelay(h, i).start()
    gather(4)
    @pl.when(apart != 0)
    def _():
        near(0)
        near(1)
    for h in range(2):
        yfar_in(h, 0).wait_recv()
        yfar_in(h, 1).wait_recv()
        launch(h, 2)
    for c in range(5, 8):
        gather(c)
    each(2, 32, lambda s: fetch(s).wait())
    for h in range(2):
        for i in range(2):
            wforward(h, i, n4(col, 2)).wait_recv()
        home(h).wait()

    def gray(k):
        return k + jnp.where(k == 2, 1, 0) - jnp.where(k == 3, 1, 0)

    def product(e, k, z):
        for h in range(2):
            swapped(h, e, k, z).wait_recv()
        update(e, z)

    def pass_on(k, carry):
        e = gray(k)
        for h in range(2):
            for i in range(2):
                arrive(h, e, i).wait_recv()
                @pl.when((e < 2) if i == 0 else (e >= 2))
                def _():
                    onward(h, e, i, -2 * step[i]).start()
                swap(h, e, 1 + i, -2 * step[i]).start()

        def three(j, c):
            @pl.when((j == 0) | (k > 0))
            def _():
                product(jnp.where(j == 0, e, gray(lax.max(k - 1, 0))), j, jnp.where(j == 0, 0, 4 * j - 6))
            return c
        lax.fori_loop(0, 3, three, 0)
        return carry
    lax.fori_loop(0, 4, pass_on, 0)

    for q in range(4):
        pair = [brow_ref[s, q, :, pl.ds(pl.multiple_of(col * 128, 128), 128)] for s in range(2)]
        pout_ref[q] = jnp.stack([x.astype(F32) for x in pair], 1).astype(BF)

    def last(k, carry):
        @pl.when(k < 4)
        def _():
            e = gray(k)
            for h in range(2):
                onward(h, e, 0, 4).wait_recv()
                swap(h, e, 3, 4).start()

        def two(j, c):
            @pl.when((j == 0) | (k == 0))
            def _():
                product(jnp.where(k == 0, 2, gray(lax.max(k - 1, 0))), jnp.where(k == 0, 1 + j, 3), jnp.where(k == 0, 4 * j - 2, 4))
            return c
        lax.fori_loop(0, 2, two, 0)
        return carry
    lax.fori_loop(0, 5, last, 0)
    early(0).wait()
    early(1).wait()
    each(2, 32, lambda s: put(s).wait())

    for h in range(2):
        for d in (1, 2, 3):
            take(h, d).wait_send()
        for i in range(2):
            xsend(h, i).wait_send()
            wsend(h, i).wait_send()
            xforward(h, i, n4(row, -step[i])).wait_send()
            wforward(h, i, n4(col, -step[i])).wait_send()
            ynear(h, i).wait_send()
            yfar(h, i).wait_send()
            yrelay(h, i).wait_send()
        for e in range(4):
            own(h, e, 0).wait_send()
            own(h, e, 1).wait_send()
            onward(h, e, side[e], -2 * step[side[e]]).wait_send()
            swap(h, e, 0, 0).wait_send()
            swap(h, e, 1, -2).wait_send()
            swap(h, e, 2, 2).wait_send()
            swap(h, e, 3, 4).wait_send()


def panel_exchange(order, panel, hi, lo, low, front, arrived):
    D = pltpu.SemaphoreType.DMA
    H = pltpu.HBM
    return pl.pallas_call(
        panel_kernel,
        out_shape=(jax.ShapeDtypeStruct((4, 1, 128, 32, 1, 128), F32), jax.ShapeDtypeStruct((4, 128, 2, 128), BF)),
        in_specs=[pl.BlockSpec(memory_space=pltpu.SMEM), pl.BlockSpec(memory_space=V)] + [pl.BlockSpec(memory_space=H)] * 5,
        out_specs=(pl.BlockSpec(memory_space=H), pl.BlockSpec(memory_space=V)),
        scratch_shapes=[V((2, 4, 128, 512), BF), V((2, 4, 8, 128, 512), BF), V((32, 4, 128, 128), F32), V((256, 128, 128), BF),
                        V((256, 128, 128), F32), V((4, 2, 128, 128), F32), V((128, 1024), BF), V((128, 1024), BF),
                        V((1024, 1024), BF), V((1024, 1024), BF),
                        V((128, 1024), BF), V((2, 4, 128, 512), BF), V((2, 2, 64, 512), BF), D((32,)), D((8,)), D((32,)), D((6,))]
        + [D((2, 3))] * 2 + [D((2, 4))] * 6 + [D((2, 2))] * 2 + [D((2, 2, 4))] * 2 + [D((2, 4))] * 2 + [D((2, 4, 4))] * 2,
        compiler_params=pltpu.CompilerParams(vmem_limit_bytes=60 << 20, collective_id=2, has_side_effects=True),
        name="panel",
    )(order, panel, hi, lo, low, front, arrived)


def lead_kernel(idx_ref, front_ref, code_ref, child_ref, lead_ref, codes_ref, sent_ref, own_ref, tile_ref, pack_ref, tsem, psem, lsem, zs, zr, zls, zlr, xs, xr, ys, yr, as_, ar, bs, br, cas, car, cbs, cbr, afs, afr, bfs, bfr):
    sub, row, col = lax.axis_index("sub"), lax.axis_index("row"), lax.axis_index("col")
    par = lax.rem(sub, 2)
    mate = sub + 1 - 2 * par
    line = 4 * par + row
    need = (par == 1) | (col <= row)

    def remote(src, dst, send, recv, **where):
        return pltpu.make_async_remote_copy(src, dst, send, recv, device_id=where, device_id_type=MESH)

    barrier = pltpu.get_barrier_semaphore()
    for d in range(1, 8):
        pl.semaphore_signal(barrier, inc=1, device_id={"sub": lax.rem(sub + d, 8)}, device_id_type=MESH)
    for d in range(1, 4):
        pl.semaphore_signal(barrier, inc=1, device_id={"row": lax.rem(row + d, 4)}, device_id_type=MESH)
        pl.semaphore_signal(barrier, inc=1, device_id={"col": lax.rem(col + d, 4)}, device_id_type=MESH)

    mine = [pltpu.make_async_copy(front_ref.at[0, 0, :, s, 0, :], own_ref.at[s], lsem.at[s]) for s in range(2)]
    code = pltpu.make_async_copy(code_ref, codes_ref.at[col, row, sub], lsem.at[2])
    tiles = [pltpu.make_async_copy(child_ref.at[pl.ds(32 * g, 32)], tile_ref.at[pl.ds(32 * g, 32)], tsem.at[g]) for g in range(4)]
    packs = [pltpu.make_async_copy(pack_ref.at[pl.ds(16 * g, 16)], sent_ref.at[pl.ds(16 * g, 16)], psem.at[g]) for g in range(8)]

    def pack(g):
        def go(j, c):
            for u in range(2):
                pack_ref[16 * g + j, u] = tile_ref[idx_ref[u, 16 * g + j]]
            return c
        lax.fori_loop(0, 16, go, 0)
        packs[g].start()

    code.start()
    mine[0].start()
    mine[1].start()
    for copy in tiles:
        copy.start()
    mine[0].wait()
    mine[1].wait()
    keep = [pltpu.make_async_copy(own_ref.at[s], lead_ref.at[line, 4 * s + col], lsem.at[3 + s]) for s in range(2)]

    @pl.when(sub < 2)
    def _():
        keep[0].start()
        keep[1].start()
    pl.semaphore_wait(barrier, 13)

    def zcode(d):
        return remote(code_ref, codes_ref.at[col, row, sub], zs.at[d - 1], zr.at[d - 1], sub=lax.rem(sub + d, 8))
    def zcode_in(d):
        return remote(code_ref, codes_ref.at[col, row, lax.rem(sub + 8 - d, 8)], zs.at[d - 1], zr.at[d - 1], sub=lax.rem(sub + d, 8))
    need1 = (par == 1) & (col <= row)

    @pl.when(sub < 2)
    def _():
        for d in (1, 3, 2):
            @pl.when(need)
            def _():
                remote(own_ref.at[0], lead_ref.at[line, col], zls.at[d - 1, 0], zlr.at[0], sub=sub + 2 * d).start()
            @pl.when(need1)
            def _():
                remote(own_ref.at[1], lead_ref.at[line, 4 + col], zls.at[d - 1, 1], zlr.at[1], sub=sub + 2 * d).start()
    for d in range(1, 8):
        zcode(d).start()
    for copy in tiles:
        copy.wait()
    for g in range(4):
        pack(g)

    @pl.when(sub < 2)
    def _():
        keep[0].wait()
        keep[1].wait()

    @pl.when(sub >= 2)
    def _():
        @pl.when(need)
        def _():
            remote(own_ref.at[0], lead_ref.at[line, col], zls.at[0, 0], zlr.at[0], sub=par).wait_recv()
        @pl.when(need1)
        def _():
            remote(own_ref.at[1], lead_ref.at[line, 4 + col], zls.at[0, 1], zlr.at[1], sub=par).wait_recv()

    def ax(d, r):
        return remote(lead_ref.at[4 + r, col], lead_ref.at[4 + r, col], as_.at[0, d - 1], ar.at[0, d - 1], row=lax.rem(row + d, 4))
    def ay(d, c):
        return remote(lead_ref.at[pl.ds(4, 4), c], lead_ref.at[pl.ds(4, 4), c], as_.at[1, d - 1], ar.at[1, d - 1], col=lax.rem(col + d, 4))
    def by(d, c):
        at = lead_ref.at[line, 4 * par + c]
        return remote(at, at, bs.at[d - 1, 4], br.at[d - 1, 4], col=lax.rem(col + d, 4))
    def bx(d, r, c):
        at = lead_ref.at[4 * par + r, 4 * par + c]
        return remote(at, at, bs.at[d - 1, c], br.at[d - 1, c], row=lax.rem(row + d, 4))
    for d in (1, 3, 2):
        @pl.when(par == 1)
        def _():
            ax(d, row).start()
        @pl.when(col <= row)
        def _():
            by(d, col).start()
    code.wait()
    for d in range(1, 8):
        zcode_in(d).wait_recv()
    def cx(d, r):
        return remote(codes_ref.at[col, r], codes_ref.at[col, r], xs.at[d - 1], xr.at[d - 1], row=lax.rem(row + d, 4))
    def cy(d, c):
        return remote(codes_ref.at[c], codes_ref.at[c], ys.at[d - 1], yr.at[d - 1], col=lax.rem(col + d, 4))
    for d in range(1, 4):
        cx(d, row).start()
    for d in (1, 3, 2):
        @pl.when(par == 1)
        def _():
            ax(d, lax.rem(row + 4 - d, 4)).wait_recv()
        @pl.when(lax.rem(col + 4 - d, 4) <= row)
        def _():
            by(d, lax.rem(col + 4 - d, 4)).wait_recv()
    for d in (1, 3):
        @pl.when(par == 1)
        def _():
            ay(d, col).start()
        for c in range(4):
            @pl.when(c <= row)
            def _():
                bx(d, row, c).start()
    def ay2(i, c):
        at = lead_ref.at[pl.ds(4 + 2 * i, 2), c]
        return remote(at, at, afs.at[i], afr.at[i], col=lax.rem(col + (1, 3)[i], 4))
    def bx2(r, c):
        at = lead_ref.at[4 * par + r, 4 * par + c]
        return remote(at, at, bfs.at[c], bfr.at[c], row=lax.rem(row + (1, 3)[c // 2], 4))

    def swap_a(c):
        at = lead_ref.at[pl.ds(4, 4), c]
        return remote(at, at, cas.at[c], car.at[c], sub=mate)
    def swap_b(p, r, c):
        at = lead_ref.at[4 * p + r, 4 * p + c]
        return remote(at, at, cbs.at[r, c], cbr.at[r, c], sub=mate)
    def hand(r, c):
        @pl.when(par == 1)
        def _():
            swap_a(c).start()
        for u in range(4):
            @pl.when(u <= r)
            def _():
                swap_b(par, r, u).start()
    hand(row, col)
    for g in range(4, 6):
        pack(g)
    for d in range(1, 4):
        cx(d, lax.rem(row + 4 - d, 4)).wait_recv()
    for d in range(1, 4):
        cy(d, col).start()
    for i in range(2):
        d = (1, 3)[i]
        r = lax.rem(row + 4 - d, 4)
        @pl.when(par == 1)
        def _():
            ay(d, lax.rem(col + 4 - d, 4)).wait_recv()
            ay2(i, lax.rem(col + 4 - d, 4)).start()
        for c in range(4):
            @pl.when(c <= r)
            def _():
                bx(d, r, c).wait_recv()
                if c // 2 == i:
                    bx2(r, c).start()
        hand(r, lax.rem(col + 4 - d, 4))
    across, beyond = lax.rem(row + 2, 4), lax.rem(col + 2, 4)
    @pl.when(par == 1)
    def _():
        for i in range(2):
            ay2(i, beyond).wait_recv()
    for c in range(4):
        @pl.when(c <= across)
        def _():
            bx2(across, c).wait_recv()
    hand(across, beyond)
    for g in range(6, 8):
        pack(g)
    @pl.when(par == 0)
    def _():
        for c in range(4):
            swap_a(c).wait_recv()
    for r in range(4):
        for c in range(r + 1):
            swap_b(1 - par, r, c).wait_recv()
    for d in range(1, 4):
        cy(d, lax.rem(col + 4 - d, 4)).wait_recv()

    for d in range(1, 8):
        zcode(d).wait_send()
    @pl.when(sub < 2)
    def _():
        for d in (1, 2, 3):
            @pl.when(need)
            def _():
                remote(own_ref.at[0], lead_ref.at[line, col], zls.at[d - 1, 0], zlr.at[0], sub=sub + 2 * d).wait_send()
            @pl.when(need1)
            def _():
                remote(own_ref.at[1], lead_ref.at[line, 4 + col], zls.at[d - 1, 1], zlr.at[1], sub=sub + 2 * d).wait_send()
    for d in range(1, 4):
        cx(d, row).wait_send()
        cy(d, col).wait_send()
        @pl.when(par == 1)
        def _():
            ax(d, row).wait_send()
        @pl.when(col <= row)
        def _():
            by(d, col).wait_send()
    for i in range(2):
        d = (1, 3)[i]
        r = lax.rem(row + 4 - d, 4)
        @pl.when(par == 1)
        def _():
            ay(d, col).wait_send()
            ay2(i, lax.rem(col + 4 - d, 4)).wait_send()
        for c in range(4):
            @pl.when(c <= row)
            def _():
                bx(d, row, c).wait_send()
        for c in (2 * i, 2 * i + 1):
            @pl.when(c <= r)
            def _():
                bx2(r, c).wait_send()
    @pl.when(par == 1)
    def _():
        for c in range(4):
            swap_a(c).wait_send()
    for r in range(4):
        for c in range(r + 1):
            swap_b(par, r, c).wait_send()
    for copy in packs:
        copy.wait()


def lead_gather(idx, front, code, child):
    D = pltpu.SemaphoreType.DMA
    return pl.pallas_call(
        lead_kernel,
        out_shape=(jax.ShapeDtypeStruct((8, 8, 128, 128), F32), jax.ShapeDtypeStruct((4, 4, 8, 1, 128), jnp.int32),
                   jax.ShapeDtypeStruct((128, 2, 128, 128), BF)),
        in_specs=[pl.BlockSpec(memory_space=pltpu.SMEM), pl.BlockSpec(memory_space=pltpu.HBM), pl.BlockSpec(memory_space=V),
                  pl.BlockSpec(memory_space=pltpu.HBM)],
        out_specs=(pl.BlockSpec(memory_space=V), pl.BlockSpec(memory_space=V), pl.BlockSpec(memory_space=pltpu.HBM)),
        scratch_shapes=[V((2, 128, 128), F32), V((128, 128, 128), BF), V((128, 2, 128, 128), BF), D((4,)), D((8,)), D((5,)), D((7,)), D((7,)), D((3, 2)), D((2,)), D((3,)), D((3,)), D((3,)), D((3,)),
                        D((2, 3)), D((2, 3)), D((3, 5)), D((3, 5)), D((4,)), D((4,)), D((4, 4)), D((4, 4)), D((2,)), D((2,)), D((4,)), D((4,))],
        compiler_params=pltpu.CompilerParams(vmem_limit_bytes=60 << 20, collective_id=1, has_side_effects=True),
        name="lead",
    )(idx, front, code, child)


def landings(codes, me):
    codes = codes[:, :, :, 0, :].transpose(2, 1, 0, 3).reshape(128, 128)
    place = lax.broadcasted_iota(jnp.int32, (128, 128), 1) * 128 + codes % 128
    match = codes // 128 == me
    first = jnp.min(jnp.where(match, place, 1 << 20), 1)
    last = jnp.max(jnp.where(match, place, -1), 1)
    one = jnp.where(last >= 0, first % 128, -1)
    two = jnp.where(last > first, last % 128, -1)
    return jnp.stack([one, two], 1).reshape(256)


def local(front, child_tiles, tile_owner, tile_slot):
    sub = lax.axis_index("sub")
    row = lax.axis_index("row")
    col = lax.axis_index("col")
    group = sub * 4 + row
    idx, code = index(tile_owner.reshape(1, 128), tile_slot.reshape(1, 128))
    lead, codes, outgoing = lead_gather(idx, front, code, child_tiles)
    arrived = lax.all_to_all(outgoing, ("sub", "row", "col"), split_axis=0, concat_axis=0, tiled=True)
    arrived = arrived.reshape(256, 128, 128)
    factor, hi, lo = chol(lead)
    landing = landings(codes, group * 4 + col)
    order = plan(landing)
    panel = head(landing, order, front, arrived)
    out, panel_out = panel_exchange(order, panel, hi, lo, factor, front, arrived)
    return out, panel_out.reshape(4, 1, 128, 2, 1, 128)


def solution(mesh):
    return jax.shard_map(
        local,
        mesh=mesh,
        in_specs=(
            P(None, ("sub", "row"), None, None, "col", None),
            P(("sub", "row", "col"), None, None),
            P(("sub", "row", "col"), None),
            P(("sub", "row", "col")),
        ),
        out_specs=(
            P(None, ("sub", "row"), None, None, "col", None),
            P(None, ("sub", "row"), None, None, "col", None),
        ),
        check_vma=False,
    )
```
